32 devices in a mesh: dp: 16 (over z, x, core), tensor: 2 (over y).
Axes of the slice: x: 2, y: 2, z: 4, core: 2. Of those that a mesh axis runs over, the one named last changes fastest.
Arguments:
- x_input: bfloat16 [16, 768, 1536], P('dp', 'tensor'), may hold values from -6 to 6
- cond_tokens: bfloat16 [16, 130, 1536], P('dp'), may hold values from -6 to 6
- teacher: bfloat16 [16, 768, 1536], P('dp', 'tensor'), may hold values from -6 to 6
- valid_mask: int32 [16, 768], P('dp', 'tensor'), may hold values from 0 to 1, as said below
- norm_gains: bfloat16 [3, 1536], P(None, 'dp'), may hold values from 0.099609375 to 1.8984375
- w_query: bfloat16 [1536, 1536], P('dp', 'tensor'), may hold values from -0.15625 to 0.15625
- w_key: bfloat16 [1536, 1536], P('dp', 'tensor'), may hold values from -0.15625 to 0.15625
- w_value: bfloat16 [1536, 1536], P('dp', 'tensor'), may hold values from -0.15625 to 0.15625
- w_out: bfloat16 [1536, 1536], P('tensor', 'dp'), may hold values from -3 to 3
- c_query: bfloat16 [1536, 1536], P('dp', 'tensor'), may hold values from -0.15625 to 0.15625
- c_key: bfloat16 [1536, 1536], P('dp', 'tensor'), may hold values from -0.15625 to 0.15625
- c_value: bfloat16 [1536, 1536], P('dp', 'tensor'), may hold values from -0.15625 to 0.15625
- c_out: bfloat16 [1536, 1536], P('tensor', 'dp'), may hold values from -1.25 to 1.25
- w_gate: bfloat16 [1536, 6144], P('dp', 'tensor'), may hold values from -0.15625 to 0.15625
- w_up: bfloat16 [1536, 6144], P('dp', 'tensor'), may hold values from -0.15625 to 0.15625
- w_down: bfloat16 [6144, 1536], P('tensor', 'dp'), may hold values from -0.078125 to 0.078125
Outputs:
- output: bfloat16 [16, 768, 1536], P('dp', 'tensor')
- mean_loss: float32 [], replicated
- grad_input: float32 [16, 768, 1536], P('dp', 'tensor')
- grad_cond: float32 [16, 130, 1536], P('dp')
- grad_w_query: float32 [1536, 1536], P('dp', 'tensor')
- grad_w_key: float32 [1536, 1536], P('dp', 'tensor')
- grad_w_value: float32 [1536, 1536], P('dp', 'tensor')
- grad_w_out: float32 [1536, 1536], P('tensor', 'dp')
- grad_c_query: float32 [1536, 1536], P('dp', 'tensor')
- grad_c_key: float32 [1536, 1536], P('dp', 'tensor')
- grad_c_value: float32 [1536, 1536], P('dp', 'tensor')
- grad_c_out: float32 [1536, 1536], P('tensor', 'dp')
- grad_w_gate: float32 [1536, 6144], P('dp', 'tensor')
- grad_w_up: float32 [1536, 6144], P('dp', 'tensor')
- grad_w_down: float32 [6144, 1536], P('tensor', 'dp')
- grad_norm_gains: float32 [3, 1536], P(None, 'dp')
The draws below stay inside these ranges and needn't reach their ends.
Inputs may be any that keep to these rules, and one draw needn't show every extreme that they name: `valid_mask`: the valid tokens of each latent form a prefix of it, and every latent has a valid token.
All inputs are finite; a program needn't handle non-finite values.
Results may differ from the reference program's by a relative error of at most 0.017.
Values may be sent and summed in bfloat16 or wider, within the bound.
No kernel may reach another device: no remote copies, remote signals or barrier semaphores. Data moves between devices by JAX's collectives and lax.ppermute only.
A program may use at most 256 MiB of HBM per device.

```python
import math
import jax
import jax.numpy as jnp
from jax import lax

D = 1536
HEADS = 24
HEAD_DIM = 64
FF = 6144
CTX = 130
LEN = 768
BATCH = 16


def draw_valid_mask(key, part):
    latents = jnp.arange(BATCH, dtype=jnp.int32)
    lowest = LEN // 4 + latents * (LEN // 2) // BATCH
    extra = jax.random.randint(key, (BATCH,), 0, LEN // 4 + 1, dtype=jnp.int32)
    lengths = jnp.minimum(lowest + extra, LEN)
    places = jnp.arange(LEN, dtype=jnp.int32)
    return (places[None, :] < lengths[:, None]).astype(jnp.int32)


def shard_levels(own_key, dims, cuts, least, high):
    factor_of, own = 1.0, jax.random.fold_in(own_key, 6)
    for dim, blocks in cuts:
        draws = jnp.exp(jax.random.uniform(jax.random.fold_in(own, dim), (blocks,), jnp.float32, least / len(cuts), high / len(cuts)))
        factor_of = factor_of * jnp.repeat(draws, dims[dim] // blocks).reshape([-1 if axis == dim else 1 for axis in range(len(dims))])
    return factor_of


def bell_draw(stream_key, dims, scale, limit, split=(), kind=jnp.bfloat16):
    result = jax.random.normal(stream_key, dims, jnp.float32) * scale
    if len(split) > 0:
        result = shard_levels(stream_key, dims, split, -0.22, 0.18) * result
    return jnp.clip(result, min=-limit, max=limit).astype(kind)


def setup_inputs(seed: int = 0) -> dict:
    keys = jax.random.split(jax.random.key(seed), 17)
    return {
        "x_input": bell_draw(keys[0], (BATCH, LEN, D), 1.0, 6.0, ((0, 16), (1, 2))),
        "cond_tokens": bell_draw(keys[1], (BATCH, CTX, D), 1.0, 6.0, ((0, 16),)),
        "teacher": bell_draw(keys[2], (BATCH, LEN, D), 1.0, 6.0, ((0, 16), (1, 2))),
        "valid_mask": draw_valid_mask(jax.random.fold_in(keys[16], 71), 0),
        "norm_gains": jnp.clip(1.0 + 0.18 * jax.random.normal(keys[4], (3, D), jnp.float32), 0.099609375, 1.8984375).astype(jnp.bfloat16),
        "w_query": bell_draw(keys[5], (D, D), D ** -0.5, 0.15625, ((0, 16), (1, 2))),
        "w_key": bell_draw(keys[6], (D, D), D ** -0.5, 0.15625, ((0, 16), (1, 2))),
        "w_value": bell_draw(keys[7], (D, D), D ** -0.5, 0.15625, ((0, 16), (1, 2))),
        "w_out": bell_draw(keys[8], (D, D), (max(1, 2 * D // LEN)) ** -0.5, 3.0, ((0, 2), (1, 16))),
        "c_query": bell_draw(keys[9], (D, D), D ** -0.5, 0.15625, ((0, 16), (1, 2))),
        "c_key": bell_draw(keys[10], (D, D), D ** -0.5, 0.15625, ((0, 16), (1, 2))),
        "c_value": bell_draw(keys[11], (D, D), D ** -0.5, 0.15625, ((0, 16), (1, 2))),
        "c_out": bell_draw(keys[12], (D, D), (max(1, 2 * D // CTX)) ** -0.5, 1.25, ((0, 2), (1, 16))),
        "w_gate": bell_draw(keys[13], (D, FF), D ** -0.5, 0.15625, ((0, 16), (1, 2))),
        "w_up": bell_draw(keys[14], (D, FF), D ** -0.5, 0.15625, ((0, 16), (1, 2))),
        "w_down": bell_draw(keys[15], (FF, D), FF ** -0.5, 0.078125, ((0, 2), (1, 16))),
    }


@jax.custom_vjp
def low(v):
    return lax.optimization_barrier(v.astype(jnp.bfloat16)).astype(jnp.float32)

@jax.custom_vjp
def low_back(v):
    return v

def low_keep(v):
    return (low(v), None)

def low_pass(kept, grad):
    return (grad,)

def back_keep(v):
    return (v, None)

def back_low(kept, grad):
    return (low(grad),)
low.defvjp(low_keep, low_pass)
low_back.defvjp(back_keep, back_low)

def matmul(left_side, right_side):
    return jnp.dot(left_side, right_side, precision=lax.Precision.HIGHEST, preferred_element_type=jnp.float32)

def layer_norm(values, gain_row):
    row_mean = lax.optimization_barrier(jnp.mean(values, axis=-1, keepdims=True))
    centred = values - row_mean
    row_var = lax.optimization_barrier(jnp.mean(centred * centred, axis=-1, keepdims=True))
    return centred * lax.rsqrt(row_var + 1e-05) * gain_row

def rotary_tables(length):
    half_dim = HEAD_DIM // 2
    freqs = jnp.exp(jnp.arange(half_dim, dtype=jnp.float32) * (-math.log(10000.0) / half_dim))
    angles = jnp.arange(length, dtype=jnp.float32)[:, None] * freqs[None, :]
    return (jnp.cos(angles)[:, None, :], jnp.sin(angles)[:, None, :])

def rotate(values, rot_cos, rot_sin):
    half_dim = HEAD_DIM // 2
    lower = values[..., :half_dim]
    upper = values[..., half_dim:]
    return jnp.concatenate([lower * rot_cos - upper * rot_sin, upper * rot_cos + lower * rot_sin], axis=-1)

def attend(queries, keys_in, values_in):
    scale_factor = HEAD_DIM ** (-0.5)
    scores = low_back(jnp.einsum('qhd,khd->hqk', queries, keys_in, precision=lax.Precision.HIGHEST) * scale_factor)
    soft_probs = low(jax.nn.softmax(scores, axis=-1))
    return jnp.einsum('hqk,khd->qhd', soft_probs, values_in, precision=lax.Precision.HIGHEST)

def forward(x_rows, cond_rows, params):
    gains, weight_q, weight_k, weight_v, weight_o, cross_q, cross_k, cross_v, cross_o, weight_gate, weight_up, weight_down = params
    rot_cos, rot_sin = rotary_tables(LEN)
    normed_one = low(layer_norm(x_rows, gains[0]))
    query_pre = low_back(matmul(normed_one, weight_q)).reshape(LEN, HEADS, HEAD_DIM)
    key_pre = low_back(matmul(normed_one, weight_k)).reshape(LEN, HEADS, HEAD_DIM)
    query_rot = low(rotate(query_pre, rot_cos, rot_sin))
    key_rot = low(rotate(key_pre, rot_cos, rot_sin))
    value_self = low(low_back(matmul(normed_one, weight_v))).reshape(LEN, HEADS, HEAD_DIM)
    mixed_self = low(low_back(attend(query_rot, key_rot, value_self).reshape(LEN, D)))
    hidden_one = x_rows + low_back(matmul(mixed_self, weight_o))
    normed_two = low(layer_norm(hidden_one, gains[1]))
    query_cross = low(low_back(matmul(normed_two, cross_q))).reshape(LEN, HEADS, HEAD_DIM)
    key_cross = low(low_back(matmul(cond_rows, cross_k))).reshape(CTX, HEADS, HEAD_DIM)
    value_cross = low(low_back(matmul(cond_rows, cross_v))).reshape(CTX, HEADS, HEAD_DIM)
    mixed_cross = low(low_back(attend(query_cross, key_cross, value_cross).reshape(LEN, D)))
    hidden_two = hidden_one + low_back(matmul(mixed_cross, cross_o))
    normed_three = low(layer_norm(hidden_two, gains[2]))
    gate_pre = low_back(matmul(normed_three, weight_gate))
    up_pre = low_back(matmul(normed_three, weight_up))
    hidden_ff = low(jax.nn.silu(gate_pre) * up_pre)
    return hidden_two + low_back(matmul(hidden_ff, weight_down))

def add_pair(earlier, later):
    return earlier + later

def reference(x_input, cond_tokens, teacher, valid_mask, norm_gains, w_query, w_key, w_value, w_out, c_query, c_key, c_value, c_out, w_gate, w_up, w_down):
    params = tuple((item.astype(jnp.float32) for item in (norm_gains, w_query, w_key, w_value, w_out, c_query, c_key, c_value, c_out, w_gate, w_up, w_down)))
    mask_float = valid_mask.astype(jnp.float32)
    valid_count = jnp.sum(mask_float)
    factor = BATCH * LEN / valid_count

    def one_latent(totals, items):
        x_rows, cond_rows, target, weights_row = items

        def objective(x_value, cond_value, param_value):
            final = forward(x_value, cond_value, param_value)
            error_diff = final - target.astype(jnp.float32)
            error_total = jnp.sum(weights_row[:, None] * error_diff * error_diff)
            return (error_total * factor, (final, error_total))
        value_out, pullback, aux_out = jax.vjp(objective, x_rows.astype(jnp.float32), cond_rows.astype(jnp.float32), params, has_aux=True)
        grad_rows, grad_context, grad_params = pullback(jnp.ones_like(value_out))
        totals = jax.tree.map(add_pair, totals, grad_params)
        return (totals, (aux_out[0].astype(jnp.bfloat16), grad_rows, grad_context, aux_out[1]))
    zero_grads = jax.tree.map(jnp.zeros_like, params)
    totals, results = lax.scan(one_latent, zero_grads, (x_input, cond_tokens, teacher, mask_float))
    output, grad_input, grad_cond, errors = results
    mean_loss = jnp.sum(errors) / (D * valid_count)
    return (output, mean_loss, grad_input, grad_cond, totals[1], totals[2], totals[3], totals[4], totals[5], totals[6], totals[7], totals[8], totals[9], totals[10], totals[11], totals[0])
```

```python
import math

import jax
import jax.numpy as jnp
from jax import lax
from jax.sharding import Mesh, PartitionSpec as P

HEAD_DIM = 64
EPSILON = 1e-05
F32 = jnp.float32
BF16 = jnp.bfloat16


def dot(left, right, left_dim, right_dim):
    return lax.dot_general(
        left, right, (((left_dim,), (right_dim,)), ((), ())), preferred_element_type=F32
    )


def norm_stats(values):
    row_mean = jnp.mean(values, axis=-1, keepdims=True)
    centred = values - row_mean
    row_var = jnp.mean(centred * centred, axis=-1, keepdims=True)
    inverse = lax.rsqrt(row_var + EPSILON)
    return (centred * inverse, inverse)


def norm_back(grad_normed, normed, inverse, gain_row):
    scaled = grad_normed * gain_row
    mean_scaled = jnp.mean(scaled, axis=-1, keepdims=True)
    mean_product = jnp.mean(scaled * normed, axis=-1, keepdims=True)
    grad_values = inverse * (scaled - mean_scaled - normed * mean_product)
    return (grad_values, jnp.sum(grad_normed * normed, axis=0))


def rotary_tables(positions):
    half_dim = HEAD_DIM // 2
    freqs = jnp.exp(jnp.arange(half_dim, dtype=F32) * (-math.log(10000.0) / half_dim))
    angles = positions.astype(F32)[:, None] * freqs[None, :]
    return (jnp.cos(angles)[:, None, :], jnp.sin(angles)[:, None, :])


def rotate(values, rot_cos, rot_sin):
    half_dim = HEAD_DIM // 2
    lower = values[..., :half_dim]
    upper = values[..., half_dim:]
    return jnp.concatenate(
        [lower * rot_cos - upper * rot_sin, upper * rot_cos + lower * rot_sin], axis=-1
    )


def attend_forward(queries, keys_in, values_in):
    scale_factor = HEAD_DIM ** (-0.5)
    scores = (
        jnp.einsum("qhd,khd->hqk", queries, keys_in, preferred_element_type=F32) * scale_factor
    )
    row_max = jnp.max(scores, axis=-1, keepdims=True)
    shifted = jnp.exp(scores - row_max)
    row_total = jnp.sum(shifted, axis=-1, keepdims=True)
    soft_probs = (shifted / row_total).astype(BF16)
    mixed = jnp.einsum("hqk,khd->qhd", soft_probs, values_in, preferred_element_type=F32)
    return (mixed, row_max + jnp.log(row_total))


def attend_back(queries, keys_in, values_in, log_total, grad_mixed):
    scale_factor = HEAD_DIM ** (-0.5)
    scores = (
        jnp.einsum("qhd,khd->hqk", queries, keys_in, preferred_element_type=F32) * scale_factor
    )
    soft_probs = jnp.exp(scores - log_total)
    grad_values = jnp.einsum(
        "hqk,qhd->khd", soft_probs.astype(BF16), grad_mixed, preferred_element_type=F32
    )
    grad_probs = jnp.einsum("qhd,khd->hqk", grad_mixed, values_in, preferred_element_type=F32)
    weighted = jnp.sum(soft_probs * grad_probs, axis=-1, keepdims=True)
    grad_scores = (soft_probs * (grad_probs - weighted)).astype(BF16)
    grad_queries = (
        jnp.einsum("hqk,khd->qhd", grad_scores, keys_in, preferred_element_type=F32) * scale_factor
    )
    grad_keys = (
        jnp.einsum("hqk,qhd->khd", grad_scores, queries, preferred_element_type=F32) * scale_factor
    )
    return (grad_queries, grad_keys, grad_values)


def body(
    x_input,
    cond_tokens,
    teacher,
    valid_mask,
    norm_gains,
    w_query,
    w_key,
    w_value,
    w_out,
    c_query,
    c_key,
    c_value,
    c_out,
    w_gate,
    w_up,
    w_down,
):
    chips = lax.axis_size("ring")
    pair = lax.axis_index("core")
    share = lax.axis_index("tensor")
    dp_size = 2 * chips
    dp_axes = ("ring", "core")
    swap = [(0, 1), (1, 0)]

    def to_peer(values):
        return lax.ppermute(values, "tensor", swap)

    def to_core(values):
        return lax.ppermute(values, "core", swap)

    def gather(values):
        return lax.all_gather(values, dp_axes, axis=0, tiled=True)

    def half_of(values, index):
        width = values.shape[1] // 2
        return lax.dynamic_slice(values, (0, index * width), (values.shape[0], width))

    x_bf = x_input[0]
    rows, width = x_bf.shape
    slab = w_query.shape[0]
    heads_width = w_query.shape[1]
    ff_width = w_gate.shape[1]
    cond_rows = cond_tokens[0]
    mask_float = valid_mask[0].astype(F32)
    x_peer_bf = to_peer(x_bf)

    own_count = jnp.sum(valid_mask[0])
    row_ids = lax.broadcasted_iota(jnp.int32, (slab, 1), 0)
    count_col = jnp.where(
        row_ids == 0, own_count // 128, jnp.where(row_ids == 1, own_count % 128, 0)
    ).astype(BF16)
    extra = jnp.pad(
        jnp.concatenate([norm_gains.T, count_col], axis=1), ((0, 0), (0, 124))
    )
    gath_a = gather(jnp.concatenate([w_query, w_key, w_value, extra], axis=1))
    gath_b = gather(jnp.concatenate([w_out.T, c_query, c_key, c_value, c_out.T], axis=1))
    gath_c = gather(jnp.concatenate([w_gate, w_up], axis=1))
    gath_d = gather(w_down.T)

    weight_qkv = gath_a[:, : 3 * heads_width]
    side = gath_a[:, 3 * heads_width :].T[:8].astype(F32)
    gains = side[:3]
    counts = side[3].reshape(dp_size, slab)
    part_count = jnp.sum(counts[:, 0]) * 128.0 + jnp.sum(counts[:, 1])
    part_count = jnp.full((8, 128), part_count, F32)
    valid_count = (part_count + to_peer(part_count))[0, 0]
    weight_o = gath_b[:, :heads_width]
    cross_q, cross_k, cross_v, cross_o = (
        gath_b[:, i * heads_width : (i + 1) * heads_width] for i in range(1, 5)
    )
    weight_gate = gath_c[:, :ff_width]
    weight_up = gath_c[:, ff_width:]

    def both(own):
        return jnp.concatenate([own, to_peer(own)], axis=0)

    length = 2 * rows
    ctx_len = cond_rows.shape[0]
    local_rows = x_bf.astype(F32)
    normed_one, inverse_one = norm_stats(local_rows)
    peer_one, _ = norm_stats(x_peer_bf.astype(F32))
    input_one = jnp.concatenate(
        [(normed_one * gains[0]).astype(BF16), (peer_one * gains[0]).astype(BF16)], axis=0
    )
    places = lax.iota(jnp.int32, length)
    positions = jnp.where(places < rows, places + share * rows, places - share * rows)
    rot_cos, rot_sin = rotary_tables(positions)
    qkv = dot(input_one, weight_qkv, 1, 0)
    query_rot = rotate(
        qkv[:, :heads_width].reshape(length, -1, HEAD_DIM), rot_cos, rot_sin
    ).astype(BF16)
    key_rot = rotate(
        qkv[:, heads_width : 2 * heads_width].reshape(length, -1, HEAD_DIM), rot_cos, rot_sin
    ).astype(BF16)
    value_self = qkv[:, 2 * heads_width :].astype(BF16).reshape(length, -1, HEAD_DIM)
    mixed_self, log_self = attend_forward(query_rot, key_rot, value_self)
    mixed_self = mixed_self.reshape(length, -1).astype(BF16)

    def project(values, weight, weight_dim):
        away = to_peer(dot(values[rows:], weight, 1, weight_dim).astype(BF16))
        return dot(values[:rows], weight, 1, weight_dim) + away.astype(F32)

    hidden_one = local_rows + project(mixed_self, weight_o, 1)

    normed_two, inverse_two = norm_stats(hidden_one)
    input_two = both((normed_two * gains[1]).astype(BF16))
    query_cross = dot(input_two, cross_q, 1, 0).astype(BF16).reshape(length, -1, HEAD_DIM)
    key_cross = dot(cond_rows, cross_k, 1, 0).astype(BF16).reshape(ctx_len, -1, HEAD_DIM)
    value_cross = dot(cond_rows, cross_v, 1, 0).astype(BF16).reshape(ctx_len, -1, HEAD_DIM)
    mixed_cross, log_cross = attend_forward(query_cross, key_cross, value_cross)
    mixed_cross = mixed_cross.reshape(length, -1).astype(BF16)
    hidden_two = hidden_one + project(mixed_cross, cross_o, 1)

    normed_three, inverse_three = norm_stats(hidden_two)
    input_three = both((normed_three * gains[2]).astype(BF16))
    gate_pre = dot(input_three, weight_gate, 1, 0)
    up_pre = dot(input_three, weight_up, 1, 0)
    gate_sigmoid = jax.nn.sigmoid(gate_pre)
    gate_silu = gate_pre * gate_sigmoid
    hidden_ff = (gate_silu * up_pre).astype(BF16)
    block_out = hidden_two + project(hidden_ff, gath_d, 1)

    error_diff = block_out - teacher[0].astype(F32)
    local_error = jnp.sum(mask_float[:, None] * error_diff * error_diff)
    token_total = float(dp_size * lax.axis_size("tensor") * rows)
    grad_out = 2.0 * token_total / valid_count * mask_float[:, None] * error_diff

    def half_grad(row_side, column_side):
        kept = half_of(column_side, pair)
        sent = half_of(column_side, 1 - pair)
        return (
            dot(row_side, kept, 0, 0) + dot(to_core(row_side), to_core(sent), 0, 0)
        ).astype(BF16)

    def scatter(grads):
        return lax.psum_scatter(
            jnp.concatenate(grads, axis=1) if len(grads) > 1 else grads[0],
            "ring",
            scatter_dimension=0,
            tiled=True,
        )

    def finish(scattered, count):
        kept = lax.dynamic_slice(scattered, (pair * slab, 0), (slab, scattered.shape[1]))
        sent = lax.dynamic_slice(scattered, ((1 - pair) * slab, 0), (slab, scattered.shape[1]))
        got = to_core(sent)
        first = jnp.where(pair == 0, kept, got).astype(F32)
        second = jnp.where(pair == 0, got, kept).astype(F32)
        part = scattered.shape[1] // count
        return [
            jnp.concatenate(
                [first[:, i * part : (i + 1) * part], second[:, i * part : (i + 1) * part]], axis=1
            )
            for i in range(count)
        ]

    branch_three = both(grad_out.astype(BF16))
    scat_down = scatter([half_grad(branch_three, hidden_ff)])
    grad_hidden = dot(branch_three, gath_d, 1, 0)
    grad_gate = (
        grad_hidden * up_pre * gate_sigmoid * (1.0 + gate_pre * (1.0 - gate_sigmoid))
    ).astype(BF16)
    grad_upper = (grad_hidden * gate_silu).astype(BF16)

    def pull_ff(part):
        return dot(grad_gate[part], weight_gate, 1, 1) + dot(grad_upper[part], weight_up, 1, 1)

    away = to_peer(pull_ff(slice(rows, length)).astype(BF16))
    grad_normed_three = pull_ff(slice(0, rows)) + away.astype(F32)
    scat_ff = scatter([half_grad(input_three, grad_gate), half_grad(input_three, grad_upper)])
    back_three, gain_three = norm_back(grad_normed_three, normed_three, inverse_three, gains[2])
    grad_two = grad_out + back_three

    branch_two = both(grad_two.astype(BF16))
    grad_mixed_cross = dot(branch_two, cross_o, 1, 0).astype(BF16).reshape(length, -1, HEAD_DIM)
    grad_qc, grad_kc, grad_vc = attend_back(
        query_cross, key_cross, value_cross, log_cross, grad_mixed_cross
    )
    grad_qc = grad_qc.reshape(length, -1).astype(BF16)
    grad_kc = grad_kc.reshape(ctx_len, -1).astype(BF16)
    grad_vc = grad_vc.reshape(ctx_len, -1).astype(BF16)
    cond_part = (dot(grad_kc, cross_k, 1, 1) + dot(grad_vc, cross_v, 1, 1)).astype(BF16)
    cond_sum = cond_part.astype(F32) + to_peer(cond_part).astype(F32)
    grad_normed_two = project(grad_qc, cross_q, 1)
    back_two, gain_two = norm_back(grad_normed_two, normed_two, inverse_two, gains[1])
    grad_one = grad_two + back_two

    branch_one = both(grad_one.astype(BF16))
    grad_mixed_self = dot(branch_one, weight_o, 1, 0).astype(BF16).reshape(length, -1, HEAD_DIM)
    scat_attn = scatter(
        [
            half_grad(branch_one, mixed_self),
            half_grad(input_two, grad_qc),
            half_grad(cond_rows, grad_kc),
            half_grad(cond_rows, grad_vc),
            half_grad(branch_two, mixed_cross),
        ]
    )
    grad_qs, grad_ks, grad_vs = attend_back(
        query_rot, key_rot, value_self, log_self, grad_mixed_self
    )
    grad_qs = rotate(grad_qs, rot_cos, -rot_sin).reshape(length, -1).astype(BF16)
    grad_ks = rotate(grad_ks, rot_cos, -rot_sin).reshape(length, -1).astype(BF16)
    grad_vs = grad_vs.reshape(length, -1).astype(BF16)
    scat_qkv = scatter(
        [
            half_grad(input_one, grad_qs),
            half_grad(input_one, grad_ks),
            half_grad(input_one, grad_vs),
        ]
    )
    grad_qkv = jnp.concatenate([grad_qs, grad_ks, grad_vs], axis=1)
    grad_normed_one = project(grad_qkv, weight_qkv, 1)
    back_one, gain_one = norm_back(grad_normed_one, normed_one, inverse_one, gains[0])
    grad_rows = grad_one + back_one

    small = jnp.concatenate(
        [
            jnp.stack([gain_one, gain_two, gain_three]),
            jnp.full((1, width), local_error, F32),
        ],
        axis=0,
    )
    small = lax.psum(small, ("ring", "core", "tensor"))
    mean_loss = small[3, 0] / (width * valid_count)
    place = (lax.axis_index("ring") * 2 + pair) * slab
    grad_gains = lax.dynamic_slice(small, (0, place), (3, slab))

    (down_t,) = finish(scat_down, 1)
    gate_s, up_s = finish(scat_ff, 2)
    out_t, cq_s, ck_s, cv_s, co_t = finish(scat_attn, 5)
    q_s, k_s, v_s = finish(scat_qkv, 3)
    return (
        block_out.astype(BF16)[None],
        mean_loss,
        grad_rows[None],
        cond_sum[None],
        q_s,
        k_s,
        v_s,
        out_t.T,
        cq_s,
        ck_s,
        cv_s,
        co_t.T,
        gate_s,
        up_s,
        down_t.T,
        grad_gains,
    )


def solution(mesh):
    dp_size, share = mesh.shape["dp"], mesh.shape["tensor"]
    fine = Mesh(mesh.devices.reshape(dp_size // 2, 2, share), ("ring", "core", "tensor"))
    dp = ("ring", "core")
    tokens = P(dp, "tensor", None)
    by_row = P(dp, "tensor")
    by_column = P("tensor", dp)
    return jax.shard_map(
        body,
        mesh=fine,
        in_specs=(
            tokens,
            P(dp, None, None),
            tokens,
            by_row,
            P(None, dp),
            by_row,
            by_row,
            by_row,
            by_column,
            by_row,
            by_row,
            by_row,
            by_column,
            by_row,
            by_row,
            by_column,
        ),
        out_specs=(
            tokens,
            P(),
            tokens,
            P(dp, None, None),
            by_row,
            by_row,
            by_row,
            by_column,
            by_row,
            by_row,
            by_row,
            by_column,
            by_row,
            by_row,
            by_column,
            P(None, dp),
        ),
        check_vma=False,
    )
```

```python
import functools
import math

import jax
import jax.numpy as jnp
from jax import lax
from jax.experimental import pallas as pl
from jax.experimental.pallas import tpu as pltpu
from jax.sharding import Mesh, PartitionSpec as P

HEAD_DIM = 64
PAIR = 2 * HEAD_DIM
SCALE = HEAD_DIM**-0.5
EPSILON = 1e-05
F32 = jnp.float32
BF16 = jnp.bfloat16
KERNEL_VMEM = 24 << 20
PACK_VMEM = 56 << 20
GRAD_VMEM = 32 << 20
BACK_VMEM = 44 << 20
DOWN_PIECES = (768, 512, 256)
GATE_PIECES = (1024, 512)
UP_PIECES = (256, 1280)
PULL_ROWS = 256
NORM_ROWS = 128
FEED_COLUMNS = 512
SMALL_COST = pl.CostEstimate(flops=1 << 20, bytes_accessed=1 << 14, transcendentals=0)


def dot(left, right, left_dim, right_dim):
    return lax.dot_general(
        left, right, (((left_dim,), (right_dim,)), ((), ())), preferred_element_type=F32
    )


def norm_stats(values):
    row_mean = jnp.mean(values, axis=-1, keepdims=True)
    centred = values - row_mean
    row_var = jnp.mean(centred * centred, axis=-1, keepdims=True)
    inverse = lax.rsqrt(row_var + EPSILON)
    return (centred * inverse, inverse)


def rotary_tables(positions):
    half_dim = HEAD_DIM // 2
    freqs = jnp.exp(jnp.arange(half_dim, dtype=F32) * (-math.log(10000.0) / half_dim))
    angles = positions.astype(F32)[:, None] * freqs[None, :]
    cosine, sine = jnp.cos(angles), jnp.sin(angles)
    return (
        jnp.concatenate([cosine] * 4, axis=1),
        jnp.concatenate([-sine, sine] * 2, axis=1),
    )


def spin(values, cosines, sines):
    lane = lax.broadcasted_iota(jnp.int32, values.shape, 1)
    ahead = pltpu.roll(values, PAIR - HEAD_DIM // 2, 1)
    behind = pltpu.roll(values, HEAD_DIM // 2, 1)
    other = jnp.where(lane % HEAD_DIM < HEAD_DIM // 2, ahead, behind)
    return values * cosines + other * sines


def one_head(values, head):
    lane = lax.broadcasted_iota(jnp.int32, values.shape, 1)
    return jnp.where(lane // HEAD_DIM == head, values, jnp.zeros_like(values))


def turn(values):
    return values.astype(F32).T.astype(BF16)


def attend(keys, key_count, queries, values_t, out_ref, log_ref):
    mixed = []
    for head in range(2):
        scores = dot(keys, one_head(queries, head), 1, 1)
        if key_count < keys.shape[0]:
            row = lax.broadcasted_iota(jnp.int32, scores.shape, 0)
            scores = jnp.where(row < key_count, scores, -1e30)
        top = jnp.max(scores, axis=0, keepdims=True)
        shifted = jnp.exp(scores - top)
        total = jnp.sum(shifted, axis=0, keepdims=True)
        part = values_t[head * HEAD_DIM : (head + 1) * HEAD_DIM]
        mixed.append(dot(part, shifted.astype(BF16), 1, 0) / total)
        log_ref[0, head : head + 1, :] = top + jnp.log(total)
    out_ref[...] = jnp.concatenate(mixed, axis=0).T.astype(BF16)


def attend_back(queries, keys, key_count, values, grads, logs):
    keys_t = keys.astype(F32).T.astype(BF16)
    grad_k = jnp.zeros((keys.shape[0], PAIR), F32)
    grad_v = jnp.zeros((keys.shape[0], PAIR), F32)
    grad_q = []
    for head in range(2):
        query, grad = one_head(queries, head), one_head(grads, head)
        probs = jnp.exp(dot(keys, query, 1, 1) - logs[head : head + 1])
        if key_count < keys.shape[0]:
            row = lax.broadcasted_iota(jnp.int32, probs.shape, 0)
            probs = jnp.where(row < key_count, probs, 0.0)
        product = probs * dot(values, grad, 1, 1)
        weighted = jnp.sum(product, axis=0, keepdims=True)
        grad_s = (product - probs * weighted).astype(BF16)
        grad_v = grad_v + dot(probs.astype(BF16), grad, 1, 0)
        grad_k = grad_k + dot(grad_s, query, 1, 0)
        grad_q.append(dot(keys_t[head * HEAD_DIM : (head + 1) * HEAD_DIM], grad_s, 1, 0))
    return (jnp.concatenate(grad_q, axis=0).T * SCALE, grad_k, grad_v)


def self_forward_kernel(qkv, cos_in, sin_in, mixed, q_out, k_out, v_out, logs):
    cosines, sines = cos_in[...], sin_in[...]
    queries = spin(qkv[:, :PAIR], cosines, sines).astype(BF16).astype(F32)
    queries = (queries * SCALE).astype(BF16)
    keys = spin(qkv[:, PAIR : 2 * PAIR], cosines, sines).astype(BF16)
    values = qkv[:, 2 * PAIR :]
    q_out[...] = queries
    k_out[...] = keys
    v_out[...] = values.astype(BF16)
    attend(keys, keys.shape[0], queries, values.T.astype(BF16), mixed, logs)


def self_back_kernel(
    places, q_in, k_in, v_in, own_in, peer_in, out_w, qkv_w, logs, cos_in, sin_in,
    out, sent, own_out, peer_out, peer_sum,
):
    pair, pairs = pl.program_id(0), pl.num_programs(0)
    cosines, sines = cos_in[...], -sin_in[...]
    keys, weights = k_in[...], out_w[...]
    grads = jnp.concatenate([dot(own_in[...], weights, 1, 0), dot(peer_in[...], weights, 1, 0)], axis=0)
    grad_q, grad_k, grad_v = attend_back(
        q_in[...], keys, keys.shape[0], v_in[...], grads.astype(BF16), logs[0]
    )
    out[:, :PAIR] = spin(grad_q, cosines, sines).astype(BF16)
    out[:, PAIR : 2 * PAIR] = spin(grad_k, cosines, sines).astype(BF16)
    out[:, 2 * PAIR :] = grad_v.astype(BF16)

    @pl.when((2 * pair >= pairs) == (places[1] == 0))
    def _():
        sent[...] = out[...]

    rows = own_in.shape[0]
    own = dot(out[:rows, :], qkv_w[...], 1, 1)
    peer = dot(out[rows:, :], qkv_w[...], 1, 1)

    @pl.when(pair == 0)
    def _():
        own_out[...] = own
        peer_sum[...] = peer

    @pl.when(pair > 0)
    def _():
        own_out[...] += own
        peer_sum[...] += peer

    @pl.when(pair == pairs - 1)
    def _():
        peer_out[...] = peer_sum[...].astype(BF16)


def pick(own, peer):
    return jnp.where(2 * pl.program_id(0) < pl.num_programs(0), own[...], peer[...])


def cross_forward_kernel(key_count, q_own, q_peer, kv_own, kv_peer, mixed, logs):
    queries, keyvals = pick(q_own, q_peer), pick(kv_own, kv_peer)
    queries = (queries.astype(F32) * SCALE).astype(BF16)
    attend(keyvals[:, :PAIR], key_count, queries, turn(keyvals[:, PAIR:]), mixed, logs)


def cross_back_kernel(
    key_count, q_own, q_peer, g_own, g_peer, kv_own, kv_peer, logs, q_out, kv_out
):
    queries, keyvals = pick(q_own, q_peer), pick(kv_own, kv_peer)
    queries = (queries.astype(F32) * SCALE).astype(BF16)
    grad_q, grad_k, grad_v = attend_back(
        queries, keyvals[:, :PAIR], key_count, keyvals[:, PAIR:], pick(g_own, g_peer), logs[0]
    )
    q_out[...] = grad_q.astype(BF16)
    kv_out[:, :PAIR] = grad_k.astype(BF16)
    kv_out[:, PAIR:] = grad_v.astype(BF16)


def column_block(count):
    return pl.BlockSpec((count, PAIR), lambda i: (0, i))


def call_pairs(kernel, width, in_specs, out_specs, out_shape, args):
    return pl.pallas_call(
        kernel,
        grid=(width // PAIR,),
        in_specs=in_specs,
        out_specs=out_specs,
        out_shape=out_shape,
        compiler_params=pltpu.CompilerParams(vmem_limit_bytes=KERNEL_VMEM),
        cost_estimate=SMALL_COST,
    )(*args)


def self_forward(qkv, cosines, sines):
    rows, width = qkv.shape[0], qkv.shape[1] // 3
    pairs = width // PAIR
    table = pl.BlockSpec((rows, PAIR), lambda i: (0, 0))
    act = jax.ShapeDtypeStruct((rows, width), BF16)
    return call_pairs(
        self_forward_kernel,
        width,
        [pl.BlockSpec((rows, 3 * PAIR), lambda i: (0, i)), table, table],
        [column_block(rows)] * 4 + [pl.BlockSpec((1, 2, rows), lambda i: (i, 0, 0))],
        [act] * 4 + [jax.ShapeDtypeStruct((pairs, 2, rows), F32)],
        (qkv, cosines, sines),
    )


def self_back(places, queries, keys, values, own, peer, weights, logs, cosines, sines):
    rows, width = queries.shape
    count, depth = own.shape
    pairs = width // PAIR
    block = pl.BlockSpec((rows, PAIR), lambda i, places: (0, i))
    table = pl.BlockSpec((rows, PAIR), lambda i, places: (0, 0))
    token = pl.BlockSpec((count, depth), lambda i, places: (0, 0))
    half = pairs // 2
    return pl.pallas_call(
        self_back_kernel,
        grid_spec=pltpu.PrefetchScalarGridSpec(
            num_scalar_prefetch=1,
            grid=(pairs,),
            in_specs=[
                block,
                block,
                block,
                token,
                token,
                pl.BlockSpec((depth, PAIR), lambda i, places: (0, 3 * pairs + i)),
                pl.BlockSpec((depth, 3 * PAIR), lambda i, places: (0, i)),
                pl.BlockSpec((1, 2, rows), lambda i, places: (i, 0, 0)),
                table,
                table,
            ],
            out_specs=[
                pl.BlockSpec((rows, 3 * PAIR), lambda i, places: (0, i)),
                pl.BlockSpec(
                    (rows, 3 * PAIR),
                    lambda i, places: (0, jnp.clip(i - half * (1 - places[1]), 0, half - 1)),
                ),
                token,
                token,
            ],
            scratch_shapes=[pltpu.VMEM((count, depth), F32)],
        ),
        out_shape=[
            jax.ShapeDtypeStruct((rows, 3 * width), BF16),
            jax.ShapeDtypeStruct((rows, 3 * width // 2), BF16),
            jax.ShapeDtypeStruct((count, depth), F32),
            jax.ShapeDtypeStruct((count, depth), BF16),
        ],
        compiler_params=pltpu.CompilerParams(vmem_limit_bytes=BACK_VMEM),
        cost_estimate=SMALL_COST,
    )(places, queries, keys, values, own, peer, weights, weights, logs, cosines, sines)


def cross_call(kernel, key_count, arrays, logs, out_specs, out_shape):
    pairs = arrays[0][0].shape[1] // PAIR
    specs, args = [], []
    for own, peer in arrays:
        block = (own.shape[0], own.shape[1] // pairs)
        specs.append(pl.BlockSpec(block, lambda i: (0, jnp.minimum(i, pairs - 1))))
        specs.append(pl.BlockSpec(block, lambda i: (0, jnp.maximum(i - pairs, 0))))
        args += [own, peer]
    if logs is not None:
        specs.append(pl.BlockSpec((1,) + logs.shape[1:], lambda i: (i, 0, 0)))
        args.append(logs)
    return pl.pallas_call(
        functools.partial(kernel, key_count),
        grid=(2 * pairs,),
        in_specs=specs,
        out_specs=out_specs,
        out_shape=out_shape,
        compiler_params=pltpu.CompilerParams(vmem_limit_bytes=KERNEL_VMEM),
        cost_estimate=SMALL_COST,
    )(*args)


def cross_forward(queries, keyvals, key_count):
    rows, width = queries[0].shape
    return cross_call(
        cross_forward_kernel,
        key_count,
        (queries, keyvals),
        None,
        [column_block(rows), pl.BlockSpec((1, 2, rows), lambda i: (i, 0, 0))],
        [
            jax.ShapeDtypeStruct((rows, 2 * width), BF16),
            jax.ShapeDtypeStruct((2 * width // PAIR, 2, rows), F32),
        ],
    )


def cross_back(queries, grads, keyvals, logs, key_count):
    rows, width = queries[0].shape
    keys = keyvals[0].shape[0]
    return cross_call(
        cross_back_kernel,
        key_count,
        (queries, grads, keyvals),
        logs,
        [column_block(rows), pl.BlockSpec((keys, 2 * PAIR), lambda i: (0, i))],
        [
            jax.ShapeDtypeStruct((rows, 2 * width), BF16),
            jax.ShapeDtypeStruct((keys, 4 * width), BF16),
        ],
    )


def norm_back_kernel(away, *refs):
    pulled, peer = refs[0], refs[1] if away else None
    hidden, gain_row, skip, total_out, low_out, gain_out = refs[1 + away :]
    grad = pulled[...] + peer[...].astype(F32) if away else pulled[...]
    normed, inverse = norm_stats(hidden[...].astype(F32))
    scaled = grad * gain_row[...]
    mean_scaled = jnp.mean(scaled, axis=-1, keepdims=True)
    mean_product = jnp.mean(scaled * normed, axis=-1, keepdims=True)
    total = skip[...] + inverse * (scaled - mean_scaled - normed * mean_product)
    total_out[...] = total
    low_out[...] = total.astype(BF16)
    received = jnp.sum(grad * normed, axis=0, keepdims=True)

    @pl.when(pl.program_id(0) == 0)
    def _():
        gain_out[...] = received

    @pl.when(pl.program_id(0) > 0)
    def _():
        gain_out[...] += received


def norm_back(pulled, away, hidden, gain_row, skip):
    rows, depth = pulled.shape
    block = pl.BlockSpec((NORM_ROWS, depth), lambda i: (i, 0))
    row = pl.BlockSpec((1, depth), lambda i: (0, 0))
    arrays = (pulled,) if away is None else (pulled, away)
    return pl.pallas_call(
        functools.partial(norm_back_kernel, len(arrays) - 1),
        grid=(rows // NORM_ROWS,),
        in_specs=[block] * len(arrays) + [block, row, block],
        out_specs=[block, block, row],
        out_shape=[
            jax.ShapeDtypeStruct((rows, depth), F32),
            jax.ShapeDtypeStruct((rows, depth), BF16),
            jax.ShapeDtypeStruct((1, depth), F32),
        ],
        compiler_params=pltpu.CompilerParams(vmem_limit_bytes=KERNEL_VMEM),
        cost_estimate=SMALL_COST,
    )(*arrays, hidden, gain_row, skip)


def feed_back_kernel(places, g_in, weights, gate_in, up_in, gate_out, up_out, sent):
    grad_hidden = dot(g_in[...], weights[...], 1, 0)
    gate_pre, up_pre = gate_in[...].astype(F32), up_in[...].astype(F32)
    sigmoid = 1.0 / (1.0 + jnp.exp(-gate_pre))
    grad_gate = grad_hidden * up_pre * sigmoid * (1.0 + gate_pre * (1.0 - sigmoid))
    gate_out[...] = grad_gate.astype(BF16)
    up_out[...] = (grad_hidden * (gate_pre * sigmoid)).astype(BF16)

    @pl.when((2 * pl.program_id(0) >= pl.num_programs(0)) == (places[1] == 0))
    def _():
        sent[0] = gate_out[...]
        sent[1] = up_out[...]


def feed_back(places, grads, weights, gate_pre, up_pre, part):
    rows, depth = grads.shape
    width = gate_pre.shape[1]
    steps = width // FEED_COLUMNS
    half = steps // 2
    column = pl.BlockSpec((rows, FEED_COLUMNS), lambda i, places: (0, i))
    row_part = pl.BlockSpec((rows, FEED_COLUMNS), lambda i, places: (part, i))
    act = jax.ShapeDtypeStruct((rows, width), BF16)
    return pl.pallas_call(
        feed_back_kernel,
        grid_spec=pltpu.PrefetchScalarGridSpec(
            num_scalar_prefetch=1,
            grid=(steps,),
            in_specs=[
                pl.BlockSpec((rows, depth), lambda i, places: (0, 0)),
                pl.BlockSpec((depth, FEED_COLUMNS), lambda i, places: (0, 2 * steps + i)),
                row_part,
                row_part,
            ],
            out_specs=[
                column,
                column,
                pl.BlockSpec(
                    (2, rows, FEED_COLUMNS),
                    lambda i, places: (0, 0, jnp.clip(i - half * (1 - places[1]), 0, half - 1)),
                ),
            ],
        ),
        out_shape=[act, act, jax.ShapeDtypeStruct((2, rows, width // 2), BF16)],
        compiler_params=pltpu.CompilerParams(vmem_limit_bytes=BACK_VMEM),
        cost_estimate=SMALL_COST,
    )(places, grads, weights, gate_pre, up_pre)


def weight_grad_kernel(count, pieces, group, places, *refs):
    outs = refs[2 * count :]
    total = dot(refs[0][...], refs[1][...], 0, 0)
    for index in range(1, count):
        total = total + dot(refs[2 * index][...], refs[2 * index + 1][...], 0, 0)

    def side(index):
        starts = range(index * group, total.shape[0], 2 * group)
        parts = [total[at : at + group] for at in starts]
        return (jnp.concatenate(parts, axis=0) if len(parts) > 1 else parts[0]).astype(BF16)

    first, second = side(0), side(1)

    def write(values, targets):
        at = 0
        for piece, target in zip(pieces, targets, strict=True):
            target[...] = values[:, at : at + piece]
            at += piece

    @pl.when(places[0] == 0)
    def _():
        write(first, outs[: len(pieces)])
        write(second, outs[len(pieces) :])

    @pl.when(places[0] != 0)
    def _():
        write(second, outs[: len(pieces)])
        write(first, outs[len(pieces) :])


def weight_grad(places, far, pieces, parts):
    columns = sum(pieces)
    sides = [[side if isinstance(side, tuple) else (side, None) for side in part[:2]] for part in parts]
    depth = sides[0][0][0].shape[1]
    block = math.lcm(depth // far, 128)
    specs, args = [], []
    for ((left, left_half), (right, right_half)), (_, _, at) in zip(sides, parts, strict=True):
        tokens = left.shape[0] if left_half is None else left.shape[0] // 2
        first, second = left_half or 0, right_half or 0
        specs.append(pl.BlockSpec((tokens, block), lambda i, places, first=first: (first, i)))
        if at is None:
            spec = pl.BlockSpec(
                (tokens, columns), lambda i, places, second=second: (second, places[1])
            )
        elif right.ndim == 3:
            spec = pl.BlockSpec(
                (pl.Squeezed(), tokens, columns), lambda i, places, at=at: (at, 0, 0)
            )
        else:
            spec = pl.BlockSpec(
                (tokens, columns), lambda i, places, second=second, at=at: (second, at)
            )
        specs.append(spec)
        args += [left, right]
    outs = pl.pallas_call(
        functools.partial(weight_grad_kernel, len(parts), pieces, depth // far // 2),
        grid_spec=pltpu.PrefetchScalarGridSpec(
            num_scalar_prefetch=1,
            grid=(depth // block,),
            in_specs=specs,
            out_specs=[
                pl.BlockSpec((block // 2, piece), lambda i, places: (i, 0)) for piece in 2 * pieces
            ],
        ),
        out_shape=[jax.ShapeDtypeStruct((depth // 2, piece), BF16) for piece in 2 * pieces],
        compiler_params=pltpu.CompilerParams(vmem_limit_bytes=GRAD_VMEM),
        cost_estimate=SMALL_COST,
    )(places, *args)
    return outs[: len(pieces)], outs[len(pieces) :]


def pull_kernel(gate_in, up_in, weights, out):
    width = gate_in.shape[1]
    total = dot(gate_in[...], weights[:, :width], 1, 1) + dot(up_in[...], weights[:, width:], 1, 1)
    out[...] = total.astype(out.dtype)


def pull(grad_gate, grad_upper, weights, kind):
    rows, width = grad_gate.shape
    depth = weights.shape[0]
    whole = pl.BlockSpec((rows, width), lambda i: (0, 0))
    return pl.pallas_call(
        pull_kernel,
        grid=(depth // PULL_ROWS,),
        in_specs=[whole, whole, pl.BlockSpec((PULL_ROWS, 2 * width), lambda i: (i, 0))],
        out_specs=pl.BlockSpec((rows, PULL_ROWS), lambda i: (0, i)),
        out_shape=jax.ShapeDtypeStruct((rows, depth), kind),
        compiler_params=pltpu.CompilerParams(vmem_limit_bytes=GRAD_VMEM),
        cost_estimate=SMALL_COST,
    )(grad_gate, grad_upper, weights)


def pack_attention_kernel(q_in, k_in, v_in, o_in, cq_in, ck_in, cv_in, co_in, gains, mask, out):
    width = q_in.shape[1]
    for pair in range(width // PAIR):
        for index, ref in enumerate((q_in, k_in, v_in)):
            at = (3 * pair + index) * PAIR
            out[:, at : at + PAIR] = ref[:, pair * PAIR : (pair + 1) * PAIR]
    out[:, 3 * width : 4 * width] = turn(o_in[...])
    for pair in range(width // PAIR):
        for index, ref in enumerate((ck_in, cv_in)):
            at = 4 * width + (2 * pair + index) * PAIR
            out[:, at : at + PAIR] = ref[:, pair * PAIR : (pair + 1) * PAIR]
    out[:, 6 * width : 7 * width] = cq_in[...]
    out[:, 7 * width : 8 * width] = turn(co_in[...])
    count = jnp.sum(mask[...].astype(F32), axis=1, keepdims=True)
    upper = jnp.floor(count * (1.0 / 128.0))
    side = gains[...].astype(F32).T
    row = lax.broadcasted_iota(jnp.int32, side.shape, 0)
    lane = lax.broadcasted_iota(jnp.int32, side.shape, 1)
    side = jnp.where((lane == 3) & (row == 0), upper, side)
    side = jnp.where((lane == 3) & (row == 1), count - 128.0 * upper, side)
    out[:, 8 * width :] = side.astype(BF16)


def pack_feed_kernel(gate_in, up_in, down_in, out):
    width = gate_in.shape[1]
    out[:, :width] = gate_in[...]
    out[:, width : 2 * width] = up_in[...]
    out[:, 2 * width :] = turn(down_in[...])


def pack(kernel, columns, *parts):
    return pl.pallas_call(
        kernel,
        out_shape=jax.ShapeDtypeStruct((parts[0].shape[0], columns), BF16),
        compiler_params=pltpu.CompilerParams(vmem_limit_bytes=PACK_VMEM),
    )(*parts)


def after(value, *earlier):
    return lax.optimization_barrier((value, *earlier))[0]


def body(
    x_input,
    cond_tokens,
    teacher,
    valid_mask,
    norm_gains,
    w_query,
    w_key,
    w_value,
    w_out,
    c_query,
    c_key,
    c_value,
    c_out,
    w_gate,
    w_up,
    w_down,
):
    far = lax.axis_size("far")
    near_at, pair, share = (lax.axis_index(name) for name in ("near", "core", "tensor"))
    dp_axes = ("far", "near", "core")
    dp_size = 4 * far
    swap = [(0, 1), (1, 0)]

    def to_peer(values):
        return lax.ppermute(values, "tensor", swap)

    def to_core(values):
        return lax.ppermute(values, "core", swap)

    def to_near(values):
        return lax.ppermute(values, "near", swap)

    def gather(values):
        return lax.all_gather(values, dp_axes, axis=0, tiled=True)

    x_bf = x_input[0]
    rows, width = x_bf.shape
    slab = w_query.shape[0]
    heads_width = w_query.shape[1]
    ff_width = w_gate.shape[1]
    length = 2 * rows
    ctx_len = cond_tokens.shape[1]
    cond_rows = jnp.pad(cond_tokens[0], ((0, -ctx_len % 16), (0, 0)))
    mask_float = valid_mask[0].astype(F32)
    x_peer_bf = to_peer(x_bf)

    gath_a = gather(
        pack(
            pack_attention_kernel,
            8 * heads_width + PAIR,
            w_query,
            w_key,
            w_value,
            w_out,
            c_query,
            c_key,
            c_value,
            c_out,
            jnp.pad(norm_gains, ((0, PAIR - 3), (0, 0))),
            valid_mask,
        )
    )
    gath_b = gather(pack(pack_feed_kernel, 3 * ff_width, w_gate, w_up, w_down))

    weight_qkv = gath_a[:, : 3 * heads_width]
    weight_o = gath_a[:, 3 * heads_width : 4 * heads_width]
    cross_kv = gath_a[:, 4 * heads_width : 6 * heads_width]
    side = gath_a[:, 8 * heads_width :].T[:8].astype(F32)
    gains = side[:3]
    counts = side[3].reshape(dp_size, slab)
    part_count = jnp.sum(counts[:, 0]) * 128.0 + jnp.sum(counts[:, 1])
    part_count = jnp.full((8, 128), part_count, F32)
    valid_count = (part_count + to_peer(part_count))[0, 0]
    half_ff, half_heads = ff_width // 2, heads_width // 2
    places = jnp.stack([near_at, pair]).astype(jnp.int32)

    def fetch_peer(first):
        return to_peer(
            lax.dynamic_slice(
                gath_a, (pair * (width // 2), first * heads_width), (width // 2, heads_width)
            )
        )

    def join_cores(got):
        other = to_core(got)
        return jnp.concatenate(
            [jnp.where(pair == 0, got, other), jnp.where(pair == 0, other, got)], axis=0
        )

    cross_q_own = gath_a[:, 6 * heads_width : 7 * heads_width]
    cross_o_own = gath_a[:, 7 * heads_width : 8 * heads_width]
    cross_q_peer = fetch_peer(6)

    local_rows = x_bf.astype(F32)
    normed_one, _ = norm_stats(local_rows)
    peer_one, _ = norm_stats(x_peer_bf.astype(F32))
    input_one = jnp.concatenate(
        [(normed_one * gains[0]).astype(BF16), (peer_one * gains[0]).astype(BF16)], axis=0
    )
    order = lax.iota(jnp.int32, length)
    positions = jnp.where(order < rows, order + share * rows, order - share * rows)
    cosines, sines = rotary_tables(positions)
    def half_of(values, index):
        half = values.shape[1] // 2
        return lax.dynamic_slice(values, (0, index * half), (values.shape[0], half))

    def other_half(values):
        return to_core(half_of(values, 1 - pair))

    def project(values, weight, weight_dim, *meanwhile):
        away = to_peer(dot(values[rows:], weight, 1, weight_dim).astype(BF16))
        mine = dot(values[:rows], weight, 1, weight_dim)
        return mine + after(away, mine, *meanwhile).astype(F32)

    qkv = dot(input_one, weight_qkv, 1, 0)
    mixed_self, query_self, key_self, value_self, logs_self = self_forward(qkv, cosines, sines)
    cross_q_peer = join_cores(after(cross_q_peer, mixed_self))
    cross_o_peer = fetch_peer(7)
    keyvals_own = dot(cond_rows, cross_kv, 1, 0).astype(BF16)
    keyvals_peer = to_peer(keyvals_own)
    core_one = to_core(input_one)
    hidden_one = local_rows + project(mixed_self, weight_o, 1, core_one, cross_q_peer)

    normed_two, _ = norm_stats(hidden_one)
    own_two = (normed_two * gains[1]).astype(BF16)
    query_cross = tuple(
        dot(own_two, weight, 1, 0).astype(BF16) for weight in (cross_q_own, cross_q_peer)
    )
    keyvals = (keyvals_own, after(keyvals_peer, own_two))
    mixed_cross, logs_cross = cross_forward(query_cross, keyvals, ctx_len)
    cross_o_peer = join_cores(after(cross_o_peer, mixed_cross))
    hidden_two = (
        hidden_one
        + dot(mixed_cross[:, :heads_width], cross_o_own, 1, 1)
        + dot(mixed_cross[:, heads_width:], cross_o_peer, 1, 1)
    )

    normed_three, _ = norm_stats(hidden_two)
    own_three = (normed_three * gains[2]).astype(BF16)
    peer_three = to_peer(own_three)
    core_mixed_self, core_cond = other_half(mixed_self), to_core(cond_rows)
    peer_three = after(peer_three, core_mixed_self, core_cond)
    input_three = jnp.concatenate([own_three, peer_three], axis=0)
    weight_gate = gath_b[:, :ff_width]
    weight_up = gath_b[:, ff_width : 2 * ff_width]
    weight_down = gath_b[:, 2 * ff_width :]
    gate_pre = dot(input_three, weight_gate, 1, 0).astype(BF16)
    up_sum = dot(input_three, weight_up, 1, 0)
    gate_sum = gate_pre.astype(F32)
    hidden_ff = (gate_sum * jax.nn.sigmoid(gate_sum) * up_sum).astype(BF16)
    up_pre = up_sum.astype(BF16)
    core_three, core_hidden = to_core(input_three), other_half(hidden_ff)
    block_out = hidden_two + project(hidden_ff, weight_down, 1, core_three, core_hidden)

    error_diff = block_out - teacher[0].astype(F32)
    local_error = jnp.sum(mask_float[:, None] * error_diff * error_diff)
    token_total = float(dp_size * lax.axis_size("tensor") * rows)
    grad_out = 2.0 * token_total / valid_count * mask_float[:, None] * error_diff

    def grad_of(pieces, *parts):
        return weight_grad(places, far, pieces, parts)

    landed, scattered = [], []

    def launch(sent, *events):
        return to_near(after(sent, *events))

    def land(got, kept, *events):
        got = after(got, *events, *scattered[:-1])
        landed.append((kept.astype(F32) + got.astype(F32)).astype(BF16))
        scattered.append(scatter(landed[-1]))
        return scattered[-1]

    def scatter(summed):
        return lax.psum_scatter(summed, "far", scatter_dimension=0, tiled=True)

    def finish(scattered):
        columns = scattered.shape[1]
        kept = lax.dynamic_slice(scattered, (pair * slab, 0), (slab, columns))
        got = to_core(lax.dynamic_slice(scattered, ((1 - pair) * slab, 0), (slab, columns)))
        first = jnp.where(pair == 0, kept, got).astype(F32)
        second = jnp.where(pair == 0, got, kept).astype(F32)
        return (first, second)

    def columns_at(sides, places, size):
        return jnp.concatenate(
            [side[:, at : at + size] for side in sides for at in places], axis=1
        )

    own_e3 = grad_out.astype(BF16)
    peer_e3 = to_peer(own_e3)
    core_own_e3 = to_core(own_e3)

    def row(index):
        return gains[index : index + 1]

    dgate_own, dup_own, halves_own = feed_back(places, own_e3, gath_b, gate_pre, up_pre, 0)
    core_own_halves = to_core(halves_own)
    pulled_own = pull(dgate_own, dup_own, gath_b, F32)
    peer_e3 = after(peer_e3, pulled_own)
    core_peer_e3 = to_core(peer_e3)
    peer_two = to_peer(after(own_two, peer_e3))
    peer_mixed = to_peer(after(mixed_cross, peer_e3)[:, heads_width:])
    dgate_peer, dup_peer, halves_peer = feed_back(places, peer_e3, gath_b, gate_pre, up_pre, 1)
    kept_down, sent_down = grad_of(
        DOWN_PIECES,
        (own_e3, (hidden_ff, 0), None),
        (after(peer_e3, dgate_peer), (hidden_ff, 1), None),
        (core_own_e3, (core_hidden, 0), 0),
        (core_peer_e3, (core_hidden, 1), 0),
    )
    near_down = launch(sent_down[0])
    dgate_peer, dup_peer, _ = lax.optimization_barrier((dgate_peer, dup_peer, sent_down[0]))
    core_peer_halves = to_core(halves_peer)
    pulled_peer, peer_two, peer_mixed = lax.optimization_barrier(
        (pull(dgate_peer, dup_peer, gath_b, BF16), peer_two, peer_mixed)
    )
    away = to_peer(pulled_peer)

    def feed_grad(pieces, own, peer, at, *earlier):
        return grad_of(
            pieces,
            (own_three, after(own, *earlier), None),
            (peer_three, peer, None),
            ((core_three, 0), core_own_halves, at),
            ((core_three, 1), core_peer_halves, at),
        )

    kept_gate, sent_gate = feed_grad(GATE_PIECES, dgate_own, dgate_peer, 0, pulled_peer)
    scat_down = [land(near_down, kept_down[0], sent_gate[0])]
    near_down = launch(sent_down[1], landed[-1])
    kept_up, sent_up = feed_grad(UP_PIECES, dup_own, dup_peer, 1, sent_gate[0])
    scat_down.append(land(near_down, kept_down[1], sent_up[0]))
    near_gate = launch(sent_gate[0], landed[-1])
    grad_two, own_e2, gain_three = norm_back(
        pulled_own, after(away, landed[-1]), hidden_two, row(2), grad_out
    )

    grad_mixed = tuple(
        dot(own_e2, weight, 1, 0).astype(BF16) for weight in (cross_o_own, cross_o_peer)
    )
    grad_qc, grad_kv = cross_back(query_cross, grad_mixed, keyvals, logs_cross, ctx_len)
    pulled_two = dot(grad_qc[:, :heads_width], cross_q_own, 1, 1) + dot(
        grad_qc[:, heads_width:], cross_q_peer, 1, 1
    )
    grad_one, own_e1, gain_two = norm_back(pulled_two, None, hidden_one, row(1), grad_two)

    peer_e1 = to_peer(own_e1)
    scat_gate = [land(near_gate, kept_gate[0], own_e1)]
    near_mid = launch(jnp.concatenate([sent_gate[1], sent_up[0]], axis=1), landed[-1])
    mid = land(near_mid, jnp.concatenate([kept_gate[1], kept_up[0]], axis=1), peer_e1)
    peer_e1 = after(peer_e1, landed[-1])
    near_up = launch(jnp.concatenate([sent_up[1], sent_down[2]], axis=1), landed[-1])
    peer_e2, peer_qc = to_peer(after(own_e2, peer_e1)), to_peer(after(grad_qc, peer_e1)[:, heads_width:])
    peer_kv = to_peer(after(grad_kv, peer_e1)[:, 2 * heads_width :])
    grad_qkv, halves_qkv, pulled_own, pulled_peer = self_back(
        places,
        query_self,
        key_self,
        value_self,
        own_e1,
        peer_e1,
        gath_a,
        logs_self,
        cosines,
        sines,
    )
    peer_e2, peer_qc, peer_kv, pulled_peer, grad_qkv = lax.optimization_barrier(
        (peer_e2, peer_qc, peer_kv, pulled_peer, grad_qkv)
    )
    away = to_peer(pulled_peer)
    core_qkv = to_core(halves_qkv)
    last_ff = land(near_up, jnp.concatenate([kept_up[1], kept_down[2]], axis=1), pulled_peer)
    kept_qkv, sent_qkv = grad_of(
        (3 * half_heads,),
        (input_one, after(grad_qkv, landed[-1]), None),
        (core_one, core_qkv, 0),
    )
    near_qkv = launch(sent_qkv[0])
    branch_one = jnp.concatenate([own_e1, peer_e1], axis=0)
    branch_two = jnp.concatenate([own_e2, peer_e2], axis=0)
    input_two = jnp.concatenate([own_two, peer_two], axis=0)
    mixed_two = jnp.concatenate([mixed_cross[:, :heads_width], peer_mixed], axis=0)
    both_qc = jnp.concatenate([grad_qc[:, :heads_width], peer_qc], axis=0)
    sum_kv = (grad_kv[:, : 2 * heads_width].astype(F32) + peer_kv.astype(F32)).astype(BF16)
    kept_wo, sent_wo = grad_of(
        (half_heads,),
        (branch_one, after(mixed_self, sent_qkv[0]), None),
        (to_core(after(branch_one, grad_qkv)), core_mixed_self, 0),
    )
    kept_co, sent_co = grad_of(
        (half_heads,),
        (branch_two, after(mixed_two, sent_wo[0]), None),
        (to_core(after(branch_two, sent_qkv[0])), other_half(mixed_two), 0),
    )
    kept_cq, sent_cq = grad_of(
        (half_heads,),
        (input_two, after(both_qc, sent_co[0]), None),
        (to_core(after(input_two, sent_wo[0])), other_half(both_qc), 0),
    )
    kept_ckv, sent_ckv = grad_of(
        (heads_width,),
        (cond_rows, after(sum_kv, sent_cq[0]), None),
        (core_cond, other_half(sum_kv), 0),
    )
    near_w = launch(jnp.concatenate(sent_wo + sent_co, axis=1))
    near_c = launch(jnp.concatenate(sent_cq + sent_ckv, axis=1))
    scat_qkv = land(near_qkv, kept_qkv[0], sent_ckv[0])
    grad_rows, _, gain_one = norm_back(
        pulled_own, after(away, landed[-1]), x_bf, row(0), grad_one
    )
    scat_w = land(near_w, jnp.concatenate(kept_wo + kept_co, axis=1), grad_rows)
    cond_part = dot(after(sum_kv, landed[-1]), cross_kv, 1, 1)[:ctx_len].astype(BF16)
    cond_sum = cond_part.astype(F32) + to_peer(cond_part).astype(F32)
    scat_c = land(near_c, jnp.concatenate(kept_cq + kept_ckv, axis=1), cond_part)

    small = jnp.concatenate(
        [gain_one, gain_two, gain_three, jnp.full((1, width), local_error, F32)],
        axis=0,
    )
    small = after(small, landed[-1])
    for axis in ("tensor", "core", "near", "far"):
        size = lax.axis_size(axis)
        if size & (size - 1):
            small = lax.psum(small, axis)
            continue
        hop = 1
        while hop < size:
            small = small + lax.ppermute(small, axis, [(i, i ^ hop) for i in range(size)])
            hop *= 2
    mean_loss = small[3, 0] / (width * valid_count)
    place = (lax.axis_index("far") * 4 + near_at * 2 + pair) * slab
    grad_gains = lax.dynamic_slice(small, (0, place), (3, slab))

    split = GATE_PIECES[1]
    gate_parts = scat_gate + [mid[:, :split]]
    up_parts = [mid[:, split:], last_ff[:, : UP_PIECES[1]]]
    down_parts = scat_down + [last_ff[:, UP_PIECES[1] :]]
    down_t, gate_s, up_s = (
        jnp.concatenate(finish(jnp.concatenate(parts, axis=1)), axis=1)
        for parts in (down_parts, gate_parts, up_parts)
    )
    sides = finish(scat_qkv)
    q_s, k_s, v_s = (
        columns_at(sides, range(i * PAIR, 3 * half_heads, 3 * PAIR), PAIR) for i in range(3)
    )
    sides = finish(scat_w)
    out_t, co_t = (columns_at(sides, [i * half_heads], half_heads) for i in range(2))
    sides = finish(scat_c)
    cq_s = columns_at(sides, [0], half_heads)
    ck_s, cv_s = (
        columns_at(sides, range(half_heads + i * PAIR, 3 * half_heads, 2 * PAIR), PAIR)
        for i in range(2)
    )
    return (
        block_out.astype(BF16)[None],
        mean_loss,
        grad_rows[None],
        cond_sum[None],
        q_s,
        k_s,
        v_s,
        out_t.T,
        cq_s,
        ck_s,
        cv_s,
        co_t.T,
        gate_s,
        up_s,
        down_t.T,
        grad_gains,
    )


def solution(mesh):
    dp_size, share = mesh.shape["dp"], mesh.shape["tensor"]
    fine = Mesh(
        mesh.devices.reshape(dp_size // 4, 2, 2, share), ("far", "near", "core", "tensor")
    )
    dp = ("far", "near", "core")
    tokens = P(dp, "tensor", None)
    per_latent = P(dp, None, None)
    by_row = P(dp, "tensor")
    by_column = P("tensor", dp)
    weights = (by_row,) * 3 + (by_column,) + (by_row,) * 3 + (by_column, by_row, by_row, by_column)
    return jax.shard_map(
        body,
        mesh=fine,
        in_specs=(tokens, per_latent, tokens, by_row, P(None, dp)) + weights,
        out_specs=(tokens, P(), tokens, per_latent) + weights + (P(None, dp),),
        check_vma=False,
    )
```

```python
import functools
import math

import jax
import jax.numpy as jnp
from jax import lax
from jax.experimental import pallas as pl
from jax.experimental.pallas import tpu as pltpu
from jax.sharding import Mesh, PartitionSpec as P

HEAD_DIM = 64
PAIR = 2 * HEAD_DIM
SCALE = HEAD_DIM**-0.5
EPSILON = 1e-05
F32 = jnp.float32
BF16 = jnp.bfloat16
KERNEL_VMEM = 60 << 20
PACK_VMEM = 60 << 20
GRAD_VMEM = 60 << 20
BACK_VMEM = 60 << 20
DOWN_PIECES = (768, 512, 256)
GATE_PIECES = (1408, 128)
UP_PIECES = (768, 768)
PULL_ROWS = 256
NORM_ROWS = 128
FEED_COLUMNS = 512
SMALL_COST = pl.CostEstimate(flops=1 << 20, bytes_accessed=1 << 14, transcendentals=0)


def dot(left, right, left_dim, right_dim):
    return lax.dot_general(
        left, right, (((left_dim,), (right_dim,)), ((), ())), preferred_element_type=F32
    )


def norm_stats(values):
    row_mean = jnp.mean(values, axis=-1, keepdims=True)
    centred = values - row_mean
    row_var = jnp.mean(centred * centred, axis=-1, keepdims=True)
    inverse = lax.rsqrt(row_var + EPSILON)
    return (centred * inverse, inverse)


def rotary_tables(positions):
    half_dim = HEAD_DIM // 2
    freqs = jnp.exp(jnp.arange(half_dim, dtype=F32) * (-math.log(10000.0) / half_dim))
    angles = positions.astype(F32)[:, None] * freqs[None, :]
    cosine, sine = jnp.cos(angles), jnp.sin(angles)
    return (
        jnp.concatenate([cosine] * 4, axis=1),
        jnp.concatenate([-sine, sine] * 2, axis=1),
    )


def spin(values, cosines, sines):
    lane = lax.broadcasted_iota(jnp.int32, values.shape, 1)
    ahead = pltpu.roll(values, PAIR - HEAD_DIM // 2, 1)
    behind = pltpu.roll(values, HEAD_DIM // 2, 1)
    other = jnp.where(lane % HEAD_DIM < HEAD_DIM // 2, ahead, behind)
    return values * cosines + other * sines


def one_head(values, head):
    lane = lax.broadcasted_iota(jnp.int32, values.shape, 1)
    return jnp.where(lane // HEAD_DIM == head, values, jnp.zeros_like(values))


def turn(values):
    return values.astype(F32).T.astype(BF16)


def attend(keys, key_count, queries, values_t, out_ref, log_ref):
    mixed = []
    for head in range(2):
        scores = dot(keys, one_head(queries, head), 1, 1)
        if key_count < keys.shape[0]:
            row = lax.broadcasted_iota(jnp.int32, scores.shape, 0)
            scores = jnp.where(row < key_count, scores, -1e30)
        top = jnp.max(scores, axis=0, keepdims=True)
        shifted = jnp.exp(scores - top)
        total = jnp.sum(shifted, axis=0, keepdims=True)
        part = values_t[head * HEAD_DIM : (head + 1) * HEAD_DIM]
        mixed.append(dot(part, shifted.astype(BF16), 1, 0) / total)
        log_ref[0, head : head + 1, :] = top + jnp.log(total)
    out_ref[...] = jnp.concatenate(mixed, axis=0).T.astype(BF16)


def attend_back(queries, keys, key_count, values, grads, logs):
    keys_t = keys.astype(F32).T.astype(BF16)
    grad_k = jnp.zeros((keys.shape[0], PAIR), F32)
    grad_v = jnp.zeros((keys.shape[0], PAIR), F32)
    grad_q = []
    for head in range(2):
        query, grad = one_head(queries, head), one_head(grads, head)
        probs = jnp.exp(dot(keys, query, 1, 1) - logs[head : head + 1])
        if key_count < keys.shape[0]:
            row = lax.broadcasted_iota(jnp.int32, probs.shape, 0)
            probs = jnp.where(row < key_count, probs, 0.0)
        product = probs * dot(values, grad, 1, 1)
        weighted = jnp.sum(product, axis=0, keepdims=True)
        grad_s = (product - probs * weighted).astype(BF16)
        grad_v = grad_v + dot(probs.astype(BF16), grad, 1, 0)
        grad_k = grad_k + dot(grad_s, query, 1, 0)
        grad_q.append(dot(keys_t[head * HEAD_DIM : (head + 1) * HEAD_DIM], grad_s, 1, 0))
    return (jnp.concatenate(grad_q, axis=0).T * SCALE, grad_k, grad_v)


def self_forward_kernel(qkv, cos_in, sin_in, mixed, q_out, k_out, v_out, logs):
    cosines, sines = cos_in[...], sin_in[...]
    queries = spin(qkv[:, :PAIR], cosines, sines).astype(BF16).astype(F32)
    queries = (queries * SCALE).astype(BF16)
    keys = spin(qkv[:, PAIR : 2 * PAIR], cosines, sines).astype(BF16)
    values = qkv[:, 2 * PAIR :]
    q_out[...] = queries
    k_out[...] = keys
    v_out[...] = values.astype(BF16)
    attend(keys, keys.shape[0], queries, values.T.astype(BF16), mixed, logs)


def self_back_kernel(
    places, q_in, k_in, v_in, own_in, peer_in, out_w, qkv_w, logs, cos_in, sin_in,
    out, sent, own_out, peer_out, peer_sum,
):
    pair, pairs = pl.program_id(0), pl.num_programs(0)
    cosines, sines = cos_in[...], -sin_in[...]
    keys, weights = k_in[...], out_w[...]
    grads = jnp.concatenate([dot(own_in[...], weights, 1, 0), dot(peer_in[...], weights, 1, 0)], axis=0)
    grad_q, grad_k, grad_v = attend_back(
        q_in[...], keys, keys.shape[0], v_in[...], grads.astype(BF16), logs[0]
    )
    out[:, :PAIR] = spin(grad_q, cosines, sines).astype(BF16)
    out[:, PAIR : 2 * PAIR] = spin(grad_k, cosines, sines).astype(BF16)
    out[:, 2 * PAIR :] = grad_v.astype(BF16)

    @pl.when((2 * pair >= pairs) == (places[1] == 0))
    def _():
        sent[...] = out[...]

    rows = own_in.shape[0]
    own = dot(out[:rows, :], qkv_w[...], 1, 1)
    peer = dot(out[rows:, :], qkv_w[...], 1, 1)

    @pl.when(pair == 0)
    def _():
        own_out[...] = own
        peer_sum[...] = peer

    @pl.when(pair > 0)
    def _():
        own_out[...] += own
        peer_sum[...] += peer

    @pl.when(pair == pairs - 1)
    def _():
        peer_out[...] = peer_sum[...].astype(BF16)


def pick(own, peer):
    return jnp.where(2 * pl.program_id(0) < pl.num_programs(0), own[...], peer[...])


def cross_forward_kernel(key_count, q_own, q_peer, kv_own, kv_peer, mixed, logs):
    queries, keyvals = pick(q_own, q_peer), pick(kv_own, kv_peer)
    queries = (queries.astype(F32) * SCALE).astype(BF16)
    attend(keyvals[:, :PAIR], key_count, queries, turn(keyvals[:, PAIR:]), mixed, logs)


def cross_back_kernel(
    key_count, q_own, q_peer, g_own, g_peer, kv_own, kv_peer, logs, q_out, kv_out
):
    queries, keyvals = pick(q_own, q_peer), pick(kv_own, kv_peer)
    queries = (queries.astype(F32) * SCALE).astype(BF16)
    grad_q, grad_k, grad_v = attend_back(
        queries, keyvals[:, :PAIR], key_count, keyvals[:, PAIR:], pick(g_own, g_peer), logs[0]
    )
    q_out[...] = grad_q.astype(BF16)
    kv_out[:, :PAIR] = grad_k.astype(BF16)
    kv_out[:, PAIR:] = grad_v.astype(BF16)


def column_block(count):
    return pl.BlockSpec((count, PAIR), lambda i: (0, i))


def call_pairs(kernel, width, in_specs, out_specs, out_shape, args):
    return pl.pallas_call(
        kernel,
        grid=(width // PAIR,),
        in_specs=in_specs,
        out_specs=out_specs,
        out_shape=out_shape,
        compiler_params=pltpu.CompilerParams(vmem_limit_bytes=KERNEL_VMEM),
        cost_estimate=SMALL_COST,
    )(*args)


def self_forward(qkv, cosines, sines):
    rows, width = qkv.shape[0], qkv.shape[1] // 3
    pairs = width // PAIR
    table = pl.BlockSpec((rows, PAIR), lambda i: (0, 0))
    act = jax.ShapeDtypeStruct((rows, width), BF16)
    return call_pairs(
        self_forward_kernel,
        width,
        [pl.BlockSpec((rows, 3 * PAIR), lambda i: (0, i)), table, table],
        [column_block(rows)] * 4 + [pl.BlockSpec((1, 2, rows), lambda i: (i, 0, 0))],
        [act] * 4 + [jax.ShapeDtypeStruct((pairs, 2, rows), F32)],
        (qkv, cosines, sines),
    )


def self_back(places, queries, keys, values, own, peer, weights, logs, cosines, sines):
    rows, width = queries.shape
    count, depth = own.shape
    pairs = width // PAIR
    block = pl.BlockSpec((rows, PAIR), lambda i, places: (0, i))
    table = pl.BlockSpec((rows, PAIR), lambda i, places: (0, 0))
    token = pl.BlockSpec((count, depth), lambda i, places: (0, 0))
    half = pairs // 2
    return pl.pallas_call(
        self_back_kernel,
        grid_spec=pltpu.PrefetchScalarGridSpec(
            num_scalar_prefetch=1,
            grid=(pairs,),
            in_specs=[
                block,
                block,
                block,
                token,
                token,
                pl.BlockSpec((depth, PAIR), lambda i, places: (0, 3 * pairs + i)),
                pl.BlockSpec((depth, 3 * PAIR), lambda i, places: (0, i)),
                pl.BlockSpec((1, 2, rows), lambda i, places: (i, 0, 0)),
                table,
                table,
            ],
            out_specs=[
                pl.BlockSpec((rows, 3 * PAIR), lambda i, places: (0, i)),
                pl.BlockSpec(
                    (rows, 3 * PAIR),
                    lambda i, places: (0, jnp.clip(i - half * (1 - places[1]), 0, half - 1)),
                ),
                token,
                token,
            ],
            scratch_shapes=[pltpu.VMEM((count, depth), F32)],
        ),
        out_shape=[
            jax.ShapeDtypeStruct((rows, 3 * width), BF16),
            jax.ShapeDtypeStruct((rows, 3 * width // 2), BF16),
            jax.ShapeDtypeStruct((count, depth), F32),
            jax.ShapeDtypeStruct((count, depth), BF16),
        ],
        compiler_params=pltpu.CompilerParams(vmem_limit_bytes=BACK_VMEM),
        cost_estimate=SMALL_COST,
    )(places, queries, keys, values, own, peer, weights, weights, logs, cosines, sines)


def cross_call(kernel, key_count, arrays, logs, out_specs, out_shape):
    pairs = arrays[0][0].shape[1] // PAIR
    specs, args = [], []
    for own, peer in arrays:
        block = (own.shape[0], own.shape[1] // pairs)
        specs.append(pl.BlockSpec(block, lambda i: (0, jnp.minimum(i, pairs - 1))))
        specs.append(pl.BlockSpec(block, lambda i: (0, jnp.maximum(i - pairs, 0))))
        args += [own, peer]
    if logs is not None:
        specs.append(pl.BlockSpec((1,) + logs.shape[1:], lambda i: (i, 0, 0)))
        args.append(logs)
    return pl.pallas_call(
        functools.partial(kernel, key_count),
        grid=(2 * pairs,),
        in_specs=specs,
        out_specs=out_specs,
        out_shape=out_shape,
        compiler_params=pltpu.CompilerParams(vmem_limit_bytes=KERNEL_VMEM),
        cost_estimate=SMALL_COST,
    )(*args)


def cross_forward(queries, keyvals, key_count):
    rows, width = queries[0].shape
    return cross_call(
        cross_forward_kernel,
        key_count,
        (queries, keyvals),
        None,
        [column_block(rows), pl.BlockSpec((1, 2, rows), lambda i: (i, 0, 0))],
        [
            jax.ShapeDtypeStruct((rows, 2 * width), BF16),
            jax.ShapeDtypeStruct((2 * width // PAIR, 2, rows), F32),
        ],
    )


def cross_back(queries, grads, keyvals, logs, key_count):
    rows, width = queries[0].shape
    keys = keyvals[0].shape[0]
    return cross_call(
        cross_back_kernel,
        key_count,
        (queries, grads, keyvals),
        logs,
        [column_block(rows), pl.BlockSpec((keys, 2 * PAIR), lambda i: (0, i))],
        [
            jax.ShapeDtypeStruct((rows, 2 * width), BF16),
            jax.ShapeDtypeStruct((keys, 4 * width), BF16),
        ],
    )


def norm_back_kernel(away, *refs):
    pulled, peer = refs[0], refs[1] if away else None
    hidden, gain_row, skip, total_out, low_out, gain_out = refs[1 + away :]
    grad = pulled[...] + peer[...].astype(F32) if away else pulled[...]
    normed, inverse = norm_stats(hidden[...].astype(F32))
    scaled = grad * gain_row[...]
    mean_scaled = jnp.mean(scaled, axis=-1, keepdims=True)
    mean_product = jnp.mean(scaled * normed, axis=-1, keepdims=True)
    total = skip[...] + inverse * (scaled - mean_scaled - normed * mean_product)
    total_out[...] = total
    low_out[...] = total.astype(BF16)
    received = jnp.sum(grad * normed, axis=0, keepdims=True)

    @pl.when(pl.program_id(0) == 0)
    def _():
        gain_out[...] = received

    @pl.when(pl.program_id(0) > 0)
    def _():
        gain_out[...] += received


def norm_back(pulled, away, hidden, gain_row, skip):
    rows, depth = pulled.shape
    block = pl.BlockSpec((NORM_ROWS, depth), lambda i: (i, 0))
    row = pl.BlockSpec((1, depth), lambda i: (0, 0))
    arrays = (pulled,) if away is None else (pulled, away)
    return pl.pallas_call(
        functools.partial(norm_back_kernel, len(arrays) - 1),
        grid=(rows // NORM_ROWS,),
        in_specs=[block] * len(arrays) + [block, row, block],
        out_specs=[block, block, row],
        out_shape=[
            jax.ShapeDtypeStruct((rows, depth), F32),
            jax.ShapeDtypeStruct((rows, depth), BF16),
            jax.ShapeDtypeStruct((1, depth), F32),
        ],
        compiler_params=pltpu.CompilerParams(vmem_limit_bytes=KERNEL_VMEM),
        cost_estimate=SMALL_COST,
    )(*arrays, hidden, gain_row, skip)


def feed_back_kernel(places, g_in, weights, gate_in, up_in, gate_out, up_out, sent):
    grad_hidden = dot(g_in[...], weights[...], 1, 0)
    gate_pre, up_pre = gate_in[...].astype(F32), up_in[...].astype(F32)
    sigmoid = 1.0 / (1.0 + jnp.exp(-gate_pre))
    grad_gate = grad_hidden * up_pre * sigmoid * (1.0 + gate_pre * (1.0 - sigmoid))
    gate_out[...] = grad_gate.astype(BF16)
    up_out[...] = (grad_hidden * (gate_pre * sigmoid)).astype(BF16)

    @pl.when((2 * pl.program_id(0) >= pl.num_programs(0)) == (places[1] == 0))
    def _():
        sent[0] = gate_out[...]
        sent[1] = up_out[...]


def feed_back(places, grads, weights, gate_pre, up_pre, part):
    rows, depth = grads.shape
    width = gate_pre.shape[1]
    steps = width // FEED_COLUMNS
    half = steps // 2
    column = pl.BlockSpec((rows, FEED_COLUMNS), lambda i, places: (0, i))
    row_part = pl.BlockSpec((rows, FEED_COLUMNS), lambda i, places: (part, i))
    act = jax.ShapeDtypeStruct((rows, width), BF16)
    return pl.pallas_call(
        feed_back_kernel,
        grid_spec=pltpu.PrefetchScalarGridSpec(
            num_scalar_prefetch=1,
            grid=(steps,),
            in_specs=[
                pl.BlockSpec((rows, depth), lambda i, places: (0, 0)),
                pl.BlockSpec((depth, FEED_COLUMNS), lambda i, places: (0, 2 * steps + i)),
                row_part,
                row_part,
            ],
            out_specs=[
                column,
                column,
                pl.BlockSpec(
                    (2, rows, FEED_COLUMNS),
                    lambda i, places: (0, 0, jnp.clip(i - half * (1 - places[1]), 0, half - 1)),
                ),
            ],
        ),
        out_shape=[act, act, jax.ShapeDtypeStruct((2, rows, width // 2), BF16)],
        compiler_params=pltpu.CompilerParams(vmem_limit_bytes=BACK_VMEM),
        cost_estimate=SMALL_COST,
    )(places, grads, weights, gate_pre, up_pre)


def weight_grad_kernel(count, pieces, group, places, *refs):
    outs = refs[2 * count :]
    total = dot(refs[0][...], refs[1][...], 0, 0)
    for index in range(1, count):
        total = total + dot(refs[2 * index][...], refs[2 * index + 1][...], 0, 0)

    def side(index):
        starts = range(index * group, total.shape[0], 2 * group)
        parts = [total[at : at + group] for at in starts]
        return (jnp.concatenate(parts, axis=0) if len(parts) > 1 else parts[0]).astype(BF16)

    first, second = side(0), side(1)

    def write(values, targets):
        at = 0
        for piece, target in zip(pieces, targets, strict=True):
            target[...] = values[:, at : at + piece]
            at += piece

    @pl.when(places[0] == 0)
    def _():
        write(first, outs[: len(pieces)])
        write(second, outs[len(pieces) :])

    @pl.when(places[0] != 0)
    def _():
        write(second, outs[: len(pieces)])
        write(first, outs[len(pieces) :])


def weight_grad(places, far, pieces, parts):
    columns = sum(pieces)
    sides = [[side if isinstance(side, tuple) else (side, None) for side in part[:2]] for part in parts]
    depth = sides[0][0][0].shape[1]
    block = math.lcm(depth // far, 128)
    specs, args = [], []
    for ((left, left_half), (right, right_half)), (_, _, at) in zip(sides, parts, strict=True):
        tokens = left.shape[0] if left_half is None else left.shape[0] // 2
        first, second = left_half or 0, right_half or 0
        specs.append(pl.BlockSpec((tokens, block), lambda i, places, first=first: (first, i)))
        if at is None:
            spec = pl.BlockSpec(
                (tokens, columns), lambda i, places, second=second: (second, places[1])
            )
        elif right.ndim == 3:
            spec = pl.BlockSpec(
                (pl.Squeezed(), tokens, columns), lambda i, places, at=at: (at, 0, 0)
            )
        else:
            spec = pl.BlockSpec(
                (tokens, columns), lambda i, places, second=second, at=at: (second, at)
            )
        specs.append(spec)
        args += [left, right]
    outs = pl.pallas_call(
        functools.partial(weight_grad_kernel, len(parts), pieces, depth // far // 2),
        grid_spec=pltpu.PrefetchScalarGridSpec(
            num_scalar_prefetch=1,
            grid=(depth // block,),
            in_specs=specs,
            out_specs=[
                pl.BlockSpec((block // 2, piece), lambda i, places: (i, 0)) for piece in 2 * pieces
            ],
        ),
        out_shape=[jax.ShapeDtypeStruct((depth // 2, piece), BF16) for piece in 2 * pieces],
        compiler_params=pltpu.CompilerParams(vmem_limit_bytes=GRAD_VMEM),
        cost_estimate=SMALL_COST,
    )(places, *args)
    return outs[: len(pieces)], outs[len(pieces) :]


def whole_call(kernel, out_shape, *args):
    return pl.pallas_call(
        kernel,
        out_shape=out_shape,
        compiler_params=pltpu.CompilerParams(vmem_limit_bytes=BACK_VMEM),
        cost_estimate=SMALL_COST,
    )(*args)


def join_kernel(axis, *refs):
    refs[-1][...] = jnp.concatenate([ref[...] for ref in refs[:-1]], axis=axis)


def join(axis, *parts):
    shape = list(parts[0].shape)
    shape[axis] = sum(part.shape[axis] for part in parts)
    return whole_call(
        functools.partial(join_kernel, axis), jax.ShapeDtypeStruct(shape, parts[0].dtype), *parts
    )


def near_sum_kernel(*refs):
    got, out = refs[-2:]
    at = 0
    for ref in refs[:-2]:
        end = at + ref.shape[1]
        out[:, at:end] = (ref[...].astype(F32) + got[:, at:end].astype(F32)).astype(BF16)
        at = end


def near_sum(kept, got):
    rows, columns = got.shape
    block = rows // 4 if rows % 64 == 0 else rows

    def spec(width):
        return pl.BlockSpec((block, width), lambda i: (i, 0))

    return pl.pallas_call(
        near_sum_kernel,
        grid=(rows // block,),
        in_specs=[spec(part.shape[1]) for part in kept] + [spec(columns)],
        out_specs=spec(columns),
        out_shape=jax.ShapeDtypeStruct(got.shape, BF16),
        compiler_params=pltpu.CompilerParams(vmem_limit_bytes=KERNEL_VMEM),
        cost_estimate=SMALL_COST,
    )(*kept, got)


def other_half_kernel(places, *refs):
    out, at = refs[-1], 0
    for ref in refs[:-1]:
        out[at : at + ref.shape[0], :] = ref[...]
        at += ref.shape[0]


def other_half(places, width, *parts):
    half = width // 2
    rows = sum(part.shape[0] for part in parts)
    return pl.pallas_call(
        other_half_kernel,
        grid_spec=pltpu.PrefetchScalarGridSpec(
            num_scalar_prefetch=1,
            grid=(1,),
            in_specs=[
                pl.BlockSpec((part.shape[0], half), lambda i, places: (0, 1 - places[1]))
                for part in parts
            ],
            out_specs=pl.BlockSpec((rows, half), lambda i, places: (0, 0)),
        ),
        out_shape=jax.ShapeDtypeStruct((rows, half), BF16),
        compiler_params=pltpu.CompilerParams(vmem_limit_bytes=KERNEL_VMEM),
        cost_estimate=SMALL_COST,
    )(places, *parts)


def mixed_back_kernel(g_in, own_w, peer_w, own_out, peer_out):
    own_out[...] = dot(g_in[...], own_w[...], 1, 0).astype(BF16)
    peer_out[...] = dot(g_in[...], peer_w[...], 1, 0).astype(BF16)


def mixed_back(grads, weights, at, peer_weights):
    rows, depth = grads.shape
    width = peer_weights.shape[1]
    half = width // 2
    act = jax.ShapeDtypeStruct((rows, width), BF16)
    return pl.pallas_call(
        mixed_back_kernel,
        grid=(2,),
        in_specs=[
            pl.BlockSpec((rows, depth), lambda i: (0, 0)),
            pl.BlockSpec((depth, half), lambda i: (0, 2 * at + i)),
            pl.BlockSpec((depth, half), lambda i: (0, i)),
        ],
        out_specs=[pl.BlockSpec((rows, half), lambda i: (0, i))] * 2,
        out_shape=[act, act],
        compiler_params=pltpu.CompilerParams(vmem_limit_bytes=KERNEL_VMEM),
        cost_estimate=SMALL_COST,
    )(grads, weights, peer_weights)


def pull_query_kernel(g_in, own_w, peer_w, out):
    width = own_w.shape[1]
    out[...] = dot(g_in[:, :width], own_w[...], 1, 1) + dot(g_in[:, width:], peer_w[...], 1, 1)


def pull_query(grads, weights, at, peer_weights):
    rows = grads.shape[0]
    depth, width = peer_weights.shape
    return pl.pallas_call(
        pull_query_kernel,
        grid=(depth // PULL_ROWS,),
        in_specs=[
            pl.BlockSpec(grads.shape, lambda i: (0, 0)),
            pl.BlockSpec((PULL_ROWS, width), lambda i: (i, at)),
            pl.BlockSpec((PULL_ROWS, width), lambda i: (i, 0)),
        ],
        out_specs=pl.BlockSpec((rows, PULL_ROWS), lambda i: (0, i)),
        out_shape=jax.ShapeDtypeStruct((rows, depth), F32),
        compiler_params=pltpu.CompilerParams(vmem_limit_bytes=KERNEL_VMEM),
        cost_estimate=SMALL_COST,
    )(grads, weights, peer_weights)


def pull_kernel(gate_in, up_in, weights, out):
    width = gate_in.shape[1]
    total = dot(gate_in[...], weights[:, :width], 1, 1) + dot(up_in[...], weights[:, width:], 1, 1)
    out[...] = total.astype(out.dtype)


def pull(grad_gate, grad_upper, weights, kind):
    rows, width = grad_gate.shape
    depth = weights.shape[0]
    whole = pl.BlockSpec((rows, width), lambda i: (0, 0))
    return pl.pallas_call(
        pull_kernel,
        grid=(depth // PULL_ROWS,),
        in_specs=[whole, whole, pl.BlockSpec((PULL_ROWS, 2 * width), lambda i: (i, 0))],
        out_specs=pl.BlockSpec((rows, PULL_ROWS), lambda i: (0, i)),
        out_shape=jax.ShapeDtypeStruct((rows, depth), kind),
        compiler_params=pltpu.CompilerParams(vmem_limit_bytes=GRAD_VMEM),
        cost_estimate=SMALL_COST,
    )(grad_gate, grad_upper, weights)


def meet(*values):
    return lax.optimization_barrier(values)


def pack_attention_kernel(q_in, k_in, v_in, o_in, cq_in, ck_in, cv_in, co_in, gains, mask, out):
    width = q_in.shape[1]
    for pair in range(width // PAIR):
        for index, ref in enumerate((q_in, k_in, v_in)):
            at = (3 * pair + index) * PAIR
            out[:, at : at + PAIR] = ref[:, pair * PAIR : (pair + 1) * PAIR]
    out[:, 3 * width : 4 * width] = turn(o_in[...])
    for pair in range(width // PAIR):
        for index, ref in enumerate((ck_in, cv_in)):
            at = 4 * width + (2 * pair + index) * PAIR
            out[:, at : at + PAIR] = ref[:, pair * PAIR : (pair + 1) * PAIR]
    out[:, 6 * width : 7 * width] = cq_in[...]
    out[:, 7 * width : 8 * width] = turn(co_in[...])
    count = jnp.sum(mask[...].astype(F32), axis=1, keepdims=True)
    upper = jnp.floor(count * (1.0 / 128.0))
    side = gains[...].astype(F32).T
    row = lax.broadcasted_iota(jnp.int32, side.shape, 0)
    lane = lax.broadcasted_iota(jnp.int32, side.shape, 1)
    side = jnp.where((lane == 3) & (row == 0), upper, side)
    side = jnp.where((lane == 3) & (row == 1), count - 128.0 * upper, side)
    out[:, 8 * width :] = side.astype(BF16)


def pack_feed_kernel(gate_in, up_in, down_in, out):
    width = gate_in.shape[1]
    out[:, :width] = gate_in[...]
    out[:, width : 2 * width] = up_in[...]
    out[:, 2 * width :] = turn(down_in[...])


def pack(kernel, columns, *parts):
    return pl.pallas_call(
        kernel,
        out_shape=jax.ShapeDtypeStruct((parts[0].shape[0], columns), BF16),
        compiler_params=pltpu.CompilerParams(vmem_limit_bytes=PACK_VMEM),
    )(*parts)


def after(value, *earlier):
    return lax.optimization_barrier((value, *earlier))[0]


def body(
    x_input,
    cond_tokens,
    teacher,
    valid_mask,
    norm_gains,
    w_query,
    w_key,
    w_value,
    w_out,
    c_query,
    c_key,
    c_value,
    c_out,
    w_gate,
    w_up,
    w_down,
):
    far = lax.axis_size("far")
    near_at, pair, share = (lax.axis_index(name) for name in ("near", "core", "tensor"))
    dp_axes = ("far", "near", "core")
    dp_size = 4 * far
    swap = [(0, 1), (1, 0)]

    def to_peer(values):
        return lax.ppermute(values, "tensor", swap)

    def to_core(values):
        return lax.ppermute(values, "core", swap)

    def to_near(values):
        return lax.ppermute(values, "near", swap)

    def gather(values):
        return lax.all_gather(values, dp_axes, axis=0, tiled=True)

    x_bf = x_input[0]
    rows, width = x_bf.shape
    slab = w_query.shape[0]
    heads_width = w_query.shape[1]
    ff_width = w_gate.shape[1]
    length = 2 * rows
    ctx_len = cond_tokens.shape[1]
    cond_rows = jnp.pad(cond_tokens[0], ((0, -ctx_len % 16), (0, 0)))
    mask_float = valid_mask[0].astype(F32)
    x_peer_bf = to_peer(x_bf)

    gath_a = gather(
        pack(
            pack_attention_kernel,
            8 * heads_width + PAIR,
            w_query,
            w_key,
            w_value,
            w_out,
            c_query,
            c_key,
            c_value,
            c_out,
            jnp.pad(norm_gains, ((0, PAIR - 3), (0, 0))),
            valid_mask,
        )
    )
    gath_b = gather(pack(pack_feed_kernel, 3 * ff_width, w_gate, w_up, w_down))

    weight_qkv = gath_a[:, : 3 * heads_width]
    weight_o = gath_a[:, 3 * heads_width : 4 * heads_width]
    cross_kv = gath_a[:, 4 * heads_width : 6 * heads_width]
    side = gath_a[:, 8 * heads_width :].T[:8].astype(F32)
    gains = side[:3]
    counts = side[3].reshape(dp_size, slab)
    part_count = jnp.sum(counts[:, 0]) * 128.0 + jnp.sum(counts[:, 1])
    part_count = jnp.full((8, 128), part_count, F32)
    valid_count = (part_count + to_peer(part_count))[0, 0]
    half_ff, half_heads = ff_width // 2, heads_width // 2
    places = jnp.stack([near_at, pair]).astype(jnp.int32)

    def fetch_peer(first):
        return to_peer(
            lax.dynamic_slice(
                gath_a, (pair * (width // 2), first * heads_width), (width // 2, heads_width)
            )
        )

    def join_cores(got):
        other = to_core(got)
        return jnp.concatenate(
            [jnp.where(pair == 0, got, other), jnp.where(pair == 0, other, got)], axis=0
        )

    cross_q_own = gath_a[:, 6 * heads_width : 7 * heads_width]
    cross_o_own = gath_a[:, 7 * heads_width : 8 * heads_width]
    cross_q_peer = fetch_peer(6)

    local_rows = x_bf.astype(F32)
    normed_one, _ = norm_stats(local_rows)
    peer_one, _ = norm_stats(x_peer_bf.astype(F32))
    input_one = jnp.concatenate(
        [(normed_one * gains[0]).astype(BF16), (peer_one * gains[0]).astype(BF16)], axis=0
    )
    order = lax.iota(jnp.int32, length)
    positions = jnp.where(order < rows, order + share * rows, order - share * rows)
    cosines, sines = rotary_tables(positions)
    def project(values, weight, weight_dim, *meanwhile):
        away = to_peer(dot(values[rows:], weight, 1, weight_dim).astype(BF16))
        mine = dot(values[:rows], weight, 1, weight_dim)
        return mine + after(away, mine, *meanwhile).astype(F32)

    qkv = dot(input_one, weight_qkv, 1, 0)
    mixed_self, query_self, key_self, value_self, logs_self = self_forward(qkv, cosines, sines)
    cross_q_peer = join_cores(after(cross_q_peer, mixed_self))
    cross_o_peer = fetch_peer(7)
    keyvals_own = dot(cond_rows, cross_kv, 1, 0).astype(BF16)
    keyvals_peer = to_peer(keyvals_own)
    core_one = to_core(input_one)
    hidden_one = local_rows + project(mixed_self, weight_o, 1, core_one, cross_q_peer)

    normed_two, _ = norm_stats(hidden_one)
    own_two = (normed_two * gains[1]).astype(BF16)
    query_cross = tuple(
        dot(own_two, weight, 1, 0).astype(BF16) for weight in (cross_q_own, cross_q_peer)
    )
    keyvals = (keyvals_own, after(keyvals_peer, own_two))
    mixed_cross, logs_cross = cross_forward(query_cross, keyvals, ctx_len)
    cross_o_peer = join_cores(after(cross_o_peer, mixed_cross))
    hidden_two = (
        hidden_one
        + dot(mixed_cross[:, :heads_width], cross_o_own, 1, 1)
        + dot(mixed_cross[:, heads_width:], cross_o_peer, 1, 1)
    )

    normed_three, _ = norm_stats(hidden_two)
    own_three = (normed_three * gains[2]).astype(BF16)
    peer_three = to_peer(own_three)
    core_mixed_self, core_cond = to_core(other_half(places, heads_width, mixed_self)), to_core(cond_rows)
    peer_three = after(peer_three, core_mixed_self, core_cond)
    input_three = jnp.concatenate([own_three, peer_three], axis=0)
    weight_gate = gath_b[:, :ff_width]
    weight_up = gath_b[:, ff_width : 2 * ff_width]
    weight_down = gath_b[:, 2 * ff_width :]
    gate_pre = dot(input_three, weight_gate, 1, 0).astype(BF16)
    up_sum = dot(input_three, weight_up, 1, 0)
    gate_sum = gate_pre.astype(F32)
    hidden_ff = (gate_sum * jax.nn.sigmoid(gate_sum) * up_sum).astype(BF16)
    up_pre = up_sum.astype(BF16)
    core_three = to_core(input_three)
    core_hidden = to_core(other_half(places, ff_width, hidden_ff))
    block_out = hidden_two + project(hidden_ff, weight_down, 1, core_three, core_hidden)

    error_diff = block_out - teacher[0].astype(F32)
    local_error = jnp.sum(mask_float[:, None] * error_diff * error_diff)
    token_total = float(dp_size * lax.axis_size("tensor") * rows)
    grad_out = 2.0 * token_total / valid_count * mask_float[:, None] * error_diff

    def grad_of(pieces, *parts):
        return weight_grad(places, far, pieces, parts)

    scattered = []

    def add_pair(kept, got):
        return near_sum(kept, after(got, *scattered[:-1]))

    def scatter_on(summed):
        scattered.append(scatter(summed))
        return scattered[-1]

    def scatter(summed):
        return lax.psum_scatter(summed, "far", scatter_dimension=0, tiled=True)

    def finish(scattered):
        columns = scattered.shape[1]
        kept = lax.dynamic_slice(scattered, (pair * slab, 0), (slab, columns))
        got = to_core(lax.dynamic_slice(scattered, ((1 - pair) * slab, 0), (slab, columns)))
        first = jnp.where(pair == 0, kept, got).astype(F32)
        second = jnp.where(pair == 0, got, kept).astype(F32)
        return (first, second)

    def columns_at(sides, places, size):
        return jnp.concatenate(
            [side[:, at : at + size] for side in sides for at in places], axis=1
        )

    own_e3 = grad_out.astype(BF16)
    peer_e3 = to_peer(own_e3)
    core_own_e3 = to_core(own_e3)

    def row(index):
        return gains[index : index + 1]

    dgate_own, dup_own, halves_own = feed_back(places, own_e3, gath_b, gate_pre, up_pre, 0)
    dgate_own, dup_own, halves_own, pulled_own, peer_e3, core_own_e3 = meet(
        dgate_own, dup_own, halves_own, pull(dgate_own, dup_own, gath_b, F32), peer_e3, core_own_e3
    )
    dgate_peer, dup_peer, halves_peer, core_peer_e3, core_own_halves = meet(
        *feed_back(places, peer_e3, gath_b, gate_pre, up_pre, 1),
        to_core(peer_e3),
        to_core(halves_own),
    )
    kept_down, sent_down = grad_of(
        DOWN_PIECES,
        (own_e3, (hidden_ff, 0), None),
        (peer_e3, (hidden_ff, 1), None),
        (core_own_e3, (core_hidden, 0), 0),
        (core_peer_e3, (core_hidden, 1), 0),
    )
    *sent_down, dgate_peer, dup_peer, halves_peer = meet(
        *sent_down, dgate_peer, dup_peer, halves_peer
    )
    near_a = to_near(sent_down[0])
    pulled_peer, core_peer_halves = meet(
        pull(dgate_peer, dup_peer, gath_b, BF16), to_core(halves_peer)
    )
    away = to_peer(pulled_peer)

    def feed_grad(pieces, own, peer, at):
        kept, sent = grad_of(
            pieces,
            (own_three, own, None),
            (peer_three, peer, None),
            ((core_three, 0), core_own_halves, at),
            ((core_three, 1), core_peer_halves, at),
        )
        return kept + sent

    *gate_w, near_a = meet(
        *feed_grad(GATE_PIECES, dgate_own, after(dgate_peer, pulled_peer), 0), near_a
    )
    near_b = to_near(after(sent_down[1], near_a))
    *up_w, sum_a, near_b, away = meet(
        *feed_grad(UP_PIECES, dup_own, after(dup_peer, gate_w[0]), 1),
        add_pair(kept_down[:1], near_a),
        near_b,
        away,
    )
    scat_down = [scatter_on(sum_a)]
    near_c = to_near(after(gate_w[2], near_b))
    peer_two = to_peer(after(own_two, away))
    peer_mixed = to_peer(after(mixed_cross, away)[:, heads_width:])
    grad_two, own_e2, gain_three = norm_back(pulled_own, away, hidden_two, row(2), grad_out)

    grad_mixed = mixed_back(own_e2, gath_a, 7, cross_o_peer)
    grad_qc, grad_kv = cross_back(query_cross, grad_mixed, keyvals, logs_cross, ctx_len)
    pulled_two = pull_query(grad_qc, gath_a, 6, cross_q_peer)
    grad_one, own_e1, gain_two = norm_back(pulled_two, None, hidden_one, row(1), grad_two)
    sum_b = add_pair(kept_down[1:2], near_b)
    scat_down.append(scatter_on(sum_b))
    sent_d = up_w[2]
    grad_one, own_e1, gain_two, sum_b, own_e2, sent_d, near_c, peer_two, peer_mixed = meet(
        grad_one, own_e1, gain_two, sum_b, own_e2, sent_d, near_c, peer_two, peer_mixed
    )

    near_d = to_near(sent_d)
    peer_e1 = to_peer(own_e1)
    input_two = join(0, own_two, peer_two)
    mixed_two = join(0, mixed_cross[:, :heads_width], peer_mixed)
    sum_c = add_pair(gate_w[:1], near_c)
    scat_gate = [scatter_on(sum_c)]
    sum_c, peer_e1, near_d, input_two, mixed_two, half_mixed = meet(
        sum_c,
        peer_e1,
        near_d,
        input_two,
        mixed_two,
        other_half(places, heads_width, mixed_two),
    )
    own_e2, grad_qc, _ = meet(own_e2, grad_qc, peer_e1)

    def head_grad(*parts):
        kept, sent = grad_of((half_heads,), *parts)
        return kept[0], sent[0]

    sum_d = add_pair([up_w[0]], near_d)
    mid = scatter_on(sum_d)
    branch_one = join(0, own_e1, peer_e1)
    sum_d, core_e1, branch_one = meet(sum_d, to_core(branch_one), branch_one)
    kept_wo, sent_wo = head_grad(
        (branch_one, mixed_self, None), (core_e1, core_mixed_self, 0)
    )
    kept_wo, sent_e = meet(kept_wo, join(1, up_w[3], sent_down[2], gate_w[3], sent_wo))
    near_e = to_near(sent_e)
    grad_qkv, halves_qkv, pulled_own, pulled_peer, peer_e2, peer_qc, near_e = meet(
        *self_back(
            places,
            query_self,
            key_self,
            value_self,
            own_e1,
            after(peer_e1, sent_e),
            gath_a,
            logs_self,
            cosines,
            sines,
        ),
        to_peer(own_e2),
        to_peer(grad_qc[:, heads_width:]),
        near_e,
    )
    away = to_peer(pulled_peer)
    sum_e = add_pair([up_w[1], kept_down[2], gate_w[1], kept_wo], near_e)
    last_ff = scatter_on(sum_e)
    sum_e, core_qkv = meet(sum_e, to_core(halves_qkv))
    piece = 3 * half_heads // 2 // PAIR * PAIR
    kept_qkv, sent_qkv = grad_of(
        (piece, 3 * half_heads - piece),
        (input_one, after(grad_qkv, sum_e), None),
        (core_one, core_qkv, 0),
    )
    *kept_qkv, sent_f, sent_g = meet(*kept_qkv, *sent_qkv)
    near_f = to_near(sent_f)
    both_qc = join(0, grad_qc[:, :heads_width], after(peer_qc, sent_f))
    branch_two, both_qc, half_qc, away, near_f = meet(
        join(0, own_e2, after(peer_e2, sent_f)),
        both_qc,
        other_half(places, heads_width, both_qc),
        away,
        near_f,
    )
    near_g = to_near(sent_g)
    sum_f = add_pair([kept_qkv[0]], near_f)
    scat_qkv = [scatter_on(sum_f)]
    core_e2, core_qc, core_two, core_mixed = (
        to_core(after(part, branch_two)) for part in (branch_two, half_qc, input_two, half_mixed)
    )
    sum_f, core_e2, core_mixed, core_qc, core_two = meet(
        sum_f, core_e2, core_mixed, core_qc, core_two
    )
    peer_kv = to_peer(after(grad_kv, sum_f)[:, 2 * heads_width :])
    kept_co, sent_co = head_grad((branch_two, mixed_two, None), (core_e2, core_mixed, 0))
    kept_cq, sent_cq = head_grad(
        (input_two, after(both_qc, sent_co), None), (core_two, core_qc, 0)
    )
    kept_co, kept_cq, sent_w, near_g, peer_kv = meet(
        kept_co, kept_cq, join(1, sent_co, sent_cq), near_g, peer_kv
    )
    near_w = to_near(sent_w)
    sum_g = add_pair([kept_qkv[1]], near_g)
    scat_qkv.append(scatter_on(sum_g))
    sum_kv = near_sum([grad_kv[:, : 2 * heads_width]], after(peer_kv, sum_g))
    sum_kv, half_kv = meet(sum_kv, other_half(places, 2 * heads_width, sum_kv))
    grad_rows, _, gain_one = norm_back(
        pulled_own, after(away, half_kv), x_bf, row(0), grad_one
    )
    grad_rows, gain_one, core_kv = meet(grad_rows, gain_one, to_core(half_kv))
    kept_ckv, sent_ckv = grad_of(
        (heads_width,), (cond_rows, after(sum_kv, grad_rows), None), (core_cond, core_kv, 0)
    )
    kept_ckv, sent_ckv, near_w, last_ff = meet(kept_ckv[0], sent_ckv[0], near_w, last_ff)
    near_c = to_near(sent_ckv)
    sum_w, *scat_qkv = meet(near_sum([kept_co, kept_cq], near_w), *scat_qkv)
    scat_w = scatter(sum_w)
    cond_part = dot(after(sum_kv, sum_w), cross_kv, 1, 1)[:ctx_len].astype(BF16)
    near_c, cond_part = meet(near_c, cond_part)
    cond_sum = cond_part.astype(F32) + to_peer(cond_part).astype(F32)
    sum_c = near_sum([kept_ckv], near_c)
    scat_c = scatter(sum_c)

    small = jnp.concatenate(
        [gain_one, gain_two, gain_three, jnp.full((1, width), local_error, F32)],
        axis=0,
    )
    small = after(small, scat_w)
    for axis in ("tensor", "core", "near", "far"):
        size = lax.axis_size(axis)
        if size & (size - 1):
            small = lax.psum(small, axis)
            continue
        hop = 1
        while hop < size:
            small = small + lax.ppermute(small, axis, [(i, i ^ hop) for i in range(size)])
            hop *= 2
    mean_loss = small[3, 0] / (width * valid_count)
    place = (lax.axis_index("far") * 4 + near_at * 2 + pair) * slab
    grad_gains = lax.dynamic_slice(small, (0, place), (3, slab))

    ends = (
        UP_PIECES[1],
        UP_PIECES[1] + DOWN_PIECES[2],
        UP_PIECES[1] + DOWN_PIECES[2] + GATE_PIECES[1],
    )
    gate_parts = scat_gate + [last_ff[:, ends[1] : ends[2]]]
    up_parts = [mid, last_ff[:, : ends[0]]]
    down_parts = scat_down + [last_ff[:, ends[0] : ends[1]]]
    down_t, gate_s, up_s = (
        jnp.concatenate(finish(jnp.concatenate(parts, axis=1)), axis=1)
        for parts in (down_parts, gate_parts, up_parts)
    )
    sides = finish(jnp.concatenate(scat_qkv, axis=1))
    q_s, k_s, v_s = (
        columns_at(sides, range(i * PAIR, 3 * half_heads, 3 * PAIR), PAIR) for i in range(3)
    )
    out_t = jnp.concatenate(finish(last_ff[:, ends[2] :]), axis=1)
    sides = finish(scat_w)
    co_t, cq_s = (columns_at(sides, [i * half_heads], half_heads) for i in range(2))
    sides = finish(scat_c)
    ck_s, cv_s = (columns_at(sides, range(i * PAIR, heads_width, 2 * PAIR), PAIR) for i in range(2))
    return (
        block_out.astype(BF16)[None],
        mean_loss,
        grad_rows[None],
        cond_sum[None],
        q_s,
        k_s,
        v_s,
        out_t.T,
        cq_s,
        ck_s,
        cv_s,
        co_t.T,
        gate_s,
        up_s,
        down_t.T,
        grad_gains,
    )


def solution(mesh):
    dp_size, share = mesh.shape["dp"], mesh.shape["tensor"]
    fine = Mesh(
        mesh.devices.reshape(dp_size // 4, 2, 2, share), ("far", "near", "core", "tensor")
    )
    dp = ("far", "near", "core")
    tokens = P(dp, "tensor", None)
    per_latent = P(dp, None, None)
    by_row = P(dp, "tensor")
    by_column = P("tensor", dp)
    weights = (by_row,) * 3 + (by_column,) + (by_row,) * 3 + (by_column, by_row, by_row, by_column)
    return jax.shard_map(
        body,
        mesh=fine,
        in_specs=(tokens, per_latent, tokens, by_row, P(None, dp)) + weights,
        out_specs=(tokens, P(), tokens, per_latent) + weights + (P(None, dp),),
        check_vma=False,
    )
```

```python
import functools
import math

import jax
import jax.numpy as jnp
from jax import lax
from jax.experimental import pallas as pl
from jax.experimental.pallas import tpu as pltpu
from jax.sharding import Mesh, PartitionSpec as P

HEAD_DIM = 64
PAIR = 2 * HEAD_DIM
SCALE = HEAD_DIM**-0.5
EPSILON = 1e-05
F32 = jnp.float32
BF16 = jnp.bfloat16
KERNEL_VMEM = 60 << 20
PACK_VMEM = 60 << 20
GRAD_VMEM = 60 << 20
BACK_VMEM = 60 << 20
DOWN_PIECES = (896, 640)
GATE_PIECES = (1408, 128)
UP_PIECES = (768, 768)
PULL_ROWS = 256
NORM_ROWS = 128
FEED_COLUMNS = 512
SMALL_COST = pl.CostEstimate(flops=1 << 20, bytes_accessed=1 << 14, transcendentals=0)


def dot(left, right, left_dim, right_dim):
    return lax.dot_general(
        left, right, (((left_dim,), (right_dim,)), ((), ())), preferred_element_type=F32
    )


def norm_stats(values):
    row_mean = jnp.mean(values, axis=-1, keepdims=True)
    centred = values - row_mean
    row_var = jnp.mean(centred * centred, axis=-1, keepdims=True)
    inverse = lax.rsqrt(row_var + EPSILON)
    return (centred * inverse, inverse)


def rotary_tables(positions):
    half_dim = HEAD_DIM // 2
    freqs = jnp.exp(jnp.arange(half_dim, dtype=F32) * (-math.log(10000.0) / half_dim))
    angles = positions.astype(F32)[:, None] * freqs[None, :]
    cosine, sine = jnp.cos(angles), jnp.sin(angles)
    return (
        jnp.concatenate([cosine] * 4, axis=1),
        jnp.concatenate([-sine, sine] * 2, axis=1),
    )


def spin(values, cosines, sines):
    lane = lax.broadcasted_iota(jnp.int32, values.shape, 1)
    ahead = pltpu.roll(values, PAIR - HEAD_DIM // 2, 1)
    behind = pltpu.roll(values, HEAD_DIM // 2, 1)
    other = jnp.where(lane % HEAD_DIM < HEAD_DIM // 2, ahead, behind)
    return values * cosines + other * sines


def one_head(values, head):
    lane = lax.broadcasted_iota(jnp.int32, values.shape, 1)
    return jnp.where(lane // HEAD_DIM == head, values, jnp.zeros_like(values))


def turn(values):
    return values.astype(F32).T.astype(BF16)


def attend(keys, key_count, queries, values_t, out_ref, log_ref):
    mixed = []
    for head in range(2):
        scores = dot(keys, one_head(queries, head), 1, 1)
        if key_count < keys.shape[0]:
            row = lax.broadcasted_iota(jnp.int32, scores.shape, 0)
            scores = jnp.where(row < key_count, scores, -1e30)
        top = jnp.max(scores, axis=0, keepdims=True)
        shifted = jnp.exp(scores - top)
        total = jnp.sum(shifted, axis=0, keepdims=True)
        part = values_t[head * HEAD_DIM : (head + 1) * HEAD_DIM]
        mixed.append(dot(part, shifted.astype(BF16), 1, 0) / total)
        log_ref[0, head : head + 1, :] = top + jnp.log(total)
    out_ref[...] = jnp.concatenate(mixed, axis=0).T.astype(BF16)


def attend_back(queries, keys, key_count, values, grads, logs):
    keys_t = keys.astype(F32).T.astype(BF16)
    grad_k = jnp.zeros((keys.shape[0], PAIR), F32)
    grad_v = jnp.zeros((keys.shape[0], PAIR), F32)
    grad_q = []
    for head in range(2):
        query, grad = one_head(queries, head), one_head(grads, head)
        probs = jnp.exp(dot(keys, query, 1, 1) - logs[head : head + 1])
        if key_count < keys.shape[0]:
            row = lax.broadcasted_iota(jnp.int32, probs.shape, 0)
            probs = jnp.where(row < key_count, probs, 0.0)
        product = probs * dot(values, grad, 1, 1)
        weighted = jnp.sum(product, axis=0, keepdims=True)
        grad_s = (product - probs * weighted).astype(BF16)
        grad_v = grad_v + dot(probs.astype(BF16), grad, 1, 0)
        grad_k = grad_k + dot(grad_s, query, 1, 0)
        grad_q.append(dot(keys_t[head * HEAD_DIM : (head + 1) * HEAD_DIM], grad_s, 1, 0))
    return (jnp.concatenate(grad_q, axis=0).T * SCALE, grad_k, grad_v)


def self_forward_kernel(qkv, cos_in, sin_in, mixed, q_out, k_out, v_out, logs):
    cosines, sines = cos_in[...], sin_in[...]
    queries = spin(qkv[:, :PAIR], cosines, sines).astype(BF16).astype(F32)
    queries = (queries * SCALE).astype(BF16)
    keys = spin(qkv[:, PAIR : 2 * PAIR], cosines, sines).astype(BF16)
    values = qkv[:, 2 * PAIR :]
    q_out[...] = queries
    k_out[...] = keys
    v_out[...] = values.astype(BF16)
    attend(keys, keys.shape[0], queries, values.T.astype(BF16), mixed, logs)


def self_back_kernel(
    places, q_in, k_in, v_in, own_in, peer_in, out_w, qkv_w, logs, cos_in, sin_in,
    out, sent, own_out, peer_out, peer_sum,
):
    pair, pairs = pl.program_id(0), pl.num_programs(0)
    cosines, sines = cos_in[...], -sin_in[...]
    keys, weights = k_in[...], out_w[...]
    grads = jnp.concatenate([dot(own_in[...], weights, 1, 0), dot(peer_in[...], weights, 1, 0)], axis=0)
    grad_q, grad_k, grad_v = attend_back(
        q_in[...], keys, keys.shape[0], v_in[...], grads.astype(BF16), logs[0]
    )
    out[:, :PAIR] = spin(grad_q, cosines, sines).astype(BF16)
    out[:, PAIR : 2 * PAIR] = spin(grad_k, cosines, sines).astype(BF16)
    out[:, 2 * PAIR :] = grad_v.astype(BF16)

    @pl.when((2 * pair >= pairs) == (places[1] == 0))
    def _():
        sent[...] = out[...]

    rows = own_in.shape[0]
    own = dot(out[:rows, :], qkv_w[...], 1, 1)
    peer = dot(out[rows:, :], qkv_w[...], 1, 1)

    @pl.when(pair == 0)
    def _():
        own_out[...] = own
        peer_sum[...] = peer

    @pl.when(pair > 0)
    def _():
        own_out[...] += own
        peer_sum[...] += peer

    @pl.when(pair == pairs - 1)
    def _():
        peer_out[...] = peer_sum[...].astype(BF16)


def pick(own, peer):
    return jnp.where(2 * pl.program_id(0) < pl.num_programs(0), own[...], peer[...])


def cross_forward_kernel(key_count, q_own, q_peer, kv_own, kv_peer, mixed, logs):
    queries, keyvals = pick(q_own, q_peer), pick(kv_own, kv_peer)
    queries = (queries.astype(F32) * SCALE).astype(BF16)
    attend(keyvals[:, :PAIR], key_count, queries, turn(keyvals[:, PAIR:]), mixed, logs)


def cross_back_kernel(
    key_count, q_own, q_peer, g_own, g_peer, kv_own, kv_peer, logs, q_out, kv_out
):
    queries, keyvals = pick(q_own, q_peer), pick(kv_own, kv_peer)
    queries = (queries.astype(F32) * SCALE).astype(BF16)
    grad_q, grad_k, grad_v = attend_back(
        queries, keyvals[:, :PAIR], key_count, keyvals[:, PAIR:], pick(g_own, g_peer), logs[0]
    )
    q_out[...] = grad_q.astype(BF16)
    kv_out[:, :PAIR] = grad_k.astype(BF16)
    kv_out[:, PAIR:] = grad_v.astype(BF16)


def column_block(count):
    return pl.BlockSpec((count, PAIR), lambda i: (0, i))


def call_pairs(kernel, width, in_specs, out_specs, out_shape, args):
    return pl.pallas_call(
        kernel,
        grid=(width // PAIR,),
        in_specs=in_specs,
        out_specs=out_specs,
        out_shape=out_shape,
        compiler_params=pltpu.CompilerParams(vmem_limit_bytes=KERNEL_VMEM),
        cost_estimate=SMALL_COST,
    )(*args)


def self_forward(qkv, cosines, sines):
    rows, width = qkv.shape[0], qkv.shape[1] // 3
    pairs = width // PAIR
    table = pl.BlockSpec((rows, PAIR), lambda i: (0, 0))
    act = jax.ShapeDtypeStruct((rows, width), BF16)
    return call_pairs(
        self_forward_kernel,
        width,
        [pl.BlockSpec((rows, 3 * PAIR), lambda i: (0, i)), table, table],
        [column_block(rows)] * 4 + [pl.BlockSpec((1, 2, rows), lambda i: (i, 0, 0))],
        [act] * 4 + [jax.ShapeDtypeStruct((pairs, 2, rows), F32)],
        (qkv, cosines, sines),
    )


def self_back(places, queries, keys, values, own, peer, weights, logs, cosines, sines):
    rows, width = queries.shape
    count, depth = own.shape
    pairs = width // PAIR
    block = pl.BlockSpec((rows, PAIR), lambda i, places: (0, i))
    table = pl.BlockSpec((rows, PAIR), lambda i, places: (0, 0))
    token = pl.BlockSpec((count, depth), lambda i, places: (0, 0))
    half = pairs // 2
    return pl.pallas_call(
        self_back_kernel,
        grid_spec=pltpu.PrefetchScalarGridSpec(
            num_scalar_prefetch=1,
            grid=(pairs,),
            in_specs=[
                block,
                block,
                block,
                token,
                token,
                pl.BlockSpec((depth, PAIR), lambda i, places: (0, 3 * pairs + i)),
                pl.BlockSpec((depth, 3 * PAIR), lambda i, places: (0, i)),
                pl.BlockSpec((1, 2, rows), lambda i, places: (i, 0, 0)),
                table,
                table,
            ],
            out_specs=[
                pl.BlockSpec((rows, 3 * PAIR), lambda i, places: (0, i)),
                pl.BlockSpec(
                    (rows, 3 * PAIR),
                    lambda i, places: (0, jnp.clip(i - half * (1 - places[1]), 0, half - 1)),
                ),
                token,
                token,
            ],
            scratch_shapes=[pltpu.VMEM((count, depth), F32)],
        ),
        out_shape=[
            jax.ShapeDtypeStruct((rows, 3 * width), BF16),
            jax.ShapeDtypeStruct((rows, 3 * width // 2), BF16),
            jax.ShapeDtypeStruct((count, depth), F32),
            jax.ShapeDtypeStruct((count, depth), BF16),
        ],
        compiler_params=pltpu.CompilerParams(vmem_limit_bytes=BACK_VMEM),
        cost_estimate=SMALL_COST,
    )(places, queries, keys, values, own, peer, weights, weights, logs, cosines, sines)


def cross_call(kernel, key_count, arrays, logs, out_specs, out_shape):
    pairs = arrays[0][0].shape[1] // PAIR
    specs, args = [], []
    for own, peer in arrays:
        block = (own.shape[0], own.shape[1] // pairs)
        specs.append(pl.BlockSpec(block, lambda i: (0, jnp.minimum(i, pairs - 1))))
        specs.append(pl.BlockSpec(block, lambda i: (0, jnp.maximum(i - pairs, 0))))
        args += [own, peer]
    if logs is not None:
        specs.append(pl.BlockSpec((1,) + logs.shape[1:], lambda i: (i, 0, 0)))
        args.append(logs)
    return pl.pallas_call(
        functools.partial(kernel, key_count),
        grid=(2 * pairs,),
        in_specs=specs,
        out_specs=out_specs,
        out_shape=out_shape,
        compiler_params=pltpu.CompilerParams(vmem_limit_bytes=KERNEL_VMEM),
        cost_estimate=SMALL_COST,
    )(*args)


def cross_forward(queries, keyvals, key_count):
    rows, width = queries[0].shape
    return cross_call(
        cross_forward_kernel,
        key_count,
        (queries, keyvals),
        None,
        [column_block(rows), pl.BlockSpec((1, 2, rows), lambda i: (i, 0, 0))],
        [
            jax.ShapeDtypeStruct((rows, 2 * width), BF16),
            jax.ShapeDtypeStruct((2 * width // PAIR, 2, rows), F32),
        ],
    )


def cross_back(queries, grads, keyvals, logs, key_count):
    rows, width = queries[0].shape
    keys = keyvals[0].shape[0]
    return cross_call(
        cross_back_kernel,
        key_count,
        (queries, grads, keyvals),
        logs,
        [column_block(rows), pl.BlockSpec((keys, 2 * PAIR), lambda i: (0, i))],
        [
            jax.ShapeDtypeStruct((rows, 2 * width), BF16),
            jax.ShapeDtypeStruct((keys, 4 * width), BF16),
        ],
    )


def norm_back_kernel(away, *refs):
    pulled, peer = refs[0], refs[1] if away else None
    hidden, gain_row, skip, total_out, low_out, gain_out = refs[1 + away :]
    grad = pulled[...] + peer[...].astype(F32) if away else pulled[...]
    normed, inverse = norm_stats(hidden[...].astype(F32))
    scaled = grad * gain_row[...]
    mean_scaled = jnp.mean(scaled, axis=-1, keepdims=True)
    mean_product = jnp.mean(scaled * normed, axis=-1, keepdims=True)
    total = skip[...] + inverse * (scaled - mean_scaled - normed * mean_product)
    total_out[...] = total
    low_out[...] = total.astype(BF16)
    received = jnp.sum(grad * normed, axis=0, keepdims=True)

    @pl.when(pl.program_id(0) == 0)
    def _():
        gain_out[...] = received

    @pl.when(pl.program_id(0) > 0)
    def _():
        gain_out[...] += received


def norm_back(pulled, away, hidden, gain_row, skip):
    rows, depth = pulled.shape
    block = pl.BlockSpec((NORM_ROWS, depth), lambda i: (i, 0))
    row = pl.BlockSpec((1, depth), lambda i: (0, 0))
    arrays = (pulled,) if away is None else (pulled, away)
    return pl.pallas_call(
        functools.partial(norm_back_kernel, len(arrays) - 1),
        grid=(rows // NORM_ROWS,),
        in_specs=[block] * len(arrays) + [block, row, block],
        out_specs=[block, block, row],
        out_shape=[
            jax.ShapeDtypeStruct((rows, depth), F32),
            jax.ShapeDtypeStruct((rows, depth), BF16),
            jax.ShapeDtypeStruct((1, depth), F32),
        ],
        compiler_params=pltpu.CompilerParams(vmem_limit_bytes=KERNEL_VMEM),
        cost_estimate=SMALL_COST,
    )(*arrays, hidden, gain_row, skip)


def feed_back_kernel(places, g_in, weights, gate_in, up_in, gate_out, up_out, sent):
    grad_hidden = dot(g_in[...], weights[...], 1, 0)
    gate_pre, up_pre = gate_in[...].astype(F32), up_in[...].astype(F32)
    sigmoid = 1.0 / (1.0 + jnp.exp(-gate_pre))
    grad_gate = grad_hidden * up_pre * sigmoid * (1.0 + gate_pre * (1.0 - sigmoid))
    gate_out[...] = grad_gate.astype(BF16)
    up_out[...] = (grad_hidden * (gate_pre * sigmoid)).astype(BF16)

    @pl.when((2 * pl.program_id(0) >= pl.num_programs(0)) == (places[1] == 0))
    def _():
        sent[0] = gate_out[...]
        sent[1] = up_out[...]


def feed_back(places, grads, weights, gate_pre, up_pre, part):
    rows, depth = grads.shape
    width = gate_pre.shape[1]
    steps = width // FEED_COLUMNS
    half = steps // 2
    column = pl.BlockSpec((rows, FEED_COLUMNS), lambda i, places: (0, i))
    row_part = pl.BlockSpec((rows, FEED_COLUMNS), lambda i, places: (part, i))
    act = jax.ShapeDtypeStruct((rows, width), BF16)
    return pl.pallas_call(
        feed_back_kernel,
        grid_spec=pltpu.PrefetchScalarGridSpec(
            num_scalar_prefetch=1,
            grid=(steps,),
            in_specs=[
                pl.BlockSpec((rows, depth), lambda i, places: (0, 0)),
                pl.BlockSpec((depth, FEED_COLUMNS), lambda i, places: (0, 2 * steps + i)),
                row_part,
                row_part,
            ],
            out_specs=[
                column,
                column,
                pl.BlockSpec(
                    (2, rows, FEED_COLUMNS),
                    lambda i, places: (0, 0, jnp.clip(i - half * (1 - places[1]), 0, half - 1)),
                ),
            ],
        ),
        out_shape=[act, act, jax.ShapeDtypeStruct((2, rows, width // 2), BF16)],
        compiler_params=pltpu.CompilerParams(vmem_limit_bytes=BACK_VMEM),
        cost_estimate=SMALL_COST,
    )(places, grads, weights, gate_pre, up_pre)


def weight_grad_kernel(count, pieces, group, places, *refs):
    outs = refs[2 * count :]
    total = dot(refs[0][...], refs[1][...], 0, 0)
    for index in range(1, count):
        total = total + dot(refs[2 * index][...], refs[2 * index + 1][...], 0, 0)

    def side(index):
        starts = range(index * group, total.shape[0], 2 * group)
        parts = [total[at : at + group] for at in starts]
        return (jnp.concatenate(parts, axis=0) if len(parts) > 1 else parts[0]).astype(BF16)

    first, second = side(0), side(1)

    def write(values, targets):
        at = 0
        for piece, target in zip(pieces, targets, strict=True):
            target[...] = values[:, at : at + piece]
            at += piece

    @pl.when(places[0] == 0)
    def _():
        write(first, outs[: len(pieces)])
        write(second, outs[len(pieces) :])

    @pl.when(places[0] != 0)
    def _():
        write(second, outs[: len(pieces)])
        write(first, outs[len(pieces) :])


def weight_grad(places, far, pieces, parts):
    columns = sum(pieces)
    sides = [[side if isinstance(side, tuple) else (side, None) for side in part[:2]] for part in parts]
    depth = sides[0][0][0].shape[1]
    block = math.lcm(depth // far, 128)
    specs, args = [], []
    for ((left, left_half), (right, right_half)), (_, _, at) in zip(sides, parts, strict=True):
        tokens = left.shape[0] if left_half is None else left.shape[0] // 2
        first, second = left_half or 0, right_half or 0
        specs.append(pl.BlockSpec((tokens, block), lambda i, places, first=first: (first, i)))
        if at is None:
            spec = pl.BlockSpec(
                (tokens, columns), lambda i, places, second=second: (second, places[1])
            )
        elif right.ndim == 3:
            spec = pl.BlockSpec(
                (pl.Squeezed(), tokens, columns), lambda i, places, at=at: (at, 0, 0)
            )
        else:
            spec = pl.BlockSpec(
                (tokens, columns), lambda i, places, second=second, at=at: (second, at)
            )
        specs.append(spec)
        args += [left, right]
    outs = pl.pallas_call(
        functools.partial(weight_grad_kernel, len(parts), pieces, depth // far // 2),
        grid_spec=pltpu.PrefetchScalarGridSpec(
            num_scalar_prefetch=1,
            grid=(depth // block,),
            in_specs=specs,
            out_specs=[
                pl.BlockSpec((block // 2, piece), lambda i, places: (i, 0)) for piece in 2 * pieces
            ],
        ),
        out_shape=[jax.ShapeDtypeStruct((depth // 2, piece), BF16) for piece in 2 * pieces],
        compiler_params=pltpu.CompilerParams(vmem_limit_bytes=GRAD_VMEM),
        cost_estimate=SMALL_COST,
    )(places, *args)
    return outs[: len(pieces)], outs[len(pieces) :]


def whole_call(kernel, out_shape, *args):
    return pl.pallas_call(
        kernel,
        out_shape=out_shape,
        compiler_params=pltpu.CompilerParams(vmem_limit_bytes=BACK_VMEM),
        cost_estimate=SMALL_COST,
    )(*args)


def join_kernel(axis, *refs):
    refs[-1][...] = jnp.concatenate([ref[...] for ref in refs[:-1]], axis=axis)


def join(axis, *parts):
    shape = list(parts[0].shape)
    shape[axis] = sum(part.shape[axis] for part in parts)
    return whole_call(
        functools.partial(join_kernel, axis), jax.ShapeDtypeStruct(shape, parts[0].dtype), *parts
    )


def near_sum_kernel(*refs):
    got, out = refs[-2:]
    at = 0
    for ref in refs[:-2]:
        end = at + ref.shape[1]
        out[:, at:end] = (ref[...].astype(F32) + got[:, at:end].astype(F32)).astype(BF16)
        at = end


def near_sum(kept, got):
    rows, columns = got.shape
    block = rows // 4 if rows % 64 == 0 else rows

    def spec(width):
        return pl.BlockSpec((block, width), lambda i: (i, 0))

    return pl.pallas_call(
        near_sum_kernel,
        grid=(rows // block,),
        in_specs=[spec(part.shape[1]) for part in kept] + [spec(columns)],
        out_specs=spec(columns),
        out_shape=jax.ShapeDtypeStruct(got.shape, BF16),
        compiler_params=pltpu.CompilerParams(vmem_limit_bytes=KERNEL_VMEM),
        cost_estimate=SMALL_COST,
    )(*kept, got)


def other_half_kernel(places, *refs):
    out, at = refs[-1], 0
    for ref in refs[:-1]:
        out[at : at + ref.shape[0], :] = ref[...]
        at += ref.shape[0]


def other_half(places, width, *parts):
    half = width // 2
    rows = sum(part.shape[0] for part in parts)
    return pl.pallas_call(
        other_half_kernel,
        grid_spec=pltpu.PrefetchScalarGridSpec(
            num_scalar_prefetch=1,
            grid=(1,),
            in_specs=[
                pl.BlockSpec((part.shape[0], half), lambda i, places: (0, 1 - places[1]))
                for part in parts
            ],
            out_specs=pl.BlockSpec((rows, half), lambda i, places: (0, 0)),
        ),
        out_shape=jax.ShapeDtypeStruct((rows, half), BF16),
        compiler_params=pltpu.CompilerParams(vmem_limit_bytes=KERNEL_VMEM),
        cost_estimate=SMALL_COST,
    )(places, *parts)


def mixed_back_kernel(g_in, own_w, peer_w, own_out, peer_out):
    own_out[...] = dot(g_in[...], own_w[...], 1, 0).astype(BF16)
    peer_out[...] = dot(g_in[...], peer_w[...], 1, 0).astype(BF16)


def mixed_back(grads, weights, at, peer_weights):
    rows, depth = grads.shape
    width = peer_weights.shape[1]
    half = width // 2
    act = jax.ShapeDtypeStruct((rows, width), BF16)
    return pl.pallas_call(
        mixed_back_kernel,
        grid=(2,),
        in_specs=[
            pl.BlockSpec((rows, depth), lambda i: (0, 0)),
            pl.BlockSpec((depth, half), lambda i: (0, 2 * at + i)),
            pl.BlockSpec((depth, half), lambda i: (0, i)),
        ],
        out_specs=[pl.BlockSpec((rows, half), lambda i: (0, i))] * 2,
        out_shape=[act, act],
        compiler_params=pltpu.CompilerParams(vmem_limit_bytes=KERNEL_VMEM),
        cost_estimate=SMALL_COST,
    )(grads, weights, peer_weights)


def pull_query_kernel(g_in, own_w, peer_w, out):
    width = own_w.shape[1]
    out[...] = dot(g_in[:, :width], own_w[...], 1, 1) + dot(g_in[:, width:], peer_w[...], 1, 1)


def pull_query(grads, weights, at, peer_weights):
    rows = grads.shape[0]
    depth, width = peer_weights.shape
    return pl.pallas_call(
        pull_query_kernel,
        grid=(depth // PULL_ROWS,),
        in_specs=[
            pl.BlockSpec(grads.shape, lambda i: (0, 0)),
            pl.BlockSpec((PULL_ROWS, width), lambda i: (i, at)),
            pl.BlockSpec((PULL_ROWS, width), lambda i: (i, 0)),
        ],
        out_specs=pl.BlockSpec((rows, PULL_ROWS), lambda i: (0, i)),
        out_shape=jax.ShapeDtypeStruct((rows, depth), F32),
        compiler_params=pltpu.CompilerParams(vmem_limit_bytes=KERNEL_VMEM),
        cost_estimate=SMALL_COST,
    )(grads, weights, peer_weights)


def pull_kernel(gate_in, up_in, weights, out):
    width = gate_in.shape[1]
    total = dot(gate_in[...], weights[:, :width], 1, 1) + dot(up_in[...], weights[:, width:], 1, 1)
    out[...] = total.astype(out.dtype)


def pull(grad_gate, grad_upper, weights, kind):
    rows, width = grad_gate.shape
    depth = weights.shape[0]
    whole = pl.BlockSpec((rows, width), lambda i: (0, 0))
    return pl.pallas_call(
        pull_kernel,
        grid=(depth // PULL_ROWS,),
        in_specs=[whole, whole, pl.BlockSpec((PULL_ROWS, 2 * width), lambda i: (i, 0))],
        out_specs=pl.BlockSpec((rows, PULL_ROWS), lambda i: (0, i)),
        out_shape=jax.ShapeDtypeStruct((rows, depth), kind),
        compiler_params=pltpu.CompilerParams(vmem_limit_bytes=GRAD_VMEM),
        cost_estimate=SMALL_COST,
    )(grad_gate, grad_upper, weights)


def meet(*values):
    return lax.optimization_barrier(values)


def pack_attention_kernel(q_in, k_in, v_in, o_in, cq_in, ck_in, cv_in, co_in, gains, mask, out):
    width = q_in.shape[1]
    for pair in range(width // PAIR):
        for index, ref in enumerate((q_in, k_in, v_in)):
            at = (3 * pair + index) * PAIR
            out[:, at : at + PAIR] = ref[:, pair * PAIR : (pair + 1) * PAIR]
    out[:, 3 * width : 4 * width] = turn(o_in[...])
    for pair in range(width // PAIR):
        for index, ref in enumerate((ck_in, cv_in)):
            at = 4 * width + (2 * pair + index) * PAIR
            out[:, at : at + PAIR] = ref[:, pair * PAIR : (pair + 1) * PAIR]
    out[:, 6 * width : 7 * width] = cq_in[...]
    out[:, 7 * width : 8 * width] = turn(co_in[...])
    count = jnp.sum(mask[...].astype(F32), axis=1, keepdims=True)
    upper = jnp.floor(count * (1.0 / 128.0))
    side = gains[...].astype(F32).T
    row = lax.broadcasted_iota(jnp.int32, side.shape, 0)
    lane = lax.broadcasted_iota(jnp.int32, side.shape, 1)
    side = jnp.where((lane == 3) & (row == 0), upper, side)
    side = jnp.where((lane == 3) & (row == 1), count - 128.0 * upper, side)
    out[:, 8 * width :] = side.astype(BF16)


def pack_feed_kernel(gate_in, up_in, down_in, out):
    width = gate_in.shape[1]
    out[:, :width] = gate_in[...]
    out[:, width : 2 * width] = up_in[...]
    out[:, 2 * width :] = turn(down_in[...])


def pack(kernel, columns, *parts):
    return pl.pallas_call(
        kernel,
        out_shape=jax.ShapeDtypeStruct((parts[0].shape[0], columns), BF16),
        compiler_params=pltpu.CompilerParams(vmem_limit_bytes=PACK_VMEM),
    )(*parts)


def after(value, *earlier):
    return lax.optimization_barrier((value, *earlier))[0]


def body(
    x_input,
    cond_tokens,
    teacher,
    valid_mask,
    norm_gains,
    w_query,
    w_key,
    w_value,
    w_out,
    c_query,
    c_key,
    c_value,
    c_out,
    w_gate,
    w_up,
    w_down,
):
    far = lax.axis_size("far")
    near_at, pair, share = (lax.axis_index(name) for name in ("near", "core", "tensor"))
    dp_axes = ("far", "near", "core")
    dp_size = 4 * far
    swap = [(0, 1), (1, 0)]

    def to_peer(values):
        return lax.ppermute(values, "tensor", swap)

    def to_core(values):
        return lax.ppermute(values, "core", swap)

    def to_near(values):
        return lax.ppermute(values, "near", swap)

    def gather(values):
        return lax.all_gather(values, dp_axes, axis=0, tiled=True)

    x_bf = x_input[0]
    rows, width = x_bf.shape
    slab = w_query.shape[0]
    heads_width = w_query.shape[1]
    ff_width = w_gate.shape[1]
    length = 2 * rows
    ctx_len = cond_tokens.shape[1]
    cond_rows = jnp.pad(cond_tokens[0], ((0, -ctx_len % 16), (0, 0)))
    mask_float = valid_mask[0].astype(F32)
    x_peer_bf = to_peer(x_bf)

    gath_a = gather(
        pack(
            pack_attention_kernel,
            8 * heads_width + PAIR,
            w_query,
            w_key,
            w_value,
            w_out,
            c_query,
            c_key,
            c_value,
            c_out,
            jnp.pad(norm_gains, ((0, PAIR - 3), (0, 0))),
            valid_mask,
        )
    )
    gath_b = gather(pack(pack_feed_kernel, 3 * ff_width, w_gate, w_up, w_down))

    weight_qkv = gath_a[:, : 3 * heads_width]
    weight_o = gath_a[:, 3 * heads_width : 4 * heads_width]
    cross_kv = gath_a[:, 4 * heads_width : 6 * heads_width]
    side = gath_a[:, 8 * heads_width :].T[:8].astype(F32)
    gains = side[:3]
    counts = side[3].reshape(dp_size, slab)
    part_count = jnp.sum(counts[:, 0]) * 128.0 + jnp.sum(counts[:, 1])
    part_count = jnp.full((8, 128), part_count, F32)
    valid_count = (part_count + to_peer(part_count))[0, 0]
    half_ff, half_heads = ff_width // 2, heads_width // 2
    places = jnp.stack([near_at, pair]).astype(jnp.int32)

    def fetch_peer(first):
        return to_peer(
            lax.dynamic_slice(
                gath_a, (pair * (width // 2), first * heads_width), (width // 2, heads_width)
            )
        )

    def join_cores(got):
        other = to_core(got)
        return jnp.concatenate(
            [jnp.where(pair == 0, got, other), jnp.where(pair == 0, other, got)], axis=0
        )

    cross_q_own = gath_a[:, 6 * heads_width : 7 * heads_width]
    cross_o_own = gath_a[:, 7 * heads_width : 8 * heads_width]
    cross_q_peer = fetch_peer(6)

    local_rows = x_bf.astype(F32)
    normed_one, _ = norm_stats(local_rows)
    peer_one, _ = norm_stats(x_peer_bf.astype(F32))
    input_one = jnp.concatenate(
        [(normed_one * gains[0]).astype(BF16), (peer_one * gains[0]).astype(BF16)], axis=0
    )
    order = lax.iota(jnp.int32, length)
    positions = jnp.where(order < rows, order + share * rows, order - share * rows)
    cosines, sines = rotary_tables(positions)
    def project(values, weight, weight_dim, *meanwhile):
        away = to_peer(dot(values[rows:], weight, 1, weight_dim).astype(BF16))
        mine = dot(values[:rows], weight, 1, weight_dim)
        return mine + after(away, mine, *meanwhile).astype(F32)

    qkv = dot(input_one, weight_qkv, 1, 0)
    mixed_self, query_self, key_self, value_self, logs_self = self_forward(qkv, cosines, sines)
    cross_q_peer = join_cores(after(cross_q_peer, mixed_self))
    cross_o_peer = fetch_peer(7)
    keyvals_own = dot(cond_rows, cross_kv, 1, 0).astype(BF16)
    keyvals_peer = to_peer(keyvals_own)
    core_one = to_core(input_one)
    hidden_one = local_rows + project(mixed_self, weight_o, 1, core_one, cross_q_peer)

    normed_two, _ = norm_stats(hidden_one)
    own_two = (normed_two * gains[1]).astype(BF16)
    query_cross = tuple(
        dot(own_two, weight, 1, 0).astype(BF16) for weight in (cross_q_own, cross_q_peer)
    )
    keyvals = (keyvals_own, after(keyvals_peer, own_two))
    mixed_cross, logs_cross = cross_forward(query_cross, keyvals, ctx_len)
    cross_o_peer = join_cores(after(cross_o_peer, mixed_cross))
    hidden_two = (
        hidden_one
        + dot(mixed_cross[:, :heads_width], cross_o_own, 1, 1)
        + dot(mixed_cross[:, heads_width:], cross_o_peer, 1, 1)
    )

    normed_three, _ = norm_stats(hidden_two)
    own_three = (normed_three * gains[2]).astype(BF16)
    peer_three = to_peer(own_three)
    core_mixed_self, core_cond = to_core(other_half(places, heads_width, mixed_self)), to_core(cond_rows)
    peer_three = after(peer_three, core_mixed_self, core_cond)
    input_three = jnp.concatenate([own_three, peer_three], axis=0)
    weight_gate = gath_b[:, :ff_width]
    weight_up = gath_b[:, ff_width : 2 * ff_width]
    weight_down = gath_b[:, 2 * ff_width :]
    gate_pre = dot(input_three, weight_gate, 1, 0).astype(BF16)
    up_sum = dot(input_three, weight_up, 1, 0)
    gate_sum = gate_pre.astype(F32)
    hidden_ff = (gate_sum * jax.nn.sigmoid(gate_sum) * up_sum).astype(BF16)
    core_own_two = to_core(own_two)
    up_pre = up_sum.astype(BF16)
    core_three = to_core(input_three)
    core_hidden = to_core(other_half(places, ff_width, hidden_ff))
    block_out = hidden_two + project(hidden_ff, weight_down, 1, core_three, core_hidden, core_own_two)

    error_diff = block_out - teacher[0].astype(F32)
    local_error = jnp.sum(mask_float[:, None] * error_diff * error_diff)
    token_total = float(dp_size * lax.axis_size("tensor") * rows)
    grad_out = 2.0 * token_total / valid_count * mask_float[:, None] * error_diff

    def grad_of(pieces, *parts):
        return weight_grad(places, far, pieces, parts)

    scattered = []

    def add_pair(kept, got):
        return near_sum(kept, after(got, *scattered[:-1]))

    def scatter_on(summed):
        scattered.append(scatter(summed))
        return scattered[-1]

    def scatter(summed):
        return lax.psum_scatter(summed, "far", scatter_dimension=0, tiled=True)

    def finish(scattered):
        columns = scattered.shape[1]
        kept = lax.dynamic_slice(scattered, (pair * slab, 0), (slab, columns))
        got = to_core(lax.dynamic_slice(scattered, ((1 - pair) * slab, 0), (slab, columns)))
        first = jnp.where(pair == 0, kept, got).astype(F32)
        second = jnp.where(pair == 0, got, kept).astype(F32)
        return (first, second)

    def columns_at(sides, places, size):
        return jnp.concatenate(
            [side[:, at : at + size] for side in sides for at in places], axis=1
        )

    own_e3 = grad_out.astype(BF16)
    peer_e3 = to_peer(own_e3)
    core_own_e3 = to_core(own_e3)

    def row(index):
        return gains[index : index + 1]

    dgate_own, dup_own, halves_own = feed_back(places, own_e3, gath_b, gate_pre, up_pre, 0)
    dgate_own, dup_own, halves_own, pulled_own, peer_e3, core_own_e3 = meet(
        dgate_own, dup_own, halves_own, pull(dgate_own, dup_own, gath_b, F32), peer_e3, core_own_e3
    )
    dgate_peer, dup_peer, halves_peer, core_peer_e3, core_own_halves = meet(
        *feed_back(places, peer_e3, gath_b, gate_pre, up_pre, 1),
        to_core(peer_e3),
        to_core(halves_own),
    )
    kept_down, sent_down = grad_of(
        DOWN_PIECES,
        (own_e3, (hidden_ff, 0), None),
        (peer_e3, (hidden_ff, 1), None),
        (core_own_e3, (core_hidden, 0), 0),
        (core_peer_e3, (core_hidden, 1), 0),
    )
    *sent_down, dgate_peer, dup_peer, halves_peer, peer_mixed = meet(
        *sent_down,
        dgate_peer,
        dup_peer,
        halves_peer,
        to_peer(after(mixed_cross, dgate_peer)[:, heads_width:]),
    )
    near_a = to_near(sent_down[0])
    half_mixed = other_half(places, heads_width, mixed_cross, peer_mixed)
    peer_two = to_peer(after(own_two, half_mixed))
    pulled_peer, core_peer_halves, core_mixed = meet(
        pull(dgate_peer, dup_peer, gath_b, BF16), to_core(halves_peer), to_core(half_mixed)
    )
    away = to_peer(pulled_peer)

    def feed_grad(pieces, own, peer, at):
        kept, sent = grad_of(
            pieces,
            (own_three, own, None),
            (peer_three, peer, None),
            ((core_three, 0), core_own_halves, at),
            ((core_three, 1), core_peer_halves, at),
        )
        return kept + sent

    *gate_w, near_a = meet(
        *feed_grad(GATE_PIECES, dgate_own, after(dgate_peer, pulled_peer), 0), near_a
    )
    near_b = to_near(after(sent_down[1], near_a))
    *up_w, sum_a, near_b, peer_two, away = meet(
        *feed_grad(UP_PIECES, dup_own, after(dup_peer, gate_w[0]), 1),
        add_pair(kept_down[:1], near_a),
        near_b,
        peer_two,
        away,
    )
    scat_down = [scatter_on(sum_a)]
    near_c = to_near(after(gate_w[2], near_b))
    grad_two, own_e2, gain_three = norm_back(pulled_own, away, hidden_two, row(2), grad_out)

    grad_mixed = mixed_back(own_e2, gath_a, 7, cross_o_peer)
    grad_qc, grad_kv = cross_back(query_cross, grad_mixed, keyvals, logs_cross, ctx_len)
    pulled_two = pull_query(grad_qc, gath_a, 6, cross_q_peer)
    grad_one, own_e1, gain_two = norm_back(pulled_two, None, hidden_one, row(1), grad_two)
    sum_b = add_pair(kept_down[1:2], near_b)
    scat_down.append(scatter_on(sum_b))
    sent_d = up_w[2]
    grad_one, own_e1, gain_two, sum_b, own_e2, peer_e2, core_own_e2, near_c = meet(
        grad_one, own_e1, gain_two, sum_b, own_e2, to_peer(own_e2), to_core(own_e2), near_c
    )

    def head_grad(*parts):
        kept, sent = grad_of((half_heads,), *parts)
        return kept[0], sent[0]

    near_d = to_near(sent_d)
    peer_e1 = to_peer(own_e1)
    sum_c = add_pair(gate_w[:1], near_c)
    scat_gate = [scatter_on(sum_c)]
    core_peer_e2 = to_core(peer_e2)
    kept_co, sent_co = head_grad(
        (own_e2, mixed_cross, None),
        (peer_e2, peer_mixed, None),
        (core_own_e2, (core_mixed, 0), 0),
        (core_peer_e2, (core_mixed, 1), 0),
    )
    sum_c, peer_e1, near_d, core_own_e1, kept_co, sent_co = meet(
        sum_c, peer_e1, near_d, to_core(own_e1), kept_co, sent_co
    )
    grad_qc, grad_kv, _ = meet(grad_qc, grad_kv, peer_e1)
    sum_d = add_pair([up_w[0]], near_d)
    mid = scatter_on(sum_d)
    sum_d, core_peer_e1 = meet(sum_d, to_core(peer_e1))
    kept_wo, sent_wo = head_grad(
        (own_e1, (mixed_self, 0), None),
        (peer_e1, (mixed_self, 1), None),
        (core_own_e1, (core_mixed_self, 0), 0),
        (core_peer_e1, (core_mixed_self, 1), 0),
    )
    kept_wo, sent_e = meet(kept_wo, join(1, up_w[3], gate_w[3], sent_wo))
    near_e = to_near(sent_e)
    grad_qkv, halves_qkv, pulled_own, pulled_peer, peer_qc, peer_kv, near_e = meet(
        *self_back(
            places,
            query_self,
            key_self,
            value_self,
            own_e1,
            after(peer_e1, sent_e),
            gath_a,
            logs_self,
            cosines,
            sines,
        ),
        to_peer(grad_qc[:, heads_width:]),
        to_peer(grad_kv[:, 2 * heads_width :]),
        near_e,
    )
    near_co = to_near(after(sent_co, near_e))
    away = to_peer(pulled_peer)
    sum_e = add_pair([up_w[1], gate_w[1], kept_wo], near_e)
    last_ff = scatter_on(sum_e)
    sum_e, core_qkv = meet(sum_e, to_core(halves_qkv))
    kept_qkv, sent_qkv = grad_of(
        (3 * half_heads,), (input_one, after(grad_qkv, sum_e), None), (core_one, core_qkv, 0)
    )
    kept_qkv, sent_f, near_co = meet(kept_qkv[0], sent_qkv[0], near_co)
    near_f = to_near(sent_f)
    sum_co = add_pair([kept_co], near_co)
    scat_co = scatter_on(sum_co)
    sum_kv = near_sum([grad_kv[:, : 2 * heads_width]], after(peer_kv, sent_f))
    sum_kv, half_kv, half_qc = meet(
        sum_kv,
        other_half(places, 2 * heads_width, sum_kv),
        other_half(places, heads_width, grad_qc, after(peer_qc, sent_f)),
    )
    sum_co, core_kv, core_qc, core_peer_two = meet(
        sum_co, to_core(half_kv), to_core(half_qc), to_core(after(peer_two, half_qc))
    )
    kept_cq, sent_cq = head_grad(
        (own_two, after(grad_qc, sum_co), None),
        (peer_two, peer_qc, None),
        (core_own_two, (core_qc, 0), 0),
        (core_peer_two, (core_qc, 1), 0),
    )
    kept_ckv, sent_ckv = grad_of(
        (heads_width,), (cond_rows, after(sum_kv, sent_cq), None), (core_cond, core_kv, 0)
    )
    kept_cq, kept_ckv, sent_w, near_f = meet(
        kept_cq, kept_ckv[0], join(1, sent_cq, sent_ckv[0]), near_f
    )
    near_w = to_near(sent_w)
    sum_f = add_pair([kept_qkv], near_f)
    scat_qkv = scatter_on(sum_f)
    cond_part = dot(after(sum_kv, sum_f), cross_kv, 1, 1)[:ctx_len].astype(BF16)
    grad_rows, _, gain_one = norm_back(
        pulled_own, after(away, sum_f), x_bf, row(0), grad_one
    )
    near_w, cond_part, last_ff, scat_co, grad_rows, gain_one = meet(
        near_w, cond_part, last_ff, scat_co, grad_rows, gain_one
    )
    cond_sum = cond_part.astype(F32) + to_peer(cond_part).astype(F32)
    sum_w = near_sum([kept_cq, kept_ckv], near_w)
    scat_w = scatter(sum_w)

    small = jnp.concatenate(
        [gain_one, gain_two, gain_three, jnp.full((1, width), local_error, F32)], axis=0
    )
    small = after(small, sum_w)
    for axis in ("tensor", "core", "near", "far"):
        size = lax.axis_size(axis)
        if size & (size - 1):
            small = lax.psum(small, axis)
            continue
        hop = 1
        while hop < size:
            small = small + lax.ppermute(small, axis, [(i, i ^ hop) for i in range(size)])
            hop *= 2
    mean_loss = small[3, 0] / (width * valid_count)
    place = (lax.axis_index("far") * 4 + near_at * 2 + pair) * slab
    grad_gains = lax.dynamic_slice(small, (0, place), (3, slab))

    ends = (UP_PIECES[1], UP_PIECES[1] + GATE_PIECES[1])
    gate_parts = scat_gate + [last_ff[:, ends[0] : ends[1]]]
    up_parts = [mid, last_ff[:, : ends[0]]]
    down_parts = scat_down
    down_t, gate_s, up_s = (
        jnp.concatenate(finish(jnp.concatenate(parts, axis=1)), axis=1)
        for parts in (down_parts, gate_parts, up_parts)
    )
    sides = finish(scat_qkv)
    q_s, k_s, v_s = (
        columns_at(sides, range(i * PAIR, 3 * half_heads, 3 * PAIR), PAIR) for i in range(3)
    )
    out_t = jnp.concatenate(finish(last_ff[:, ends[1] :]), axis=1)
    co_t = jnp.concatenate(finish(scat_co), axis=1)
    sides = finish(scat_w)
    cq_s = columns_at(sides, [0], half_heads)
    ck_s, cv_s = (
        columns_at(sides, range(half_heads + i * PAIR, 3 * half_heads, 2 * PAIR), PAIR)
        for i in range(2)
    )
    return (
        block_out.astype(BF16)[None],
        mean_loss,
        grad_rows[None],
        cond_sum[None],
        q_s,
        k_s,
        v_s,
        out_t.T,
        cq_s,
        ck_s,
        cv_s,
        co_t.T,
        gate_s,
        up_s,
        down_t.T,
        grad_gains,
    )


def solution(mesh):
    dp_size, share = mesh.shape["dp"], mesh.shape["tensor"]
    fine = Mesh(
        mesh.devices.reshape(dp_size // 4, 2, 2, share), ("far", "near", "core", "tensor")
    )
    dp = ("far", "near", "core")
    tokens = P(dp, "tensor", None)
    per_latent = P(dp, None, None)
    by_row = P(dp, "tensor")
    by_column = P("tensor", dp)
    weights = (by_row,) * 3 + (by_column,) + (by_row,) * 3 + (by_column, by_row, by_row, by_column)
    return jax.shard_map(
        body,
        mesh=fine,
        in_specs=(tokens, per_latent, tokens, by_row, P(None, dp)) + weights,
        out_specs=(tokens, P(), tokens, per_latent) + weights + (P(None, dp),),
        check_vma=False,
    )
```

```python
import functools
import math

import jax
import jax.numpy as jnp
from jax import lax
from jax.experimental import pallas as pl
from jax.experimental.pallas import tpu as pltpu
from jax.sharding import Mesh, PartitionSpec as P

HEAD_DIM = 64
PAIR = 2 * HEAD_DIM
SCALE = HEAD_DIM**-0.5
EPSILON = 1e-05
F32 = jnp.float32
BF16 = jnp.bfloat16
KERNEL_VMEM = 60 << 20
PACK_VMEM = 60 << 20
GRAD_VMEM = 60 << 20
BACK_VMEM = 60 << 20
DOWN_PIECES = (896, 640)
GATE_PIECES = (1408, 128)
UP_PIECES = (768, 768)
PULL_ROWS = 512
NORM_ROWS = 192
FEED_COLUMNS = 768
SMALL_COST = pl.CostEstimate(flops=1 << 20, bytes_accessed=1 << 14, transcendentals=0)


def dot(left, right, left_dim, right_dim):
    return lax.dot_general(
        left, right, (((left_dim,), (right_dim,)), ((), ())), preferred_element_type=F32
    )


def norm_stats(values):
    row_mean = jnp.mean(values, axis=-1, keepdims=True)
    centred = values - row_mean
    row_var = jnp.mean(centred * centred, axis=-1, keepdims=True)
    inverse = lax.rsqrt(row_var + EPSILON)
    return (centred * inverse, inverse)


def rotary_tables(positions):
    half_dim = HEAD_DIM // 2
    freqs = jnp.exp(jnp.arange(half_dim, dtype=F32) * (-math.log(10000.0) / half_dim))
    angles = positions.astype(F32)[:, None] * freqs[None, :]
    cosine, sine = jnp.cos(angles), jnp.sin(angles)
    return (
        jnp.concatenate([cosine] * 4, axis=1),
        jnp.concatenate([-sine, sine] * 2, axis=1),
    )


def spin(values, cosines, sines):
    lane = lax.broadcasted_iota(jnp.int32, values.shape, 1)
    ahead = pltpu.roll(values, PAIR - HEAD_DIM // 2, 1)
    behind = pltpu.roll(values, HEAD_DIM // 2, 1)
    other = jnp.where(lane % HEAD_DIM < HEAD_DIM // 2, ahead, behind)
    return values * cosines + other * sines


def one_head(values, head):
    lane = lax.broadcasted_iota(jnp.int32, values.shape, 1)
    return jnp.where(lane // HEAD_DIM == head, values, jnp.zeros_like(values))


def turn(values):
    return values.astype(F32).T.astype(BF16)


def attend(keys, key_count, queries, values_t, out_ref, log_ref):
    mixed = []
    for head in range(2):
        scores = dot(keys, one_head(queries, head), 1, 1)
        if key_count < keys.shape[0]:
            row = lax.broadcasted_iota(jnp.int32, scores.shape, 0)
            scores = jnp.where(row < key_count, scores, -1e30)
        top = jnp.max(scores, axis=0, keepdims=True)
        shifted = jnp.exp(scores - top)
        total = jnp.sum(shifted, axis=0, keepdims=True)
        part = values_t[head * HEAD_DIM : (head + 1) * HEAD_DIM]
        mixed.append(dot(part, shifted.astype(BF16), 1, 0) / total)
        log_ref[0, head : head + 1, :] = top + jnp.log(total)
    out_ref[...] = jnp.concatenate(mixed, axis=0).T.astype(BF16)


def attend_back(queries, keys, key_count, values, grads, logs):
    keys_t = keys.astype(F32).T.astype(BF16)
    grad_k = jnp.zeros((keys.shape[0], PAIR), F32)
    grad_v = jnp.zeros((keys.shape[0], PAIR), F32)
    grad_q = []
    for head in range(2):
        query, grad = one_head(queries, head), one_head(grads, head)
        probs = jnp.exp(dot(keys, query, 1, 1) - logs[head : head + 1])
        if key_count < keys.shape[0]:
            row = lax.broadcasted_iota(jnp.int32, probs.shape, 0)
            probs = jnp.where(row < key_count, probs, 0.0)
        product = probs * dot(values, grad, 1, 1)
        weighted = jnp.sum(product, axis=0, keepdims=True)
        grad_s = (product - probs * weighted).astype(BF16)
        grad_v = grad_v + dot(probs.astype(BF16), grad, 1, 0)
        grad_k = grad_k + dot(grad_s, query, 1, 0)
        grad_q.append(dot(keys_t[head * HEAD_DIM : (head + 1) * HEAD_DIM], grad_s, 1, 0))
    return (jnp.concatenate(grad_q, axis=0).T * SCALE, grad_k, grad_v)


def self_forward_kernel(qkv, cos_in, sin_in, mixed, q_out, k_out, v_out, logs):
    cosines, sines = cos_in[...], sin_in[...]
    queries = spin(qkv[:, :PAIR], cosines, sines).astype(BF16).astype(F32)
    queries = (queries * SCALE).astype(BF16)
    keys = spin(qkv[:, PAIR : 2 * PAIR], cosines, sines).astype(BF16)
    values = qkv[:, 2 * PAIR :]
    q_out[...] = queries
    k_out[...] = keys
    v_out[...] = values.astype(BF16)
    attend(keys, keys.shape[0], queries, values.T.astype(BF16), mixed, logs)


def self_back_kernel(
    places, q_in, k_in, v_in, own_in, peer_in, out_w, qkv_w, logs, cos_in, sin_in,
    out, sent, own_out, peer_out, peer_sum,
):
    pair, pairs = pl.program_id(0), pl.num_programs(0)
    cosines, sines = cos_in[...], -sin_in[...]
    keys, weights = k_in[...], out_w[...]
    grads = jnp.concatenate([dot(own_in[...], weights, 1, 0), dot(peer_in[...], weights, 1, 0)], axis=0)
    grad_q, grad_k, grad_v = attend_back(
        q_in[...], keys, keys.shape[0], v_in[...], grads.astype(BF16), logs[0]
    )
    out[:, :PAIR] = spin(grad_q, cosines, sines).astype(BF16)
    out[:, PAIR : 2 * PAIR] = spin(grad_k, cosines, sines).astype(BF16)
    out[:, 2 * PAIR :] = grad_v.astype(BF16)

    @pl.when((2 * pair >= pairs) == (places[1] == 0))
    def _():
        sent[...] = out[...]

    rows = own_in.shape[0]
    own = dot(out[:rows, :], qkv_w[...], 1, 1)
    peer = dot(out[rows:, :], qkv_w[...], 1, 1)

    @pl.when(pair == 0)
    def _():
        own_out[...] = own
        peer_sum[...] = peer

    @pl.when(pair > 0)
    def _():
        own_out[...] += own
        peer_sum[...] += peer

    @pl.when(pair == pairs - 1)
    def _():
        peer_out[...] = peer_sum[...].astype(BF16)


def pick(own, peer):
    return jnp.where(2 * pl.program_id(0) < pl.num_programs(0), own[...], peer[...])


def cross_forward_kernel(key_count, q_own, q_peer, kv_own, kv_peer, mixed, logs):
    queries, keyvals = pick(q_own, q_peer), pick(kv_own, kv_peer)
    queries = (queries.astype(F32) * SCALE).astype(BF16)
    attend(keyvals[:, :PAIR], key_count, queries, turn(keyvals[:, PAIR:]), mixed, logs)


def cross_back_kernel(
    key_count, q_own, q_peer, g_own, g_peer, kv_own, kv_peer, logs, q_out, kv_out
):
    queries, keyvals = pick(q_own, q_peer), pick(kv_own, kv_peer)
    queries = (queries.astype(F32) * SCALE).astype(BF16)
    grad_q, grad_k, grad_v = attend_back(
        queries, keyvals[:, :PAIR], key_count, keyvals[:, PAIR:], pick(g_own, g_peer), logs[0]
    )
    q_out[...] = grad_q.astype(BF16)
    kv_out[:, :PAIR] = grad_k.astype(BF16)
    kv_out[:, PAIR:] = grad_v.astype(BF16)


def column_block(count):
    return pl.BlockSpec((count, PAIR), lambda i: (0, i))


def call_pairs(kernel, width, in_specs, out_specs, out_shape, args):
    return pl.pallas_call(
        kernel,
        grid=(width // PAIR,),
        in_specs=in_specs,
        out_specs=out_specs,
        out_shape=out_shape,
        compiler_params=pltpu.CompilerParams(vmem_limit_bytes=KERNEL_VMEM),
        cost_estimate=SMALL_COST,
    )(*args)


def self_forward(qkv, cosines, sines):
    rows, width = qkv.shape[0], qkv.shape[1] // 3
    pairs = width // PAIR
    table = pl.BlockSpec((rows, PAIR), lambda i: (0, 0))
    act = jax.ShapeDtypeStruct((rows, width), BF16)
    return call_pairs(
        self_forward_kernel,
        width,
        [pl.BlockSpec((rows, 3 * PAIR), lambda i: (0, i)), table, table],
        [column_block(rows)] * 4 + [pl.BlockSpec((1, 2, rows), lambda i: (i, 0, 0))],
        [act] * 4 + [jax.ShapeDtypeStruct((pairs, 2, rows), F32)],
        (qkv, cosines, sines),
    )


def self_back(places, queries, keys, values, own, peer, weights, logs, cosines, sines):
    rows, width = queries.shape
    count, depth = own.shape
    pairs = width // PAIR
    block = pl.BlockSpec((rows, PAIR), lambda i, places: (0, i))
    table = pl.BlockSpec((rows, PAIR), lambda i, places: (0, 0))
    token = pl.BlockSpec((count, depth), lambda i, places: (0, 0))
    half = pairs // 2
    return pl.pallas_call(
        self_back_kernel,
        grid_spec=pltpu.PrefetchScalarGridSpec(
            num_scalar_prefetch=1,
            grid=(pairs,),
            in_specs=[
                block,
                block,
                block,
                token,
                token,
                pl.BlockSpec((depth, PAIR), lambda i, places: (0, 3 * pairs + i)),
                pl.BlockSpec((depth, 3 * PAIR), lambda i, places: (0, i)),
                pl.BlockSpec((1, 2, rows), lambda i, places: (i, 0, 0)),
                table,
                table,
            ],
            out_specs=[
                pl.BlockSpec((rows, 3 * PAIR), lambda i, places: (0, i)),
                pl.BlockSpec(
                    (rows, 3 * PAIR),
                    lambda i, places: (0, jnp.clip(i - half * (1 - places[1]), 0, half - 1)),
                ),
                token,
                token,
            ],
            scratch_shapes=[pltpu.VMEM((count, depth), F32)],
        ),
        out_shape=[
            jax.ShapeDtypeStruct((rows, 3 * width), BF16),
            jax.ShapeDtypeStruct((rows, 3 * width // 2), BF16),
            jax.ShapeDtypeStruct((count, depth), F32),
            jax.ShapeDtypeStruct((count, depth), BF16),
        ],
        compiler_params=pltpu.CompilerParams(vmem_limit_bytes=BACK_VMEM),
        cost_estimate=SMALL_COST,
    )(places, queries, keys, values, own, peer, weights, weights, logs, cosines, sines)


def cross_call(kernel, key_count, arrays, logs, out_specs, out_shape):
    pairs = arrays[0][0].shape[1] // PAIR
    specs, args = [], []
    for own, peer in arrays:
        block = (own.shape[0], own.shape[1] // pairs)
        specs.append(pl.BlockSpec(block, lambda i: (0, jnp.minimum(i, pairs - 1))))
        specs.append(pl.BlockSpec(block, lambda i: (0, jnp.maximum(i - pairs, 0))))
        args += [own, peer]
    if logs is not None:
        specs.append(pl.BlockSpec((1,) + logs.shape[1:], lambda i: (i, 0, 0)))
        args.append(logs)
    return pl.pallas_call(
        functools.partial(kernel, key_count),
        grid=(2 * pairs,),
        in_specs=specs,
        out_specs=out_specs,
        out_shape=out_shape,
        compiler_params=pltpu.CompilerParams(vmem_limit_bytes=KERNEL_VMEM),
        cost_estimate=SMALL_COST,
    )(*args)


def cross_forward(queries, keyvals, key_count):
    rows, width = queries[0].shape
    return cross_call(
        cross_forward_kernel,
        key_count,
        (queries, keyvals),
        None,
        [column_block(rows), pl.BlockSpec((1, 2, rows), lambda i: (i, 0, 0))],
        [
            jax.ShapeDtypeStruct((rows, 2 * width), BF16),
            jax.ShapeDtypeStruct((2 * width // PAIR, 2, rows), F32),
        ],
    )


def cross_back(queries, grads, keyvals, logs, key_count):
    rows, width = queries[0].shape
    keys = keyvals[0].shape[0]
    return cross_call(
        cross_back_kernel,
        key_count,
        (queries, grads, keyvals),
        logs,
        [column_block(rows), pl.BlockSpec((keys, 2 * PAIR), lambda i: (0, i))],
        [
            jax.ShapeDtypeStruct((rows, 2 * width), BF16),
            jax.ShapeDtypeStruct((keys, 4 * width), BF16),
        ],
    )


def norm_back_kernel(away, *refs):
    pulled, peer = refs[0], refs[1] if away else None
    hidden, gain_row, skip, total_out, low_out, gain_out = refs[1 + away :]
    grad = pulled[...] + peer[...].astype(F32) if away else pulled[...]
    normed, inverse = norm_stats(hidden[...].astype(F32))
    scaled = grad * gain_row[...]
    mean_scaled = jnp.mean(scaled, axis=-1, keepdims=True)
    mean_product = jnp.mean(scaled * normed, axis=-1, keepdims=True)
    total = skip[...] + inverse * (scaled - mean_scaled - normed * mean_product)
    total_out[...] = total
    low_out[...] = total.astype(BF16)
    received = jnp.sum(grad * normed, axis=0, keepdims=True)

    @pl.when(pl.program_id(0) == 0)
    def _():
        gain_out[...] = received

    @pl.when(pl.program_id(0) > 0)
    def _():
        gain_out[...] += received


def norm_back(pulled, away, hidden, gain_row, skip):
    rows, depth = pulled.shape
    block = pl.BlockSpec((NORM_ROWS, depth), lambda i: (i, 0))
    row = pl.BlockSpec((1, depth), lambda i: (0, 0))
    arrays = (pulled,) if away is None else (pulled, away)
    return pl.pallas_call(
        functools.partial(norm_back_kernel, len(arrays) - 1),
        grid=(rows // NORM_ROWS,),
        in_specs=[block] * len(arrays) + [block, row, block],
        out_specs=[block, block, row],
        out_shape=[
            jax.ShapeDtypeStruct((rows, depth), F32),
            jax.ShapeDtypeStruct((rows, depth), BF16),
            jax.ShapeDtypeStruct((1, depth), F32),
        ],
        compiler_params=pltpu.CompilerParams(vmem_limit_bytes=KERNEL_VMEM),
        cost_estimate=SMALL_COST,
    )(*arrays, hidden, gain_row, skip)


def feed_back_kernel(places, g_in, weights, gate_in, up_in, gate_out, up_out, sent):
    grad_hidden = dot(g_in[...], weights[...], 1, 0)
    gate_pre, up_pre = gate_in[...].astype(F32), up_in[...].astype(F32)
    sigmoid = 1.0 / (1.0 + jnp.exp(-gate_pre))
    grad_gate = grad_hidden * up_pre * sigmoid * (1.0 + gate_pre * (1.0 - sigmoid))
    gate_out[...] = grad_gate.astype(BF16)
    up_out[...] = (grad_hidden * (gate_pre * sigmoid)).astype(BF16)

    @pl.when((2 * pl.program_id(0) >= pl.num_programs(0)) == (places[1] == 0))
    def _():
        sent[0] = gate_out[...]
        sent[1] = up_out[...]


def feed_back(places, grads, weights, gate_pre, up_pre, part):
    rows, depth = grads.shape
    width = gate_pre.shape[1]
    steps = width // FEED_COLUMNS
    half = steps // 2
    column = pl.BlockSpec((rows, FEED_COLUMNS), lambda i, places: (0, i))
    row_part = pl.BlockSpec((rows, FEED_COLUMNS), lambda i, places: (part, i))
    act = jax.ShapeDtypeStruct((rows, width), BF16)
    return pl.pallas_call(
        feed_back_kernel,
        grid_spec=pltpu.PrefetchScalarGridSpec(
            num_scalar_prefetch=1,
            grid=(steps,),
            in_specs=[
                pl.BlockSpec((rows, depth), lambda i, places: (0, 0)),
                pl.BlockSpec((depth, FEED_COLUMNS), lambda i, places: (0, 2 * steps + i)),
                row_part,
                row_part,
            ],
            out_specs=[
                column,
                column,
                pl.BlockSpec(
                    (2, rows, FEED_COLUMNS),
                    lambda i, places: (0, 0, jnp.clip(i - half * (1 - places[1]), 0, half - 1)),
                ),
            ],
        ),
        out_shape=[act, act, jax.ShapeDtypeStruct((2, rows, width // 2), BF16)],
        compiler_params=pltpu.CompilerParams(vmem_limit_bytes=BACK_VMEM),
        cost_estimate=SMALL_COST,
    )(places, grads, weights, gate_pre, up_pre)


def weight_grad_kernel(count, pieces, group, places, *refs):
    outs = refs[2 * count :]
    total = dot(refs[0][...], refs[1][...], 0, 0)
    for index in range(1, count):
        total = total + dot(refs[2 * index][...], refs[2 * index + 1][...], 0, 0)

    def side(index):
        starts = range(index * group, total.shape[0], 2 * group)
        parts = [total[at : at + group] for at in starts]
        return (jnp.concatenate(parts, axis=0) if len(parts) > 1 else parts[0]).astype(BF16)

    first, second = side(0), side(1)

    def write(values, targets):
        at = 0
        for piece, target in zip(pieces, targets, strict=True):
            target[...] = values[:, at : at + piece]
            at += piece

    @pl.when(places[0] == 0)
    def _():
        write(first, outs[: len(pieces)])
        write(second, outs[len(pieces) :])

    @pl.when(places[0] != 0)
    def _():
        write(second, outs[: len(pieces)])
        write(first, outs[len(pieces) :])


def weight_grad(places, far, pieces, parts):
    columns = sum(pieces)
    sides = [[side if isinstance(side, tuple) else (side, None) for side in part[:2]] for part in parts]
    depth = sides[0][0][0].shape[1]
    block = math.lcm(depth // far, 128)
    specs, args = [], []
    for ((left, left_half), (right, right_half)), (_, _, at) in zip(sides, parts, strict=True):
        tokens = left.shape[0] if left_half is None else left.shape[0] // 2
        first, second = left_half or 0, right_half or 0
        specs.append(pl.BlockSpec((tokens, block), lambda i, places, first=first: (first, i)))
        if at is None:
            spec = pl.BlockSpec(
                (tokens, columns), lambda i, places, second=second: (second, places[1])
            )
        elif right.ndim == 3:
            spec = pl.BlockSpec(
                (pl.Squeezed(), tokens, columns), lambda i, places, at=at: (at, 0, 0)
            )
        else:
            spec = pl.BlockSpec(
                (tokens, columns), lambda i, places, second=second, at=at: (second, at)
            )
        specs.append(spec)
        args += [left, right]
    outs = pl.pallas_call(
        functools.partial(weight_grad_kernel, len(parts), pieces, depth // far // 2),
        grid_spec=pltpu.PrefetchScalarGridSpec(
            num_scalar_prefetch=1,
            grid=(depth // block,),
            in_specs=specs,
            out_specs=[
                pl.BlockSpec((block // 2, piece), lambda i, places: (i, 0)) for piece in 2 * pieces
            ],
        ),
        out_shape=[jax.ShapeDtypeStruct((depth // 2, piece), BF16) for piece in 2 * pieces],
        compiler_params=pltpu.CompilerParams(vmem_limit_bytes=GRAD_VMEM),
        cost_estimate=SMALL_COST,
    )(places, *args)
    return outs[: len(pieces)], outs[len(pieces) :]


def whole_call(kernel, out_shape, *args):
    return pl.pallas_call(
        kernel,
        out_shape=out_shape,
        compiler_params=pltpu.CompilerParams(vmem_limit_bytes=BACK_VMEM),
        cost_estimate=SMALL_COST,
    )(*args)


def join_kernel(axis, *refs):
    refs[-1][...] = jnp.concatenate([ref[...] for ref in refs[:-1]], axis=axis)


def join(axis, *parts):
    shape = list(parts[0].shape)
    shape[axis] = sum(part.shape[axis] for part in parts)
    return whole_call(
        functools.partial(join_kernel, axis), jax.ShapeDtypeStruct(shape, parts[0].dtype), *parts
    )


def near_sum_kernel(*refs):
    got, out = refs[-2:]
    at = 0
    for ref in refs[:-2]:
        end = at + ref.shape[1]
        out[:, at:end] = (ref[...].astype(F32) + got[:, at:end].astype(F32)).astype(BF16)
        at = end


def near_sum(kept, got):
    rows, columns = got.shape
    block = rows // 4 if rows % 64 == 0 else rows

    def spec(width):
        return pl.BlockSpec((block, width), lambda i: (i, 0))

    return pl.pallas_call(
        near_sum_kernel,
        grid=(rows // block,),
        in_specs=[spec(part.shape[1]) for part in kept] + [spec(columns)],
        out_specs=spec(columns),
        out_shape=jax.ShapeDtypeStruct(got.shape, BF16),
        compiler_params=pltpu.CompilerParams(vmem_limit_bytes=KERNEL_VMEM),
        cost_estimate=SMALL_COST,
    )(*kept, got)


def other_half_kernel(places, *refs):
    out, at = refs[-1], 0
    for ref in refs[:-1]:
        out[at : at + ref.shape[0], :] = ref[...]
        at += ref.shape[0]


def other_half(places, width, *parts):
    half = width // 2
    rows = sum(part.shape[0] for part in parts)
    return pl.pallas_call(
        other_half_kernel,
        grid_spec=pltpu.PrefetchScalarGridSpec(
            num_scalar_prefetch=1,
            grid=(1,),
            in_specs=[
                pl.BlockSpec((part.shape[0], half), lambda i, places: (0, 1 - places[1]))
                for part in parts
            ],
            out_specs=pl.BlockSpec((rows, half), lambda i, places: (0, 0)),
        ),
        out_shape=jax.ShapeDtypeStruct((rows, half), BF16),
        compiler_params=pltpu.CompilerParams(vmem_limit_bytes=KERNEL_VMEM),
        cost_estimate=SMALL_COST,
    )(places, *parts)


def mixed_back_kernel(g_in, own_w, peer_w, own_out, peer_out):
    own_out[...] = dot(g_in[...], own_w[...], 1, 0).astype(BF16)
    peer_out[...] = dot(g_in[...], peer_w[...], 1, 0).astype(BF16)


def mixed_back(grads, weights, at, peer_weights):
    rows, depth = grads.shape
    width = peer_weights.shape[1]
    half = width // 2
    act = jax.ShapeDtypeStruct((rows, width), BF16)
    return pl.pallas_call(
        mixed_back_kernel,
        grid=(2,),
        in_specs=[
            pl.BlockSpec((rows, depth), lambda i: (0, 0)),
            pl.BlockSpec((depth, half), lambda i: (0, 2 * at + i)),
            pl.BlockSpec((depth, half), lambda i: (0, i)),
        ],
        out_specs=[pl.BlockSpec((rows, half), lambda i: (0, i))] * 2,
        out_shape=[act, act],
        compiler_params=pltpu.CompilerParams(vmem_limit_bytes=KERNEL_VMEM),
        cost_estimate=SMALL_COST,
    )(grads, weights, peer_weights)


def pull_query_kernel(g_in, own_w, peer_w, out):
    width = own_w.shape[1]
    out[...] = dot(g_in[:, :width], own_w[...], 1, 1) + dot(g_in[:, width:], peer_w[...], 1, 1)


def pull_query(grads, weights, at, peer_weights):
    rows = grads.shape[0]
    depth, width = peer_weights.shape
    return pl.pallas_call(
        pull_query_kernel,
        grid=(depth // PULL_ROWS,),
        in_specs=[
            pl.BlockSpec(grads.shape, lambda i: (0, 0)),
            pl.BlockSpec((PULL_ROWS, width), lambda i: (i, at)),
            pl.BlockSpec((PULL_ROWS, width), lambda i: (i, 0)),
        ],
        out_specs=pl.BlockSpec((rows, PULL_ROWS), lambda i: (0, i)),
        out_shape=jax.ShapeDtypeStruct((rows, depth), F32),
        compiler_params=pltpu.CompilerParams(vmem_limit_bytes=KERNEL_VMEM),
        cost_estimate=SMALL_COST,
    )(grads, weights, peer_weights)


def pull_kernel(gate_in, up_in, weights, out):
    width = gate_in.shape[1]
    total = dot(gate_in[...], weights[:, :width], 1, 1) + dot(up_in[...], weights[:, width:], 1, 1)
    out[...] = total.astype(out.dtype)


def pull(grad_gate, grad_upper, weights, kind):
    rows, width = grad_gate.shape
    depth = weights.shape[0]
    whole = pl.BlockSpec((rows, width), lambda i: (0, 0))
    return pl.pallas_call(
        pull_kernel,
        grid=(depth // PULL_ROWS,),
        in_specs=[whole, whole, pl.BlockSpec((PULL_ROWS, 2 * width), lambda i: (i, 0))],
        out_specs=pl.BlockSpec((rows, PULL_ROWS), lambda i: (0, i)),
        out_shape=jax.ShapeDtypeStruct((rows, depth), kind),
        compiler_params=pltpu.CompilerParams(vmem_limit_bytes=GRAD_VMEM),
        cost_estimate=SMALL_COST,
    )(grad_gate, grad_upper, weights)


def meet(*values):
    return lax.optimization_barrier(values)


def pack_attention_kernel(q_in, k_in, v_in, o_in, cq_in, ck_in, cv_in, co_in, gains, mask, out):
    width = q_in.shape[1]
    for pair in range(width // PAIR):
        for index, ref in enumerate((q_in, k_in, v_in)):
            at = (3 * pair + index) * PAIR
            out[:, at : at + PAIR] = ref[:, pair * PAIR : (pair + 1) * PAIR]
    out[:, 3 * width : 4 * width] = turn(o_in[...])
    for pair in range(width // PAIR):
        for index, ref in enumerate((ck_in, cv_in)):
            at = 4 * width + (2 * pair + index) * PAIR
            out[:, at : at + PAIR] = ref[:, pair * PAIR : (pair + 1) * PAIR]
    out[:, 6 * width : 7 * width] = cq_in[...]
    out[:, 7 * width : 8 * width] = turn(co_in[...])
    count = jnp.sum(mask[...].astype(F32), axis=1, keepdims=True)
    upper = jnp.floor(count * (1.0 / 128.0))
    side = gains[...].astype(F32).T
    row = lax.broadcasted_iota(jnp.int32, side.shape, 0)
    lane = lax.broadcasted_iota(jnp.int32, side.shape, 1)
    side = jnp.where((lane == 3) & (row == 0), upper, side)
    side = jnp.where((lane == 3) & (row == 1), count - 128.0 * upper, side)
    out[:, 8 * width :] = side.astype(BF16)


def pack_feed_kernel(gate_in, up_in, down_in, out):
    width = gate_in.shape[1]
    out[:, :width] = gate_in[...]
    out[:, width : 2 * width] = up_in[...]
    out[:, 2 * width :] = turn(down_in[...])


def pack(kernel, columns, *parts):
    return pl.pallas_call(
        kernel,
        out_shape=jax.ShapeDtypeStruct((parts[0].shape[0], columns), BF16),
        compiler_params=pltpu.CompilerParams(vmem_limit_bytes=PACK_VMEM),
    )(*parts)


def after(value, *earlier):
    return lax.optimization_barrier((value, *earlier))[0]


def body(
    x_input,
    cond_tokens,
    teacher,
    valid_mask,
    norm_gains,
    w_query,
    w_key,
    w_value,
    w_out,
    c_query,
    c_key,
    c_value,
    c_out,
    w_gate,
    w_up,
    w_down,
):
    far = lax.axis_size("far")
    near_at, pair, share = (lax.axis_index(name) for name in ("near", "core", "tensor"))
    dp_axes = ("far", "near", "core")
    dp_size = 4 * far
    swap = [(0, 1), (1, 0)]

    def to_peer(values):
        return lax.ppermute(values, "tensor", swap)

    def to_core(values):
        return lax.ppermute(values, "core", swap)

    def to_near(values):
        return lax.ppermute(values, "near", swap)

    def gather(values):
        return lax.all_gather(values, dp_axes, axis=0, tiled=True)

    x_bf = x_input[0]
    rows, width = x_bf.shape
    slab = w_query.shape[0]
    heads_width = w_query.shape[1]
    ff_width = w_gate.shape[1]
    length = 2 * rows
    ctx_len = cond_tokens.shape[1]
    cond_rows = jnp.pad(cond_tokens[0], ((0, -ctx_len % 16), (0, 0)))
    mask_float = valid_mask[0].astype(F32)
    x_peer_bf = to_peer(x_bf)

    gath_a = gather(
        pack(
            pack_attention_kernel,
            8 * heads_width + PAIR,
            w_query,
            w_key,
            w_value,
            w_out,
            c_query,
            c_key,
            c_value,
            c_out,
            jnp.pad(norm_gains, ((0, PAIR - 3), (0, 0))),
            valid_mask,
        )
    )
    gath_b = gather(pack(pack_feed_kernel, 3 * ff_width, w_gate, w_up, w_down))

    weight_qkv = gath_a[:, : 3 * heads_width]
    weight_o = gath_a[:, 3 * heads_width : 4 * heads_width]
    cross_kv = gath_a[:, 4 * heads_width : 6 * heads_width]
    side = gath_a[:, 8 * heads_width :].T[:8].astype(F32)
    gains = side[:3]
    counts = side[3].reshape(dp_size, slab)
    part_count = jnp.sum(counts[:, 0]) * 128.0 + jnp.sum(counts[:, 1])
    part_count = jnp.full((8, 128), part_count, F32)
    valid_count = (part_count + to_peer(part_count))[0, 0]
    half_ff, half_heads = ff_width // 2, heads_width // 2
    places = jnp.stack([near_at, pair]).astype(jnp.int32)

    def fetch_peer(first):
        return to_peer(
            lax.dynamic_slice(
                gath_a, (pair * (width // 2), first * heads_width), (width // 2, heads_width)
            )
        )

    def join_cores(got):
        other = to_core(got)
        return jnp.concatenate(
            [jnp.where(pair == 0, got, other), jnp.where(pair == 0, other, got)], axis=0
        )

    cross_q_own = gath_a[:, 6 * heads_width : 7 * heads_width]
    cross_o_own = gath_a[:, 7 * heads_width : 8 * heads_width]
    cross_q_peer = fetch_peer(6)

    local_rows = x_bf.astype(F32)
    normed_one, _ = norm_stats(local_rows)
    peer_one, _ = norm_stats(x_peer_bf.astype(F32))
    input_one = jnp.concatenate(
        [(normed_one * gains[0]).astype(BF16), (peer_one * gains[0]).astype(BF16)], axis=0
    )
    order = lax.iota(jnp.int32, length)
    positions = jnp.where(order < rows, order + share * rows, order - share * rows)
    cosines, sines = rotary_tables(positions)
    def project(values, weight, weight_dim, *meanwhile):
        away = to_peer(dot(values[rows:], weight, 1, weight_dim).astype(BF16))
        mine = dot(values[:rows], weight, 1, weight_dim)
        return mine + after(away, mine, *meanwhile).astype(F32)

    qkv = dot(input_one, weight_qkv, 1, 0)
    mixed_self, query_self, key_self, value_self, logs_self = self_forward(qkv, cosines, sines)
    cross_q_peer = join_cores(after(cross_q_peer, mixed_self))
    cross_o_peer = fetch_peer(7)
    keyvals_own = dot(cond_rows, cross_kv, 1, 0).astype(BF16)
    keyvals_peer = to_peer(keyvals_own)
    core_one = to_core(input_one)
    hidden_one = local_rows + project(mixed_self, weight_o, 1, core_one, cross_q_peer)

    normed_two, _ = norm_stats(hidden_one)
    own_two = (normed_two * gains[1]).astype(BF16)
    query_cross = tuple(
        dot(own_two, weight, 1, 0).astype(BF16) for weight in (cross_q_own, cross_q_peer)
    )
    keyvals = (keyvals_own, after(keyvals_peer, own_two))
    mixed_cross, logs_cross = cross_forward(query_cross, keyvals, ctx_len)
    cross_o_peer = join_cores(after(cross_o_peer, mixed_cross))
    hidden_two = (
        hidden_one
        + dot(mixed_cross[:, :heads_width], cross_o_own, 1, 1)
        + dot(mixed_cross[:, heads_width:], cross_o_peer, 1, 1)
    )

    normed_three, _ = norm_stats(hidden_two)
    own_three = (normed_three * gains[2]).astype(BF16)
    peer_three = to_peer(own_three)
    core_mixed_self, core_cond = to_core(other_half(places, heads_width, mixed_self)), to_core(cond_rows)
    peer_three = after(peer_three, core_mixed_self, core_cond)
    input_three = jnp.concatenate([own_three, peer_three], axis=0)
    weight_gate = gath_b[:, :ff_width]
    weight_up = gath_b[:, ff_width : 2 * ff_width]
    weight_down = gath_b[:, 2 * ff_width :]
    gate_pre = dot(input_three, weight_gate, 1, 0).astype(BF16)
    up_sum = dot(input_three, weight_up, 1, 0)
    gate_sum = gate_pre.astype(F32)
    hidden_ff = (gate_sum * jax.nn.sigmoid(gate_sum) * up_sum).astype(BF16)
    core_own_two = to_core(own_two)
    up_pre = up_sum.astype(BF16)
    core_three = to_core(input_three)
    core_hidden = to_core(other_half(places, ff_width, hidden_ff))
    block_out = hidden_two + project(hidden_ff, weight_down, 1, core_three, core_hidden, core_own_two)

    error_diff = block_out - teacher[0].astype(F32)
    local_error = jnp.sum(mask_float[:, None] * error_diff * error_diff)
    token_total = float(dp_size * lax.axis_size("tensor") * rows)
    grad_out = 2.0 * token_total / valid_count * mask_float[:, None] * error_diff

    def grad_of(pieces, *parts):
        return weight_grad(places, far, pieces, parts)

    scattered = []

    def add_pair(kept, got):
        return near_sum(kept, after(got, *scattered[:-1]))

    def scatter_on(summed):
        scattered.append(scatter(summed))
        return scattered[-1]

    def scatter(summed):
        return lax.psum_scatter(summed, "far", scatter_dimension=0, tiled=True)

    def finish(scattered):
        columns = scattered.shape[1]
        kept = lax.dynamic_slice(scattered, (pair * slab, 0), (slab, columns))
        got = to_core(lax.dynamic_slice(scattered, ((1 - pair) * slab, 0), (slab, columns)))
        first = jnp.where(pair == 0, kept, got).astype(F32)
        second = jnp.where(pair == 0, got, kept).astype(F32)
        return (first, second)

    def columns_at(sides, places, size):
        return jnp.concatenate(
            [side[:, at : at + size] for side in sides for at in places], axis=1
        )

    own_e3 = grad_out.astype(BF16)
    peer_e3 = to_peer(own_e3)
    core_own_e3 = to_core(own_e3)

    def row(index):
        return gains[index : index + 1]

    dgate_own, dup_own, halves_own = feed_back(places, own_e3, gath_b, gate_pre, up_pre, 0)
    dgate_own, dup_own, halves_own, pulled_own, peer_e3, core_own_e3 = meet(
        dgate_own, dup_own, halves_own, pull(dgate_own, dup_own, gath_b, F32), peer_e3, core_own_e3
    )
    dgate_peer, dup_peer, halves_peer, core_peer_e3, core_own_halves = meet(
        *feed_back(places, peer_e3, gath_b, gate_pre, up_pre, 1),
        to_core(peer_e3),
        to_core(halves_own),
    )
    kept_down, sent_down = grad_of(
        DOWN_PIECES,
        (own_e3, (hidden_ff, 0), None),
        (peer_e3, (hidden_ff, 1), None),
        (core_own_e3, (core_hidden, 0), 0),
        (core_peer_e3, (core_hidden, 1), 0),
    )
    *sent_down, dgate_peer, dup_peer, halves_peer, peer_mixed = meet(
        *sent_down,
        dgate_peer,
        dup_peer,
        halves_peer,
        to_peer(after(mixed_cross, dgate_peer)[:, heads_width:]),
    )
    near_a = to_near(sent_down[0])
    half_mixed = other_half(places, heads_width, mixed_cross, peer_mixed)
    peer_two = to_peer(after(own_two, half_mixed))
    pulled_peer, core_peer_halves, core_mixed = meet(
        pull(dgate_peer, dup_peer, gath_b, BF16), to_core(halves_peer), to_core(half_mixed)
    )
    away = to_peer(pulled_peer)

    def feed_grad(pieces, own, peer, at):
        kept, sent = grad_of(
            pieces,
            (own_three, own, None),
            (peer_three, peer, None),
            ((core_three, 0), core_own_halves, at),
            ((core_three, 1), core_peer_halves, at),
        )
        return kept + sent

    *gate_w, near_a = meet(
        *feed_grad(GATE_PIECES, dgate_own, after(dgate_peer, pulled_peer), 0), near_a
    )
    near_b = to_near(after(sent_down[1], near_a))
    *up_w, sum_a, near_b, peer_two, away = meet(
        *feed_grad(UP_PIECES, dup_own, after(dup_peer, gate_w[0]), 1),
        add_pair(kept_down[:1], near_a),
        near_b,
        peer_two,
        away,
    )
    scat_down = [scatter_on(sum_a)]
    near_c = to_near(after(gate_w[2], near_b))
    grad_two, own_e2, gain_three = norm_back(pulled_own, away, hidden_two, row(2), grad_out)

    grad_mixed = mixed_back(own_e2, gath_a, 7, cross_o_peer)
    grad_qc, grad_kv = cross_back(query_cross, grad_mixed, keyvals, logs_cross, ctx_len)
    pulled_two = pull_query(grad_qc, gath_a, 6, cross_q_peer)
    grad_one, own_e1, gain_two = norm_back(pulled_two, None, hidden_one, row(1), grad_two)
    sum_b = add_pair(kept_down[1:2], near_b)
    scat_down.append(scatter_on(sum_b))
    sent_d = up_w[2]
    grad_one, own_e1, gain_two, sum_b, own_e2, peer_e2, core_own_e2, near_c = meet(
        grad_one, own_e1, gain_two, sum_b, own_e2, to_peer(own_e2), to_core(own_e2), near_c
    )

    def head_grad(*parts):
        kept, sent = grad_of((half_heads,), *parts)
        return kept[0], sent[0]

    near_d = to_near(sent_d)
    peer_e1 = to_peer(own_e1)
    sum_c = add_pair(gate_w[:1], near_c)
    scat_gate = [scatter_on(sum_c)]
    core_peer_e2 = to_core(peer_e2)
    kept_co, sent_co = head_grad(
        (own_e2, mixed_cross, None),
        (peer_e2, peer_mixed, None),
        (core_own_e2, (core_mixed, 0), 0),
        (core_peer_e2, (core_mixed, 1), 0),
    )
    sum_c, peer_e1, near_d, core_own_e1, kept_co, sent_co = meet(
        sum_c, peer_e1, near_d, to_core(own_e1), kept_co, sent_co
    )
    grad_qc, grad_kv, _ = meet(grad_qc, grad_kv, peer_e1)
    sum_d = add_pair([up_w[0]], near_d)
    mid = scatter_on(sum_d)
    sum_d, core_peer_e1 = meet(sum_d, to_core(peer_e1))
    kept_wo, sent_wo = head_grad(
        (own_e1, (mixed_self, 0), None),
        (peer_e1, (mixed_self, 1), None),
        (core_own_e1, (core_mixed_self, 0), 0),
        (core_peer_e1, (core_mixed_self, 1), 0),
    )
    kept_wo, sent_e = meet(kept_wo, join(1, up_w[3], gate_w[3], sent_wo))
    near_e = to_near(sent_e)
    grad_qkv, halves_qkv, pulled_own, pulled_peer, peer_qc, peer_kv, near_e = meet(
        *self_back(
            places,
            query_self,
            key_self,
            value_self,
            own_e1,
            after(peer_e1, sent_e),
            gath_a,
            logs_self,
            cosines,
            sines,
        ),
        to_peer(grad_qc[:, heads_width:]),
        to_peer(grad_kv[:, 2 * heads_width :]),
        near_e,
    )
    near_co = to_near(after(sent_co, near_e))
    away = to_peer(pulled_peer)
    sum_e = add_pair([up_w[1], gate_w[1], kept_wo], near_e)
    last_ff = scatter_on(sum_e)
    sum_e, core_qkv = meet(sum_e, to_core(halves_qkv))
    kept_qkv, sent_qkv = grad_of(
        (3 * half_heads,), (input_one, after(grad_qkv, sum_e), None), (core_one, core_qkv, 0)
    )
    kept_qkv, sent_f, near_co = meet(kept_qkv[0], sent_qkv[0], near_co)
    near_f = to_near(sent_f)
    sum_co = add_pair([kept_co], near_co)
    scat_co = scatter_on(sum_co)
    sum_kv = near_sum([grad_kv[:, : 2 * heads_width]], after(peer_kv, sent_f))
    sum_kv, half_kv, half_qc = meet(
        sum_kv,
        other_half(places, 2 * heads_width, sum_kv),
        other_half(places, heads_width, grad_qc, after(peer_qc, sent_f)),
    )
    sum_co, core_kv, core_qc, core_peer_two = meet(
        sum_co, to_core(half_kv), to_core(half_qc), to_core(after(peer_two, half_qc))
    )
    kept_cq, sent_cq = head_grad(
        (own_two, after(grad_qc, sum_co), None),
        (peer_two, peer_qc, None),
        (core_own_two, (core_qc, 0), 0),
        (core_peer_two, (core_qc, 1), 0),
    )
    kept_ckv, sent_ckv = grad_of(
        (heads_width,), (cond_rows, after(sum_kv, sent_cq), None), (core_cond, core_kv, 0)
    )
    kept_cq, kept_ckv, sent_w, near_f = meet(
        kept_cq, kept_ckv[0], join(1, sent_cq, sent_ckv[0]), near_f
    )
    near_w = to_near(sent_w)
    sum_f = add_pair([kept_qkv], near_f)
    scat_qkv = scatter_on(sum_f)
    cond_part = dot(after(sum_kv, sum_f), cross_kv, 1, 1)[:ctx_len].astype(BF16)
    grad_rows, _, gain_one = norm_back(
        pulled_own, after(away, sum_f), x_bf, row(0), grad_one
    )
    near_w, cond_part, last_ff, scat_co, grad_rows, gain_one = meet(
        near_w, cond_part, last_ff, scat_co, grad_rows, gain_one
    )
    cond_sum = cond_part.astype(F32) + to_peer(cond_part).astype(F32)
    sum_w = near_sum([kept_cq, kept_ckv], near_w)
    scat_w = scatter(sum_w)

    small = jnp.concatenate(
        [gain_one, gain_two, gain_three, jnp.full((1, width), local_error, F32)], axis=0
    )
    small = after(small, sum_w)
    for axis in ("tensor", "core", "near", "far"):
        size = lax.axis_size(axis)
        if size & (size - 1):
            small = lax.psum(small, axis)
            continue
        hop = 1
        while hop < size:
            small = small + lax.ppermute(small, axis, [(i, i ^ hop) for i in range(size)])
            hop *= 2
    mean_loss = small[3, 0] / (width * valid_count)
    place = (lax.axis_index("far") * 4 + near_at * 2 + pair) * slab
    grad_gains = lax.dynamic_slice(small, (0, place), (3, slab))

    ends = (UP_PIECES[1], UP_PIECES[1] + GATE_PIECES[1])
    gate_parts = scat_gate + [last_ff[:, ends[0] : ends[1]]]
    up_parts = [mid, last_ff[:, : ends[0]]]
    down_parts = scat_down
    down_t, gate_s, up_s = (
        jnp.concatenate(finish(jnp.concatenate(parts, axis=1)), axis=1)
        for parts in (down_parts, gate_parts, up_parts)
    )
    sides = finish(scat_qkv)
    q_s, k_s, v_s = (
        columns_at(sides, range(i * PAIR, 3 * half_heads, 3 * PAIR), PAIR) for i in range(3)
    )
    out_t = jnp.concatenate(finish(last_ff[:, ends[1] :]), axis=1)
    co_t = jnp.concatenate(finish(scat_co), axis=1)
    sides = finish(scat_w)
    cq_s = columns_at(sides, [0], half_heads)
    ck_s, cv_s = (
        columns_at(sides, range(half_heads + i * PAIR, 3 * half_heads, 2 * PAIR), PAIR)
        for i in range(2)
    )
    return (
        block_out.astype(BF16)[None],
        mean_loss,
        grad_rows[None],
        cond_sum[None],
        q_s,
        k_s,
        v_s,
        out_t.T,
        cq_s,
        ck_s,
        cv_s,
        co_t.T,
        gate_s,
        up_s,
        down_t.T,
        grad_gains,
    )


def solution(mesh):
    dp_size, share = mesh.shape["dp"], mesh.shape["tensor"]
    fine = Mesh(
        mesh.devices.reshape(dp_size // 4, 2, 2, share), ("far", "near", "core", "tensor")
    )
    dp = ("far", "near", "core")
    tokens = P(dp, "tensor", None)
    per_latent = P(dp, None, None)
    by_row = P(dp, "tensor")
    by_column = P("tensor", dp)
    weights = (by_row,) * 3 + (by_column,) + (by_row,) * 3 + (by_column, by_row, by_row, by_column)
    return jax.shard_map(
        body,
        mesh=fine,
        in_specs=(tokens, per_latent, tokens, by_row, P(None, dp)) + weights,
        out_specs=(tokens, P(), tokens, per_latent) + weights + (P(None, dp),),
        check_vma=False,
    )
```
